32 devices in a mesh: dp: 8 (over z, x), mp: 4 (over y, core).
Axes of the slice: x: 2, y: 2, z: 4, core: 2. Of those that a mesh axis runs over, the one named last changes fastest.
Arguments:
- block_input: bfloat16 [2, 8192, 512], P(None, 'dp'), may hold values from -6 to 6
- out_cotangent: bfloat16 [2, 8192, 512], P(None, 'dp'), may hold values from -6 to 6
- early_up: bfloat16 [512, 2048], P('dp', 'mp'), may hold values from -0.25 to 0.25
- early_down: bfloat16 [2048, 512], P('mp', 'dp'), may hold values from -0.125 to 0.125
- attention_in: bfloat16 [3, 512, 512], P(None, 'dp', 'mp'), may hold values from -0.25 to 0.25
- attention_out: bfloat16 [512, 512], P('mp', 'dp'), may hold values from -6 to 6
- relative_bias: bfloat16 [8, 4096], P('mp', 'dp'), may hold values from -6 to 300
- pointwise_in: bfloat16 [2, 512, 512], P(None, 'dp', 'mp'), may hold values from -0.25 to 0.25
- depthwise: bfloat16 [512, 31], P(('mp', 'dp')), may hold values from -1 to 1
- batch_norm: bfloat16 [2, 512], P(None, ('mp', 'dp')), may hold values from 0.5 to 1.5
- pointwise_out: bfloat16 [512, 512], P('mp', 'dp'), may hold values from -0.25 to 0.25
- late_up: bfloat16 [512, 2048], P('dp', 'mp'), may hold values from -0.25 to 0.25
- late_down: bfloat16 [2048, 512], P('mp', 'dp'), may hold values from -0.125 to 0.125
- norm_gains: bfloat16 [5, 512], P(None, 'dp'), may hold values from 0.5 to 1.5
Outputs:
- block_output: bfloat16 [2, 8192, 512], P(None, ('dp', 'mp'))
- input_grad: float32 [2, 8192, 512], P(None, ('dp', 'mp'))
- early_up_grad: float32 [512, 2048], P('dp', 'mp')
- early_down_grad: float32 [2048, 512], P('mp', 'dp')
- attention_in_grad: float32 [3, 512, 512], P(None, 'dp', 'mp')
- attention_out_grad: float32 [512, 512], P('mp', 'dp')
- relative_bias_grad: float32 [8, 4096], P('mp', 'dp')
- pointwise_in_grad: float32 [2, 512, 512], P(None, 'dp', 'mp')
- depthwise_grad: float32 [512, 31], P(('mp', 'dp'))
- batch_norm_grad: float32 [2, 512], P(None, ('mp', 'dp'))
- pointwise_out_grad: float32 [512, 512], P('mp', 'dp')
- late_up_grad: float32 [512, 2048], P('dp', 'mp')
- late_down_grad: float32 [2048, 512], P('mp', 'dp')
- norm_gains_grad: float32 [5, 512], P(None, 'dp')
The draws below stay inside these ranges and needn't reach their ends.
All inputs are finite; a program needn't handle non-finite values.
Results may differ from the reference program's by a relative error of at most 0.035.
Values may be sent and summed in bfloat16 or wider, within the bound.
No kernel may reach another device: no remote copies, remote signals or barrier semaphores. Data moves between devices by JAX's collectives and lax.ppermute only.
A program may use at most 320 MiB of HBM per device.

```python
import jax
import jax.numpy as jnp
from jax import lax

D = 512
H = 8
HD = 64
FF = 2048
KERNEL = 31
TOK_DEV = 1024
MB = 2
TOKENS = 8192
SEQ = 2048
N_MP = 4


def draw_relative_bias(key, part):
    span = 4 * TOK_DEV
    base_key = jax.random.fold_in(key, 0)
    base = jnp.clip(jax.random.normal(base_key, (H, span), jnp.float32), -6.0, 6.0)
    return base.astype(jnp.bfloat16)


def steps_of(own_key, shape, cuts, smallest, top_value):
    level, own = 1.0, jax.random.fold_in(own_key, 6)
    for dim, blocks in cuts:
        steps = jnp.exp(jax.random.uniform(jax.random.fold_in(own, dim), (blocks,), jnp.float32, smallest / len(cuts), top_value / len(cuts)))
        level = level * jnp.repeat(steps, shape[dim] // blocks).reshape([-1 if axis == dim else 1 for axis in range(len(shape))])
    return level


def noise(key, dims, spread, most, cuts=(), kind=jnp.bfloat16):
    level = steps_of(key, dims, cuts, -0.22, 0.18) if cuts else 1.0
    entries = jax.random.normal(key, dims, jnp.float32) * spread * level
    return jnp.minimum(jnp.maximum(entries, -most), most).astype(kind)


def setup_inputs(seed: int = 0) -> dict:
    arg_keys = jax.random.split(jax.random.key(seed), 15)
    block_input = noise(arg_keys[0], (MB, TOKENS, D), 1.0, 6.0, ((1, 8),))
    out_cotangent = noise(arg_keys[1], (MB, TOKENS, D), 1.0, 6.0, ((1, 8),))
    early_up = noise(arg_keys[2], (D, FF), D ** -0.5, 0.25, ((0, 8), (1, 4)))
    early_down = noise(arg_keys[3], (FF, D), FF ** -0.5, 0.125, ((0, 4), (1, 8)))
    attention_in = noise(arg_keys[4], (3, D, D), D ** -0.5, 0.25, ((1, 8), (2, 4)))
    attention_out = noise(arg_keys[5], (D, D), (max(1, 3 * D // (2 * TOK_DEV))) ** -0.5, 6.0, ((0, 4), (1, 8)))
    relative_bias = draw_relative_bias(jax.random.fold_in(arg_keys[14], 71), 0)
    pointwise_in = noise(arg_keys[7], (2, D, D), D ** -0.5, 0.25, ((1, 8), (2, 4)))
    depthwise = noise(arg_keys[8], (D, KERNEL), KERNEL ** -0.5, 1.0, ((0, 32),))
    batch_norm = jnp.clip(0.5 + 1.0 * jax.random.uniform(arg_keys[9], (2, D), jnp.float32) ** steps_of(arg_keys[9], (2, D), ((1, 32),), -0.2, 0.2), 0.5, 1.5).astype(jnp.bfloat16)
    pointwise_out = noise(arg_keys[10], (D, D), D ** -0.5, 0.25, ((0, 4), (1, 8)))
    late_up = noise(arg_keys[11], (D, FF), D ** -0.5, 0.25, ((0, 8), (1, 4)))
    late_down = noise(arg_keys[12], (FF, D), FF ** -0.5, 0.125, ((0, 4), (1, 8)))
    norm_gains = jnp.clip(1.0 + 0.1 * jax.random.normal(arg_keys[13], (5, D), jnp.float32), 0.5, 1.5).astype(jnp.bfloat16)
    return dict(block_input=block_input, out_cotangent=out_cotangent, early_up=early_up, early_down=early_down, attention_in=attention_in, attention_out=attention_out, relative_bias=relative_bias, pointwise_in=pointwise_in, depthwise=depthwise, batch_norm=batch_norm, pointwise_out=pointwise_out, late_up=late_up, late_down=late_down, norm_gains=norm_gains)


EPS = 1e-05

def round_trip(value):
    return lax.optimization_barrier(value.astype(jnp.bfloat16)).astype(jnp.float32)

def grouped_sum(left, right):
    parts = jnp.einsum('tgk,gkd->gtd', left.astype(jnp.float32), right.astype(jnp.float32))
    return lax.optimization_barrier(jnp.sum(round_trip(parts), axis=0))

def split_cols(matrix, groups):
    return matrix.reshape(matrix.shape[0], groups, matrix.shape[1] // groups)

def split_rows(matrix, groups):
    return matrix.reshape(groups, matrix.shape[0] // groups, matrix.shape[1])

def stacked_left(stacked, groups):
    count, tokens_n, inner = stacked.shape
    part = inner // groups
    return stacked.reshape(count, tokens_n, groups, part).transpose(1, 2, 0, 3).reshape(tokens_n, groups, count * part)

def stacked_right(weights, groups):
    count, width, inner = weights.shape
    part = inner // groups
    return weights.reshape(count, width, groups, part).transpose(2, 0, 3, 1).reshape(groups, count * part, width)

def swish_grad(value):
    logistic = jax.nn.sigmoid(value)
    return logistic * (1.0 + value * (1.0 - logistic))

def layer_norm(value, gain):
    centred = value - lax.optimization_barrier(jnp.mean(value, axis=-1, keepdims=True))
    inverse = lax.rsqrt(lax.optimization_barrier(jnp.mean(centred * centred, axis=-1, keepdims=True)) + EPS)
    normed = centred * inverse
    return (normed * gain, normed, inverse)

def norm_back(normed, inverse, gain, upstream):
    scaled = upstream * gain
    inner = scaled - lax.optimization_barrier(jnp.mean(scaled, axis=-1, keepdims=True)) - normed * lax.optimization_barrier(jnp.mean(scaled * normed, axis=-1, keepdims=True))
    return (inverse * inner, lax.optimization_barrier(jnp.sum(upstream * normed, axis=0)))

def sequence_scores(query, keys, table):
    length = query.shape[0]
    position = jnp.arange(length, dtype=jnp.int32)
    offsets = (position[None, :] - position[:, None] + length).astype(jnp.int32)
    raw = jnp.einsum('thd,uhd->htu', query.astype(jnp.float32), keys.astype(jnp.float32))
    return (raw * query.shape[-1] ** (-0.5) + jnp.take(table, offsets, axis=1), offsets)

def attend_forward(query, keys, values, table):
    scores, offsets = sequence_scores(query, keys, table)
    top = lax.optimization_barrier(jnp.max(scores, axis=-1, keepdims=True))
    log_total = top + jnp.log(lax.optimization_barrier(jnp.sum(jnp.exp(scores - top), axis=-1, keepdims=True)))
    probs = jnp.exp(scores - log_total).astype(jnp.bfloat16)
    context = jnp.einsum('htu,uhd->thd', probs.astype(jnp.float32), values.astype(jnp.float32)).astype(jnp.bfloat16)
    return (context.reshape(query.shape[0], -1), log_total)

def attend_backward(query, keys, values, d_context, log_total, table):
    scores, offsets = sequence_scores(query, keys, table)
    probs_full = jnp.exp(scores - log_total)
    probs = probs_full.astype(jnp.bfloat16).astype(jnp.float32)
    d_probs = jnp.einsum('thd,uhd->htu', d_context.astype(jnp.float32), values.astype(jnp.float32))
    row_dot = lax.optimization_barrier(jnp.sum(probs_full * d_probs, axis=-1, keepdims=True))
    d_scores = probs_full * (d_probs - row_dot)
    d_table = jnp.zeros(table.shape, jnp.float32).at[:, offsets].add(d_scores)
    d_rounded = d_scores.astype(jnp.bfloat16).astype(jnp.float32)
    scale = query.shape[-1] ** (-0.5)
    d_query = (scale * jnp.einsum('htu,uhd->thd', d_rounded, keys.astype(jnp.float32))).astype(jnp.bfloat16)
    d_keys = (scale * jnp.einsum('htu,thd->uhd', d_rounded, query.astype(jnp.float32))).astype(jnp.bfloat16)
    d_values = jnp.einsum('htu,thd->uhd', probs, d_context.astype(jnp.float32)).astype(jnp.bfloat16)
    return (d_query, d_keys, d_values, d_table)

def reference(block_input, out_cotangent, early_up, early_down, attention_in, attention_out, relative_bias, pointwise_in, depthwise, batch_norm, pointwise_out, late_up, late_down, norm_gains):
    groups = N_MP
    gains = norm_gains.astype(jnp.float32)
    table = relative_bias.astype(jnp.float32)
    taps = depthwise.astype(jnp.float32)
    bn_gain = batch_norm[0].astype(jnp.float32)
    bn_shift = batch_norm[1].astype(jnp.float32)
    margin = (KERNEL - 1) // 2
    sequences = TOKENS // SEQ
    totals = None
    outputs = []
    input_grads = []
    for batch in range(MB):
        start = block_input[batch].astype(jnp.float32)
        first_out, first_normed, first_inv = layer_norm(start, gains[0])
        first_act = first_out.astype(jnp.bfloat16)
        first_pre = jnp.dot(first_act, early_up, preferred_element_type=jnp.float32)
        first_hidden = jax.nn.silu(first_pre).astype(jnp.bfloat16)
        after_first = start + 0.5 * grouped_sum(split_cols(first_hidden, groups), split_rows(early_down, groups))
        second_out, second_normed, second_inv = layer_norm(after_first, gains[1])
        second_act = second_out.astype(jnp.bfloat16)
        projected = jnp.einsum('td,idk->itk', second_act.astype(jnp.float32), attention_in.astype(jnp.float32)).astype(jnp.bfloat16)
        heads = projected.reshape(3, sequences, SEQ, H, HD)

        def forward_one(item):
            return attend_forward(item[0], item[1], item[2], table)
        context, log_total = lax.map(forward_one, (heads[0], heads[1], heads[2]))
        context = context.reshape(TOKENS, D)
        after_second = after_first + grouped_sum(split_cols(context, groups), split_rows(attention_out, groups))
        third_out, third_normed, third_inv = layer_norm(after_second, gains[2])
        third_act = third_out.astype(jnp.bfloat16)
        glu_pre = jnp.einsum('td,idc->itc', third_act.astype(jnp.float32), pointwise_in.astype(jnp.float32))
        gate_sig = jax.nn.sigmoid(glu_pre[1])
        glu = (glu_pre[0] * gate_sig).astype(jnp.bfloat16)
        extended = jnp.pad(glu.astype(jnp.float32).reshape(sequences, SEQ, D), ((0, 0), (margin, margin), (0, 0)))
        conv = jnp.zeros((sequences, SEQ, D), jnp.float32)
        for tap in range(KERNEL):
            conv = conv + taps[:, tap] * extended[:, tap:tap + SEQ]
        conv = conv.reshape(TOKENS, D)
        bmean = lax.optimization_barrier(jnp.mean(conv, axis=0))
        bvar = lax.optimization_barrier(jnp.mean(conv * conv, axis=0)) - bmean * bmean
        binv = lax.rsqrt(bvar + EPS)
        white = (conv - bmean) * binv
        bn_pre = bn_gain * white + bn_shift
        conv_act = jax.nn.silu(bn_pre).astype(jnp.bfloat16)
        after_third = after_second + grouped_sum(split_cols(conv_act, groups), split_rows(pointwise_out, groups))
        fourth_out, fourth_normed, fourth_inv = layer_norm(after_third, gains[3])
        fourth_act = fourth_out.astype(jnp.bfloat16)
        late_pre = jnp.dot(fourth_act, late_up, preferred_element_type=jnp.float32)
        late_hidden = jax.nn.silu(late_pre).astype(jnp.bfloat16)
        after_fourth = after_third + 0.5 * grouped_sum(split_cols(late_hidden, groups), split_rows(late_down, groups))
        fifth_out, fifth_normed, fifth_inv = layer_norm(after_fourth, gains[4])
        outputs.append(fifth_out.astype(jnp.bfloat16))
        upstream = out_cotangent[batch].astype(jnp.float32)
        d_fourth, gain_four = norm_back(fifth_normed, fifth_inv, gains[4], upstream)
        late_err = (0.5 * d_fourth).astype(jnp.bfloat16)
        grad_late_down = jnp.dot(late_hidden.T, late_err, preferred_element_type=jnp.float32)
        late_dpre = (jnp.dot(late_err, late_down.T, preferred_element_type=jnp.float32) * swish_grad(late_pre)).astype(jnp.bfloat16)
        grad_late_up = jnp.dot(fourth_act.T, late_dpre, preferred_element_type=jnp.float32)
        back, gain_three = norm_back(fourth_normed, fourth_inv, gains[3], grouped_sum(split_cols(late_dpre, groups), split_rows(late_up.T, groups)))
        d_third = d_fourth + back
        conv_err = d_third.astype(jnp.bfloat16)
        grad_pw_out = jnp.dot(conv_act.T, conv_err, preferred_element_type=jnp.float32)
        d_pre = jnp.dot(conv_err, pointwise_out.T, preferred_element_type=jnp.float32) * swish_grad(bn_pre)
        sum_pre = lax.optimization_barrier(jnp.sum(d_pre, axis=0))
        sum_cross = lax.optimization_barrier(jnp.sum(d_pre * white, axis=0))
        d_conv = binv * bn_gain * (d_pre - sum_pre / TOKENS - white * sum_cross / TOKENS)
        conv_seq = d_conv.reshape(sequences, SEQ, D)
        padded = jnp.pad(conv_seq, ((0, 0), (KERNEL - 1, KERNEL - 1), (0, 0)))
        d_ext = jnp.zeros((sequences, SEQ + 2 * margin, D), jnp.float32)
        tap_grads = []
        for tap in range(KERNEL):
            d_ext = d_ext + taps[:, tap] * padded[:, KERNEL - 1 - tap:KERNEL - 1 - tap + SEQ + 2 * margin]
            tap_grads.append(lax.optimization_barrier(jnp.sum(extended[:, tap:tap + SEQ] * conv_seq, axis=(0, 1))))
        grad_taps = jnp.stack(tap_grads, axis=1)
        grad_bn = jnp.stack([sum_cross, sum_pre])
        d_glu = d_ext[:, margin:margin + SEQ].reshape(TOKENS, D)
        d_lin = (d_glu * gate_sig).astype(jnp.bfloat16)
        d_gate = (d_glu * glu_pre[0] * gate_sig * (1.0 - gate_sig)).astype(jnp.bfloat16)
        both = jnp.stack([d_lin, d_gate])
        grad_pw_in = jnp.einsum('td,itc->idc', third_act.astype(jnp.float32), both.astype(jnp.float32))
        back, gain_two = norm_back(third_normed, third_inv, gains[2], grouped_sum(stacked_left(both, groups), stacked_right(pointwise_in, groups)))
        d_second = d_third + back
        att_err = d_second.astype(jnp.bfloat16)
        grad_att_out = jnp.dot(context.T, att_err, preferred_element_type=jnp.float32)
        d_context = jnp.dot(att_err, attention_out.T, preferred_element_type=jnp.float32).astype(jnp.bfloat16)

        def backward_one(item):
            return attend_backward(item[0], item[1], item[2], item[3], item[4], table)
        d_query, d_keys, d_values, d_tables = lax.map(backward_one, (heads[0], heads[1], heads[2], d_context.reshape(sequences, SEQ, H, HD), log_total))
        grad_table = lax.optimization_barrier(jnp.sum(d_tables, axis=0))
        stacked = jnp.stack([d_query, d_keys, d_values]).reshape(3, TOKENS, D)
        grad_att_in = jnp.einsum('td,itk->idk', second_act.astype(jnp.float32), stacked.astype(jnp.float32))
        back, gain_one = norm_back(second_normed, second_inv, gains[1], grouped_sum(stacked_left(stacked, groups), stacked_right(attention_in, groups)))
        d_first = d_second + back
        first_err = (0.5 * d_first).astype(jnp.bfloat16)
        grad_early_down = jnp.dot(first_hidden.T, first_err, preferred_element_type=jnp.float32)
        first_dpre = (jnp.dot(first_err, early_down.T, preferred_element_type=jnp.float32) * swish_grad(first_pre)).astype(jnp.bfloat16)
        grad_early_up = jnp.dot(first_act.T, first_dpre, preferred_element_type=jnp.float32)
        back, gain_zero = norm_back(first_normed, first_inv, gains[0], grouped_sum(split_cols(first_dpre, groups), split_rows(early_up.T, groups)))
        input_grads.append(d_first + back)
        grad_gains = jnp.stack([gain_zero, gain_one, gain_two, gain_three, gain_four])
        batch_grads = (grad_early_up, grad_early_down, grad_att_in, grad_att_out, grad_table, grad_pw_in, grad_taps, grad_bn, grad_pw_out, grad_late_up, grad_late_down, grad_gains)
        if totals is None:
            totals = batch_grads
        else:
            totals = tuple((old + new for old, new in zip(totals, batch_grads)))
    block_output = jnp.stack(outputs)
    input_grad = jnp.stack(input_grads)
    return (block_output, input_grad, totals[0], totals[1], totals[2], totals[3], totals[4], totals[5], totals[6], totals[7], totals[8], totals[9], totals[10], totals[11])
```

```python
import functools

import jax
import jax.numpy as jnp
from jax import lax
from jax.experimental import pallas as pl
from jax.experimental.pallas import tpu as pltpu
from jax.sharding import PartitionSpec as P

EPS = 1e-05
BF16 = jnp.bfloat16
F32 = jnp.float32
SUB = 128
NT = (((1,), (1,)), ((), ()))


def flip_pair(value, axis, bit):
    return lax.ppermute(value, axis, [(i, i ^ 1 << bit) for i in range(lax.axis_size(axis))])


def bits_of(axis):
    return (lax.axis_size(axis) - 1).bit_length()


def own_bit(axis, bit):
    return lax.shift_right_logical(lax.axis_index(axis), bit) & 1


def full_order():
    dp_bits, mp_bits = bits_of("dp"), bits_of("mp")
    dp_high = [("dp", bit) for bit in range(dp_bits - 1, 0, -1)]
    mp_high = [("mp", bit) for bit in range(mp_bits - 1, 0, -1)]
    first = dp_high + [("dp", 0)] + mp_high + [("mp", 0)]
    second = dp_high + mp_high + [("dp", 0)] + [("mp", 0)]
    return (first, second)


def gather_groups(shard, order):
    held = shard[None]
    done = []
    for axis, bit in order[:-1]:
        other = flip_pair(held, axis, bit)
        if axis == "mp":
            held = jnp.concatenate([held, other], axis=0)
        else:
            mine = own_bit(axis, bit) == 0
            place = 1 + sum(1 for b in done if b > bit)
            done.append(bit)
            held = jnp.stack([jnp.where(mine, held, other), jnp.where(mine, other, held)], axis=place)
    axis, bit = order[-1]
    other = flip_pair(held, axis, bit)

    def merged(value):
        return value.reshape((value.shape[0], -1) + shard.shape)

    return (merged(held), merged(other))


def kept_deltas():
    deltas = [0]
    for bit in range(bits_of("mp") - 1, 0, -1):
        deltas = deltas + [delta ^ 1 << bit for delta in deltas]
    return deltas


def scatter_groups(kept, sent, order):
    dp_bits = bits_of("dp")
    rows_shape = kept.shape[2:]
    axis, bit = order[-1]
    other = flip_pair(sent, axis, bit)
    total = kept.astype(F32) + other.astype(F32)
    held = total.astype(BF16).reshape((kept.shape[0],) + (2,) * dp_bits + rows_shape)
    left = list(range(dp_bits - 1, -1, -1))
    for axis, bit in reversed(order[:-1]):
        if axis == "mp":
            half = held.shape[0] // 2
            keep, send = held[:half], held[half:]
        else:
            place = 1 + left.index(bit)
            left.remove(bit)
            low = lax.index_in_dim(held, 0, place, keepdims=False)
            high = lax.index_in_dim(held, 1, place, keepdims=False)
            mine = own_bit(axis, bit) == 0
            keep, send = jnp.where(mine, low, high), jnp.where(mine, high, low)
        other = flip_pair(send, axis, bit)
        total = keep.astype(F32) + other.astype(F32)
        held = total.astype(BF16)
    return total.reshape(rows_shape)


def swap_groups(value, groups, delta):
    width = value.shape[-1] // groups
    parts = [value[..., (g ^ delta) * width : ((g ^ delta) + 1) * width] for g in range(groups)]
    return jnp.concatenate(parts, axis=-1)


def absolute_groups(value, groups):
    for bit in range((groups - 1).bit_length()):
        value = jnp.where(own_bit("mp", bit) == 0, value, swap_groups(value, groups, 1 << bit))
    return value


def channel_total(sums):
    groups = lax.axis_size("mp")
    for bit in range(bits_of("mp")):
        sums = sums + swap_groups(flip_pair(sums, "mp", bit), groups, 1 << bit)
    for bit in range(1, bits_of("dp")):
        sums = sums + flip_pair(sums, "dp", bit)
    return sums


def edge_rows(first_rows, last_rows, half_of_slot):
    groups = lax.axis_size("mp")
    place = lax.axis_index("mp")
    up = [(i, (i + 1) % groups) for i in range(groups)]
    down = [(i, (i - 1) % groups) for i in range(groups)]
    before = lax.ppermute(absolute_groups(last_rows, groups), "mp", up)
    after = lax.ppermute(absolute_groups(first_rows, groups), "mp", down)
    before = absolute_groups(before, groups)
    after = absolute_groups(after, groups)
    second = half_of_slot[:, None, None] == 1
    nothing = jnp.zeros_like(before)
    before = jnp.where(place == 0, jnp.where(second, before[::-1], nothing), before)
    after = jnp.where(place == groups - 1, jnp.where(second, nothing, after[::-1]), after)
    return (before, after)


def swish_grad(value):
    logistic = jax.nn.sigmoid(value)
    return logistic * (1.0 + value * (1.0 - logistic))


def normed_of(value):
    centred = value - jnp.mean(value, axis=-1, keepdims=True)
    inverse = lax.rsqrt(jnp.mean(centred * centred, axis=-1, keepdims=True) + EPS)
    return (centred * inverse, inverse)


def norm_back(normed, inverse, gain, upstream):
    scaled = upstream * gain
    inner = (
        scaled
        - jnp.mean(scaled, axis=-1, keepdims=True)
        - normed * jnp.mean(scaled * normed, axis=-1, keepdims=True)
    )
    return (inverse * inner, jnp.sum(upstream * normed, axis=0, keepdims=True))


def mm(left, right):
    return jnp.dot(left, right, preferred_element_type=F32)


def mm_nt(left, right):
    return lax.dot_general(left, right, NT, preferred_element_type=F32)


def ffn_forward_kernel(v_ref, gain_ref, ua_ref, ub_ref, da_ref, db_ref, out_ref):
    value = v_ref[...]
    normed, _ = normed_of(value)
    active = (normed * gain_ref[...]).astype(BF16)
    total = jnp.zeros_like(value)
    for up_ref, down_ref in ((ua_ref, da_ref), (ub_ref, db_ref)):
        for g in range(up_ref.shape[0]):
            pre = mm(active, up_ref[g])
            hidden = (pre * jax.nn.sigmoid(pre)).astype(BF16)
            total += mm_nt(hidden, down_ref[g])
    out_ref[...] = value + 0.5 * total


def ffn_forward(value, gain, up, down):
    return pl.pallas_call(
        ffn_forward_kernel,
        out_shape=jax.ShapeDtypeStruct(value.shape, F32),
        name="ffn_forward",
    )(value, gain, *up, *down)


def ffn_backward_kernel(
    v_ref, d_ref, gain_ref, ua_ref, ub_ref, da_ref, db_ref,
    out_ref, gua_ref, gub_ref, gda_ref, gdb_ref, gg_ref,
):
    normed, inverse = normed_of(v_ref[...])
    upstream = d_ref[...]
    active = (normed * gain_ref[...]).astype(BF16)
    error = (0.5 * upstream).astype(BF16)
    active_t = active.T
    error_t = error.T
    total = jnp.zeros_like(upstream)
    for up_ref, down_ref, gu_ref, gd_ref in (
        (ua_ref, da_ref, gua_ref, gda_ref),
        (ub_ref, db_ref, gub_ref, gdb_ref),
    ):
        for g in range(up_ref.shape[0]):
            pre = mm(active, up_ref[g])
            logistic = jax.nn.sigmoid(pre)
            hidden = (pre * logistic).astype(BF16)
            gd_ref[g] = mm(error_t, hidden).astype(BF16)
            d_hidden = mm(error, down_ref[g])
            d_pre = (d_hidden * (logistic * (1.0 + pre * (1.0 - logistic)))).astype(BF16)
            gu_ref[g] = mm(active_t, d_pre).astype(BF16)
            total += mm_nt(d_pre, up_ref[g])
    back, grad_gain = norm_back(normed, inverse, gain_ref[...], total)
    out_ref[...] = upstream + back
    gg_ref[...] = grad_gain


def ffn_backward(value, upstream, gain, up, down):
    weight = jax.ShapeDtypeStruct(up[0].shape, BF16)
    return pl.pallas_call(
        ffn_backward_kernel,
        out_shape=(
            jax.ShapeDtypeStruct(value.shape, F32),
            weight,
            weight,
            weight,
            weight,
            jax.ShapeDtypeStruct(gain.shape, F32),
        ),
        name="ffn_backward",
    )(value, upstream, gain, *up, *down)


def build_skew(line_ref, skew, heads, chunks):
    for h in range(heads):
        for c in range(chunks):
            start = SUB * (chunks - 1 - c)
            window = jnp.broadcast_to(line_ref[0, h : h + 1, start : start + 2 * SUB], (SUB, 2 * SUB))
            rolled = pltpu.roll(window, 0, 1, stride=1, stride_axis=0)
            skew[h, SUB * c : SUB * (c + 1), :] = rolled[:, SUB:]


def head_masks(width, heads, factor):
    lane = lax.broadcasted_iota(jnp.int32, (SUB, width), 1)
    size = width // heads
    return [
        jnp.where((lane >= h * size) & (lane < (h + 1) * size), factor, 0.0).astype(BF16)
        for h in range(heads)
    ]


def stack_heads(rows, masks):
    return jnp.concatenate([rows * mask for mask in masks], axis=0)


def diagonal_heads(value, heads):
    size = value.shape[0] // heads
    parts = [value[h * size : (h + 1) * size, h * SUB : (h + 1) * SUB] for h in range(heads)]
    return jnp.concatenate(parts, axis=0)


def attend_forward_kernel(pieces, heads, qpos, kpos, q_ref, line_ref, *refs):
    k_refs = refs[:pieces]
    v_refs = refs[pieces : 2 * pieces]
    ctx_ref, lse_ref, skew, scores, v_t = refs[2 * pieces :]
    rows, width = q_ref.shape
    block = rows // 2
    chunks = skew.shape[1] // SUB
    middle = skew.shape[1] // 2
    build_skew(line_ref, skew, heads, chunks)
    for p in range(pieces):
        v_t[:, p * rows : (p + 1) * rows] = v_refs[p][0].T
    masks = head_masks(width, heads, (width // heads) ** (-0.5))

    def step(qb, carry):
        start = pl.multiple_of(qb * SUB, SUB)
        query = stack_heads(q_ref[pl.ds(start, SUB), :], masks)
        top = jnp.full((1, heads * SUB), -jnp.inf, F32)
        for c in range(2 * pieces):
            keys = k_refs[c // 2][0, (c % 2) * block : (c % 2 + 1) * block, :]
            raw = mm_nt(keys, query)
            offset = pl.multiple_of(kpos[c] - qpos[qb] + middle, SUB)
            bias = [skew[h, pl.ds(offset, block), :] for h in range(heads)]
            raw = raw + jnp.concatenate(bias, axis=1)
            scores[c * block : (c + 1) * block, :] = raw
            top = jnp.maximum(top, jnp.max(raw, axis=0, keepdims=True))
        total = jnp.zeros((1, heads * SUB), F32)
        out_t = jnp.zeros((width, heads * SUB), F32)
        for c in range(2 * pieces):
            prob = jnp.exp(scores[c * block : (c + 1) * block, :] - top)
            total = total + jnp.sum(prob, axis=0, keepdims=True)
            out_t = out_t + mm(v_t[:, c * block : (c + 1) * block], prob.astype(BF16))
        out_t = out_t / total
        ctx_ref[pl.ds(start, SUB), :] = diagonal_heads(out_t, heads).T.astype(BF16)
        lse_ref[0, pl.ds(qb, 1), :] = top + jnp.log(total)
        return carry

    lax.fori_loop(0, rows // SUB, step, 0)


def attend_backward_kernel(pieces, heads, qpos, kpos, q_ref, d_ref, lse_ref, line_ref, *refs):
    k_refs = refs[:pieces]
    v_refs = refs[pieces : 2 * pieces]
    dq_ref = refs[2 * pieces]
    dkv_refs = refs[2 * pieces + 1 : 3 * pieces + 1]
    line_grad, skew, skew_grad, probs, d_probs, k_t, dk, dv = refs[3 * pieces + 1 :]
    rows, width = q_ref.shape
    block = rows // 2
    chunks = skew.shape[1] // SUB
    middle = skew.shape[1] // 2
    scale = (width // heads) ** (-0.5)
    build_skew(line_ref, skew, heads, chunks)
    skew_grad[...] = jnp.zeros_like(skew_grad)
    dk[...] = jnp.zeros_like(dk)
    dv[...] = jnp.zeros_like(dv)
    for p in range(pieces):
        k_t[:, p * rows : (p + 1) * rows] = k_refs[p][0].T
    scaled_masks = head_masks(width, heads, scale)
    plain_masks = head_masks(width, heads, 1.0)

    def step(qb, carry):
        start = pl.multiple_of(qb * SUB, SUB)
        query = stack_heads(q_ref[pl.ds(start, SUB), :], scaled_masks)
        error = stack_heads(d_ref[pl.ds(start, SUB), :], plain_masks)
        lse = lse_ref[0, pl.ds(qb, 1), :]
        dot_sum = jnp.zeros((1, heads * SUB), F32)
        for c in range(2 * pieces):
            part = slice((c % 2) * block, (c % 2 + 1) * block)
            span = slice(c * block, (c + 1) * block)
            raw = mm_nt(k_refs[c // 2][0, part, :], query)
            offset = pl.multiple_of(kpos[c] - qpos[qb] + middle, SUB)
            bias = [skew[h, pl.ds(offset, block), :] for h in range(heads)]
            prob = jnp.exp(raw + jnp.concatenate(bias, axis=1) - lse)
            d_prob = mm_nt(v_refs[c // 2][0, part, :], error)
            probs[span, :] = prob
            d_probs[span, :] = d_prob
            dot_sum = dot_sum + jnp.sum(prob * d_prob, axis=0, keepdims=True)
        dq_t = jnp.zeros((width, heads * SUB), F32)
        for c in range(2 * pieces):
            span = slice(c * block, (c + 1) * block)
            prob = probs[span, :]
            d_score = prob * (d_probs[span, :] - dot_sum)
            offset = pl.multiple_of(kpos[c] - qpos[qb] + middle, SUB)
            for h in range(heads):
                skew_grad[h, pl.ds(offset, block), :] += d_score[:, h * SUB : (h + 1) * SUB]
            rounded = d_score.astype(BF16)
            dq_t = dq_t + mm(k_t[:, span], rounded)
            dk[span, :] += mm(rounded, query)
            dv[span, :] += mm(prob.astype(BF16), error)
        dq_ref[pl.ds(start, SUB), :] = (diagonal_heads(dq_t, heads).T * scale).astype(BF16)
        return carry

    lax.fori_loop(0, rows // SUB, step, 0)
    for p in range(pieces):
        dkv_refs[p][0] = dk[p * rows : (p + 1) * rows, :].astype(BF16)
        dkv_refs[p][1] = dv[p * rows : (p + 1) * rows, :].astype(BF16)
    line_grad[...] = jnp.zeros_like(line_grad)
    for h in range(heads):
        for c in range(chunks):
            block_grad = skew_grad[h, SUB * c : SUB * (c + 1), :]
            value = jnp.concatenate([jnp.zeros_like(block_grad), block_grad], axis=1)
            half = SUB // 2
            while half >= 8:
                value = value[:half] + pltpu.roll(value[half:], 2 * SUB - half, 1)
                half //= 2
            at = SUB * (chunks - 1 - c)
            line_grad[0, h, :, at : at + 2 * SUB] += value


def attention_specs(rows, width, pieces, deltas, line_shape):
    whole_q = pl.BlockSpec((rows, width), lambda j, *_: (0, j))
    line = pl.BlockSpec((1,) + line_shape[1:], lambda j, *_: (j, 0, 0))
    keys, values = [], []
    for p in range(pieces):
        keys.append(pl.BlockSpec((1, rows, width), lambda j, *_, d=deltas[p]: (0, 0, j ^ d)))
        values.append(pl.BlockSpec((1, rows, width), lambda j, *_, d=deltas[p]: (1, 0, j ^ d)))
    return (whole_q, line, keys, values)


def attend_forward(query, pairs, deltas, line, qpos, kpos):
    rows = query.shape[0]
    groups, heads = line.shape[0], line.shape[1]
    width = query.shape[1] // groups
    pieces = len(pairs)
    table = line.shape[2] - SUB
    steps = rows // SUB
    whole_q, line_spec, keys, values = attention_specs(rows, width, pieces, deltas, line.shape)
    return pl.pallas_call(
        functools.partial(attend_forward_kernel, pieces, heads),
        out_shape=(
            jax.ShapeDtypeStruct(query.shape, BF16),
            jax.ShapeDtypeStruct((groups, steps, heads * SUB), F32),
        ),
        grid_spec=pltpu.PrefetchScalarGridSpec(
            num_scalar_prefetch=2,
            grid=(groups,),
            in_specs=[whole_q, line_spec] + keys + values,
            out_specs=(
                whole_q,
                pl.BlockSpec((1, steps, heads * SUB), lambda j, *_: (j, 0, 0)),
            ),
            scratch_shapes=[
                pltpu.VMEM((heads, table, SUB), F32),
                pltpu.VMEM((pieces * rows, heads * SUB), F32),
                pltpu.VMEM((width, pieces * rows), BF16),
            ],
        ),
        name="attend_forward",
    )(qpos, kpos, query, line, *pairs, *pairs)


def attend_backward(query, d_context, lse, pairs, deltas, line, qpos, kpos):
    rows = query.shape[0]
    groups, heads = line.shape[0], line.shape[1]
    width = query.shape[1] // groups
    pieces = len(pairs)
    table = line.shape[2] - SUB
    steps = rows // SUB
    whole_q, line_spec, keys, values = attention_specs(rows, width, pieces, deltas, line.shape)
    lse_spec = pl.BlockSpec((1, steps, heads * SUB), lambda j, *_: (j, 0, 0))
    pair_specs = [
        pl.BlockSpec((2, rows, width), lambda j, *_, d=deltas[p]: (0, 0, j ^ d))
        for p in range(pieces)
    ]
    return pl.pallas_call(
        functools.partial(attend_backward_kernel, pieces, heads),
        out_shape=(
            (jax.ShapeDtypeStruct(query.shape, BF16),)
            + tuple(jax.ShapeDtypeStruct(pairs[0].shape, BF16) for _ in range(pieces))
            + (jax.ShapeDtypeStruct((groups, heads, 8, line.shape[2]), F32),)
        ),
        grid_spec=pltpu.PrefetchScalarGridSpec(
            num_scalar_prefetch=2,
            grid=(groups,),
            in_specs=[whole_q, whole_q, lse_spec, line_spec] + keys + values,
            out_specs=(
                (whole_q,)
                + tuple(pair_specs)
                + (pl.BlockSpec((1, heads, 8, line.shape[2]), lambda j, *_: (j, 0, 0, 0)),)
            ),
            scratch_shapes=[
                pltpu.VMEM((heads, table, SUB), F32),
                pltpu.VMEM((heads, table, SUB), F32),
                pltpu.VMEM((pieces * rows, heads * SUB), F32),
                pltpu.VMEM((pieces * rows, heads * SUB), F32),
                pltpu.VMEM((width, pieces * rows), BF16),
                pltpu.VMEM((pieces * rows, width), F32),
                pltpu.VMEM((pieces * rows, width), F32),
            ],
        ),
        name="attend_backward",
    )(qpos, kpos, query, d_context, lse, line, *pairs, *pairs)


def body(
    block_input,
    out_cotangent,
    early_up,
    early_down,
    attention_in,
    attention_out,
    relative_bias,
    pointwise_in,
    depthwise,
    batch_norm,
    pointwise_out,
    late_up,
    late_down,
    norm_gains,
):
    dp_n, mp_n = lax.axis_size("dp"), lax.axis_size("mp")
    held_rows = block_input.shape[1]
    features = block_input.shape[2]
    block = held_rows // mp_n
    rows = 2 * block
    batch_rows = held_rows * dp_n
    batch = lax.axis_index("dp") % 2
    place = lax.axis_index("mp")
    shard_rows, part = early_up.shape
    heads, table_part = relative_bias.shape
    table_n = table_part * dp_n
    channel_part, kernel = depthwise.shape
    margin = (kernel - 1) // 2
    order_a, order_b = full_order()
    kept = kept_deltas()
    deltas = kept + [delta ^ 1 for delta in kept]

    def exchanged(value):
        mine = lax.dynamic_slice_in_dim(value, place * block, block, 1)
        own = lax.dynamic_index_in_dim(mine, batch, 0, keepdims=False)
        away = lax.dynamic_index_in_dim(mine, 1 - batch, 0, keepdims=False)
        return jnp.concatenate([own, flip_pair(away, "dp", 0)], axis=0).astype(F32)

    small = jnp.concatenate(
        [
            relative_bias.reshape(-1),
            depthwise.reshape(-1),
            batch_norm.reshape(-1),
            norm_gains.reshape(-1),
        ]
    )
    small_n = small.shape[0]
    small_rows = -(-small_n // (8 * part)) * 8
    small = jnp.pad(small, (0, small_rows * part - small_n)).reshape(small_rows, part)
    early = gather_groups(jnp.concatenate([early_up, small], axis=0), order_a)
    early_u = tuple(
        side[:, :, :shard_rows].reshape(side.shape[0], features, part) for side in early
    )
    early_d = tuple(
        side.reshape(side.shape[0], features, part)
        for side in gather_groups(early_down.T, order_b)
    )
    start = exchanged(block_input)

    tiny = jnp.concatenate(
        [side[:, :, shard_rows:].reshape(side.shape[0], dp_n, -1) for side in early], axis=0
    )
    tiny = jnp.stack([tiny[deltas.index(j)] for j in range(mp_n)]).astype(F32)
    ends = [heads * table_part, heads * table_part + channel_part * kernel]
    ends.append(ends[1] + 2 * channel_part)
    ends.append(small_n)
    bias_table = (
        tiny[:, :, : ends[0]]
        .reshape(mp_n, dp_n, heads, table_part)
        .transpose(0, 2, 1, 3)
        .reshape(mp_n, heads, table_n)
    )
    taps = tiny[:, :, ends[0] : ends[1]].reshape(mp_n * dp_n * channel_part, kernel)
    bn_both = (
        tiny[:, :, ends[1] : ends[2]]
        .reshape(mp_n, dp_n, 2, channel_part)
        .transpose(2, 0, 1, 3)
        .reshape(2, mp_n * dp_n * channel_part)
    )
    bn_gain, bn_shift = bn_both[0:1], bn_both[1:2]
    gains = (
        tiny[0, :, ends[2] : ends[3]].reshape(dp_n, 5, shard_rows).transpose(1, 0, 2).reshape(5, features)
    )
    gain = [gains[i : i + 1] for i in range(5)]
    line = jnp.concatenate(
        [
            jnp.zeros((mp_n, heads, 1), F32),
            jnp.flip(bias_table[:, :, 1:], axis=2),
            jnp.zeros((mp_n, heads, SUB), F32),
        ],
        axis=2,
    )

    middle_shard = jnp.concatenate(
        [
            attention_in[0],
            attention_in[1],
            attention_in[2],
            attention_out.T,
            pointwise_in[0],
            pointwise_in[1],
            pointwise_out.T,
        ],
        axis=1,
    )
    head_width = attention_out.shape[0]
    channels = mp_n * head_width
    middle = gather_groups(middle_shard, order_b)
    middle = [
        side[g].reshape(features, middle_shard.shape[1])
        for side in middle
        for g in range(side.shape[0])
    ]

    def columns(index):
        return jnp.concatenate(
            [
                middle[deltas.index(j)][:, index * head_width : (index + 1) * head_width]
                for j in range(mp_n)
            ],
            axis=1,
        )

    w_qkv = jnp.stack([columns(0), columns(1), columns(2)])
    w_out_t = columns(3)
    w_pw = jnp.stack([columns(4), columns(5)])
    w_pw_out_t = columns(6)
    late = gather_groups(jnp.concatenate([late_up, late_down.T], axis=1), order_a)
    late = [side.reshape(side.shape[0], features, 2 * part) for side in late]
    late_u = tuple(side[:, :, :part] for side in late)
    late_d = tuple(side[:, :, part:] for side in late)

    half_of_slot = jnp.stack([batch, 1 - batch]).astype(jnp.int32)
    sub_n = block // SUB
    qpos = (
        half_of_slot[:, None] * held_rows
        + place * block
        + SUB * jnp.arange(sub_n, dtype=jnp.int32)[None, :]
    ).reshape(-1)
    kpos = jnp.stack(
        [half_of_slot[r] * held_rows + (place ^ delta) * block for delta in deltas for r in (0, 1)]
    )
    after_first = ffn_forward(start, gain[0], early_u, early_d)
    second_n, second_inv = normed_of(after_first)
    second_act = (second_n * gain[1]).astype(BF16)
    projected = jnp.einsum("td,idk->itk", second_act, w_qkv, preferred_element_type=F32).astype(BF16)
    query = projected[0]
    pairs = [projected[1:]]
    for bit in range(bits_of("mp") - 1, -1, -1):
        pairs = pairs + [flip_pair(pair, "mp", bit) for pair in pairs]
    narrow = head_width < SUB
    shifts = [0] * len(deltas) if narrow else deltas
    if narrow:
        pairs = [swap_groups(pair, mp_n, delta) for pair, delta in zip(pairs, deltas)]
        line = line.reshape(channels // SUB, -1, line.shape[2])
    context, lse = attend_forward(query, pairs, shifts, line, qpos, kpos)
    after_second = after_first + mm_nt(context, w_out_t)
    third_n, third_inv = normed_of(after_second)
    third_act = (third_n * gain[2]).astype(BF16)
    glu_pre = jnp.einsum("td,idc->itc", third_act, w_pw, preferred_element_type=F32)
    gate_sig = jax.nn.sigmoid(glu_pre[1])
    glu = (glu_pre[0] * gate_sig).astype(BF16).reshape(2, block, channels)
    edge = margin + 1
    before, after = edge_rows(glu[:, :edge], glu[:, block - edge :], half_of_slot)
    extended = jnp.concatenate([before[:, 1:], glu, after[:, :margin]], axis=1).astype(F32)
    conv = jnp.zeros((2, block, channels), F32)
    for tap in range(kernel):
        conv = conv + taps[:, tap] * extended[:, tap : tap + block]
    conv = conv.reshape(rows, channels)
    sums = channel_total(
        jnp.stack([jnp.sum(conv, axis=0), jnp.sum(conv * conv, axis=0)])
    )
    bmean = sums[0:1] / batch_rows
    bvar = sums[1:2] / batch_rows - bmean * bmean
    binv = lax.rsqrt(bvar + EPS)
    white = (conv - bmean) * binv
    bn_pre = bn_gain * white + bn_shift
    conv_act = jax.nn.silu(bn_pre).astype(BF16)
    after_third = after_second + mm_nt(conv_act, w_pw_out_t)
    after_fourth = ffn_forward(after_third, gain[3], late_u, late_d)
    fifth_n, fifth_inv = normed_of(after_fourth)
    final_rows = (fifth_n * gain[4]).astype(BF16)

    upstream = exchanged(out_cotangent)
    d_fourth, gain_four = norm_back(fifth_n, fifth_inv, gain[4], upstream)
    d_third, glu_a, glu_b, gld_a, gld_b, gain_three = ffn_backward(
        after_third, d_fourth, gain[3], late_u, late_d
    )

    def by_dp(value):
        return value.reshape(value.shape[0], dp_n, shard_rows, value.shape[2])

    own_late = scatter_groups(
        by_dp(jnp.concatenate([glu_a, gld_a], axis=2)),
        by_dp(jnp.concatenate([glu_b, gld_b], axis=2)),
        order_a,
    )
    conv_err = d_third.astype(BF16)
    grad_pw_out_t = mm(conv_err.T, conv_act)
    d_pre = mm(conv_err, w_pw_out_t) * swish_grad(bn_pre)
    local_sums = jnp.stack([jnp.sum(d_pre, axis=0), jnp.sum(d_pre * white, axis=0)])
    sums = channel_total(local_sums)
    d_conv = (
        binv * bn_gain * (d_pre - sums[0:1] / batch_rows - white * sums[1:2] / batch_rows)
    ).reshape(2, block, channels)
    before, after = edge_rows(d_conv[:, :edge], d_conv[:, block - edge :], half_of_slot)
    d_extended = jnp.concatenate([before[:, 1:], d_conv, after[:, :margin]], axis=1)
    d_glu = jnp.zeros((2, block, channels), F32)
    tap_grads = []
    for tap in range(kernel):
        d_glu = d_glu + taps[:, tap] * d_extended[:, kernel - 1 - tap : kernel - 1 - tap + block]
        tap_grads.append(jnp.sum(extended[:, tap : tap + block] * d_conv, axis=(0, 1)))
    grad_taps = jnp.stack(tap_grads, axis=1)
    d_glu = d_glu.reshape(rows, channels)
    d_lin = (d_glu * gate_sig).astype(BF16)
    d_gate = (d_glu * glu_pre[0] * gate_sig * (1.0 - gate_sig)).astype(BF16)
    d_both = jnp.stack([d_lin, d_gate])
    grad_pw = jnp.einsum("td,itc->idc", third_act, d_both, preferred_element_type=F32)
    back, gain_two = norm_back(
        third_n,
        third_inv,
        gain[2],
        jnp.einsum("itc,idc->td", d_both, w_pw, preferred_element_type=F32),
    )
    d_second = d_third + back
    att_err = d_second.astype(BF16)
    grad_out_t = mm(att_err.T, context)
    d_context = mm(att_err, w_out_t).astype(BF16)

    def group_pack(parts):
        parts = [value.astype(BF16) for value in parts]

        def of(delta):
            return jnp.concatenate(
                [value[:, delta * head_width : (delta + 1) * head_width] for value in parts], axis=1
            )

        half = len(kept)
        return tuple(
            by_dp(jnp.stack([of(delta) for delta in side]))
            for side in (deltas[:half], deltas[half:])
        )

    own_middle = scatter_groups(
        *group_pack([grad_out_t, grad_pw[0], grad_pw[1], grad_pw_out_t]), order_b
    )
    grads = attend_backward(query, d_context, lse, pairs, shifts, line, qpos, kpos)
    d_query, line_grad = grads[0], grads[-1].reshape(mp_n, heads, 8, line.shape[2])
    d_pairs = dict(zip(deltas, grads[1:-1]))
    if narrow:
        d_pairs = {delta: swap_groups(value, mp_n, delta) for delta, value in d_pairs.items()}
    for bit in range(bits_of("mp")):
        for delta in [d for d in d_pairs if d >> bit & 1]:
            other = flip_pair(d_pairs.pop(delta), "mp", bit)
            home = delta ^ 1 << bit
            d_pairs[home] = (d_pairs[home].astype(F32) + other.astype(F32)).astype(BF16)
    stacked = jnp.concatenate([d_query[None], d_pairs[0]], axis=0)
    grad_qkv = jnp.einsum("td,itk->idk", second_act, stacked, preferred_element_type=F32)
    back, gain_one = norm_back(
        second_n,
        second_inv,
        gain[1],
        jnp.einsum("itk,idk->td", stacked, w_qkv, preferred_element_type=F32),
    )
    own_qkv = scatter_groups(*group_pack([grad_qkv[0], grad_qkv[1], grad_qkv[2]]), order_b)
    d_first = d_second + back
    d_start, geu_a, geu_b, ged_a, ged_b, gain_zero = ffn_backward(
        start, d_first, gain[0], early_u, early_d
    )

    width = table_n + SUB
    lines = jnp.pad(line_grad, ((0, 0), (0, 0), (0, 0), (0, 8)))
    line_total = sum(lines[:, :, row, row : row + width] for row in range(8))
    grad_table = jnp.concatenate(
        [jnp.zeros((mp_n, heads, 1), F32), jnp.flip(line_total[:, :, 1:table_n], axis=2)], axis=2
    )
    grad_gains = jnp.concatenate([gain_zero, gain_one, gain_two, gain_three, gain_four], axis=0)
    tiny = jnp.concatenate(
        [
            grad_table.reshape(mp_n, heads, dp_n, table_part)
            .transpose(0, 2, 1, 3)
            .reshape(mp_n, dp_n, heads * table_part),
            grad_taps.reshape(mp_n, dp_n, channel_part * kernel),
            local_sums[::-1]
            .reshape(2, mp_n, dp_n, channel_part)
            .transpose(1, 2, 0, 3)
            .reshape(mp_n, dp_n, 2 * channel_part),
            jnp.broadcast_to(
                grad_gains.reshape(5, dp_n, shard_rows)
                .transpose(1, 0, 2)
                .reshape(1, dp_n, 5 * shard_rows),
                (mp_n, dp_n, 5 * shard_rows),
            ),
            jnp.zeros((mp_n, dp_n, small_rows * part - small_n), F32),
        ],
        axis=2,
    ).astype(BF16)
    tiny = jnp.stack([tiny[delta] for delta in deltas]).reshape(mp_n, dp_n, small_rows, part)
    half = len(kept)
    own_early_u = scatter_groups(
        jnp.concatenate([by_dp(geu_a), tiny[:half]], axis=2),
        jnp.concatenate([by_dp(geu_b), tiny[half:]], axis=2),
        order_a,
    )
    own_early_d = scatter_groups(by_dp(ged_a), by_dp(ged_b), order_b)
    tiny = own_early_u[shard_rows:].reshape(-1)

    def returned(value):
        own, away = value[:block], value[block:]
        other = flip_pair(away, "dp", 0)
        first = batch == 0
        return jnp.stack([jnp.where(first, own, other), jnp.where(first, other, own)])

    def middle_part(value, index):
        return value[:, index * head_width : (index + 1) * head_width]

    return (
        returned(final_rows),
        returned(d_start),
        own_early_u[:shard_rows],
        own_early_d.T,
        jnp.stack([middle_part(own_qkv, i) for i in range(3)]),
        middle_part(own_middle, 0).T,
        tiny[: ends[0]].reshape(heads, table_part),
        jnp.stack([middle_part(own_middle, 1), middle_part(own_middle, 2)]),
        tiny[ends[0] : ends[1]].reshape(channel_part, kernel),
        tiny[ends[1] : ends[2]].reshape(2, channel_part),
        middle_part(own_middle, 3).T,
        own_late[:, :part],
        own_late[:, part:].T,
        tiny[ends[2] : ends[3]].reshape(5, shard_rows),
    )


def solution(mesh):
    placed = (
        P(None, "dp", None),
        P(None, "dp", None),
        P("dp", "mp"),
        P("mp", "dp"),
        P(None, "dp", "mp"),
        P("mp", "dp"),
        P("mp", "dp"),
        P(None, "dp", "mp"),
        P(("mp", "dp"), None),
        P(None, ("mp", "dp")),
        P("mp", "dp"),
        P("dp", "mp"),
        P("mp", "dp"),
        P(None, "dp"),
    )
    returned = (P(None, ("dp", "mp"), None), P(None, ("dp", "mp"), None)) + placed[2:]
    return jax.shard_map(body, mesh=mesh, in_specs=placed, out_specs=returned, check_vma=False)
```

```python
import functools

import jax
import jax.numpy as jnp
from jax import lax
from jax.experimental import pallas as pl
from jax.experimental.pallas import tpu as pltpu
from jax.sharding import PartitionSpec as P

EPS = 1e-05
BF16 = jnp.bfloat16
F32 = jnp.float32
SUB = 128
NT = (((1,), (1,)), ((), ()))


def flip_pair(value, axis, bit):
    return lax.ppermute(value, axis, [(i, i ^ 1 << bit) for i in range(lax.axis_size(axis))])


def bits_of(axis):
    return (lax.axis_size(axis) - 1).bit_length()


def own_bit(axis, bit):
    return lax.shift_right_logical(lax.axis_index(axis), bit) & 1


def full_order():
    dp_bits, mp_bits = bits_of("dp"), bits_of("mp")
    dp_high = [("dp", bit) for bit in range(dp_bits - 1, 0, -1)]
    mp_high = [("mp", bit) for bit in range(mp_bits - 1, 0, -1)]
    first = dp_high + [("dp", 0)] + mp_high + [("mp", 0)]
    second = dp_high + mp_high + [("dp", 0)] + [("mp", 0)]
    return (first, second)


def gather_groups(shard, order):
    held = shard[None]
    done = []
    for axis, bit in order[:-1]:
        other = flip_pair(held, axis, bit)
        if axis == "mp":
            held = jnp.concatenate([held, other], axis=0)
        else:
            mine = own_bit(axis, bit) == 0
            place = 1 + sum(1 for b in done if b > bit)
            done.append(bit)
            held = jnp.stack([jnp.where(mine, held, other), jnp.where(mine, other, held)], axis=place)
    axis, bit = order[-1]
    other = flip_pair(held, axis, bit)

    def merged(value):
        return value.reshape((value.shape[0], -1) + shard.shape)

    return (merged(held), merged(other))


def kept_deltas():
    deltas = [0]
    for bit in range(bits_of("mp") - 1, 0, -1):
        deltas = deltas + [delta ^ 1 << bit for delta in deltas]
    return deltas


def scatter_groups(kept, sent, order):
    dp_bits = bits_of("dp")
    rows_shape = kept.shape[2:]
    axis, bit = order[-1]
    other = flip_pair(sent, axis, bit)
    total = kept.astype(F32) + other.astype(F32)
    held = total.astype(BF16).reshape((kept.shape[0],) + (2,) * dp_bits + rows_shape)
    left = list(range(dp_bits - 1, -1, -1))
    for axis, bit in reversed(order[:-1]):
        if axis == "mp":
            half = held.shape[0] // 2
            keep, send = held[:half], held[half:]
        else:
            place = 1 + left.index(bit)
            left.remove(bit)
            low = lax.index_in_dim(held, 0, place, keepdims=False)
            high = lax.index_in_dim(held, 1, place, keepdims=False)
            mine = own_bit(axis, bit) == 0
            keep, send = jnp.where(mine, low, high), jnp.where(mine, high, low)
        other = flip_pair(send, axis, bit)
        total = keep.astype(F32) + other.astype(F32)
        held = total.astype(BF16)
    return total.reshape(rows_shape)


def swap_groups(value, groups, delta):
    width = value.shape[-1] // groups
    parts = [value[..., (g ^ delta) * width : ((g ^ delta) + 1) * width] for g in range(groups)]
    return jnp.concatenate(parts, axis=-1)


def absolute_groups(value, groups):
    for bit in range((groups - 1).bit_length()):
        value = jnp.where(own_bit("mp", bit) == 0, value, swap_groups(value, groups, 1 << bit))
    return value


def channel_total(sums):
    groups = lax.axis_size("mp")
    for bit in range(bits_of("mp")):
        sums = sums + swap_groups(flip_pair(sums, "mp", bit), groups, 1 << bit)
    for bit in range(1, bits_of("dp")):
        sums = sums + flip_pair(sums, "dp", bit)
    return sums


def edge_rows(first_rows, last_rows, half_of_slot):
    groups = lax.axis_size("mp")
    place = lax.axis_index("mp")
    up = [(i, (i + 1) % groups) for i in range(groups)]
    down = [(i, (i - 1) % groups) for i in range(groups)]
    before = lax.ppermute(absolute_groups(last_rows, groups), "mp", up)
    after = lax.ppermute(absolute_groups(first_rows, groups), "mp", down)
    before = absolute_groups(before, groups)
    after = absolute_groups(after, groups)
    second = half_of_slot[:, None, None] == 1
    nothing = jnp.zeros_like(before)
    before = jnp.where(place == 0, jnp.where(second, before[::-1], nothing), before)
    after = jnp.where(place == groups - 1, jnp.where(second, nothing, after[::-1]), after)
    return (before, after)


def swish_grad(value):
    logistic = jax.nn.sigmoid(value)
    return logistic * (1.0 + value * (1.0 - logistic))


def normed_of(value):
    centred = value - jnp.mean(value, axis=-1, keepdims=True)
    inverse = lax.rsqrt(jnp.mean(centred * centred, axis=-1, keepdims=True) + EPS)
    return (centred * inverse, inverse)


def norm_back(normed, inverse, gain, upstream):
    scaled = upstream * gain
    inner = (
        scaled
        - jnp.mean(scaled, axis=-1, keepdims=True)
        - normed * jnp.mean(scaled * normed, axis=-1, keepdims=True)
    )
    return (inverse * inner, jnp.sum(upstream * normed, axis=0, keepdims=True))


def mm(left, right):
    return jnp.dot(left, right, preferred_element_type=F32)


def mm_nt(left, right):
    return lax.dot_general(left, right, NT, preferred_element_type=F32)


def ffn_forward_kernel(v_ref, gain_ref, ua_ref, ub_ref, da_ref, db_ref, out_ref):
    value = v_ref[...]
    normed, _ = normed_of(value)
    active = (normed * gain_ref[...]).astype(BF16)
    total = jnp.zeros_like(value)
    for up_ref, down_ref in ((ua_ref, da_ref), (ub_ref, db_ref)):
        for g in range(up_ref.shape[0]):
            pre = mm(active, up_ref[g])
            hidden = (pre * jax.nn.sigmoid(pre)).astype(BF16)
            total += mm_nt(hidden, down_ref[g])
    out_ref[...] = value + 0.5 * total


def ffn_forward(value, gain, up, down):
    return pl.pallas_call(
        ffn_forward_kernel,
        out_shape=jax.ShapeDtypeStruct(value.shape, F32),
        name="ffn_forward",
    )(value, gain, *up, *down)


def ffn_backward_kernel(
    v_ref, d_ref, gain_ref, ua_ref, ub_ref, da_ref, db_ref,
    out_ref, gua_ref, gub_ref, gda_ref, gdb_ref, gg_ref,
):
    normed, inverse = normed_of(v_ref[...])
    upstream = d_ref[...]
    active = (normed * gain_ref[...]).astype(BF16)
    error = (0.5 * upstream).astype(BF16)
    active_t = active.T
    error_t = error.T
    total = jnp.zeros_like(upstream)
    for up_ref, down_ref, gu_ref, gd_ref in (
        (ua_ref, da_ref, gua_ref, gda_ref),
        (ub_ref, db_ref, gub_ref, gdb_ref),
    ):
        for g in range(up_ref.shape[0]):
            pre = mm(active, up_ref[g])
            logistic = jax.nn.sigmoid(pre)
            hidden = (pre * logistic).astype(BF16)
            gd_ref[g] = mm(error_t, hidden).astype(BF16)
            d_hidden = mm(error, down_ref[g])
            d_pre = (d_hidden * (logistic * (1.0 + pre * (1.0 - logistic)))).astype(BF16)
            gu_ref[g] = mm(active_t, d_pre).astype(BF16)
            total += mm_nt(d_pre, up_ref[g])
    back, grad_gain = norm_back(normed, inverse, gain_ref[...], total)
    out_ref[...] = upstream + back
    gg_ref[...] = grad_gain


def ffn_backward(value, upstream, gain, up, down):
    weight = jax.ShapeDtypeStruct(up[0].shape, BF16)
    return pl.pallas_call(
        ffn_backward_kernel,
        out_shape=(
            jax.ShapeDtypeStruct(value.shape, F32),
            weight,
            weight,
            weight,
            weight,
            jax.ShapeDtypeStruct(gain.shape, F32),
        ),
        name="ffn_backward",
    )(value, upstream, gain, *up, *down)


def build_skew(line_ref, skew, heads, chunks):
    for h in range(heads):
        for c in range(chunks):
            start = SUB * (chunks - 1 - c)
            window = jnp.broadcast_to(line_ref[0, h : h + 1, start : start + 2 * SUB], (SUB, 2 * SUB))
            rolled = pltpu.roll(window, 0, 1, stride=1, stride_axis=0)
            skew[h, SUB * c : SUB * (c + 1), :] = rolled[:, SUB:]


def stack_heads(rows, heads, factor):
    lane = lax.broadcasted_iota(jnp.int32, rows.shape, 1)
    size = rows.shape[1] // heads
    return jnp.concatenate(
        [
            rows * jnp.where((lane >= h * size) & (lane < (h + 1) * size), factor, 0.0).astype(BF16)
            for h in range(heads)
        ],
        axis=0,
    )


def diagonal_heads(value, heads):
    size, columns = value.shape[0] // heads, value.shape[1] // heads
    parts = [
        value[h * size : (h + 1) * size, h * columns : (h + 1) * columns] for h in range(heads)
    ]
    return jnp.concatenate(parts, axis=0)


def tile_bias(skew, columns, block, offset_of):
    parts = [
        skew[h, pl.ds(pl.multiple_of(offset_of(qb), SUB), block), :] for h, qb in columns
    ]
    return jnp.concatenate(parts, axis=1)


def column_tiles(heads, steps):
    columns = [(h, qb) for h in range(heads) for qb in range(steps)]
    return [columns[i : i + 2] for i in range(0, len(columns), 2)]


def attend_forward_kernel(pieces, heads, qpos, kpos, q_ref, line_ref, *refs):
    k_refs = refs[:pieces]
    v_refs = refs[pieces : 2 * pieces]
    ctx_ref, lse_ref, ctx32_ref, skew, query, scores, probs, v_t = refs[2 * pieces :]
    rows, width = q_ref.shape
    block = rows // 2
    chunks = skew.shape[1] // SUB
    middle = skew.shape[1] // 2
    tiles = column_tiles(heads, rows // SUB)
    span = 2 * SUB
    build_skew(line_ref, skew, heads, chunks)
    for p in range(pieces):
        v_t[:width, p * rows : (p + 1) * rows] = v_refs[p][0].T
    v_t[width:, :] = jnp.ones_like(v_t[width:, :])
    query[...] = stack_heads(q_ref[...], heads, (width // heads) ** (-0.5))
    tops = [jnp.full((8, span), -jnp.inf, F32) for _ in tiles]
    for c in range(2 * pieces):
        keys = k_refs[c // 2][0, (c % 2) * block : (c % 2 + 1) * block, :]
        for t, tile in enumerate(tiles):
            raw = mm_nt(keys, query[t * span : (t + 1) * span, :])
            raw = raw + tile_bias(skew, tile, block, lambda qb: kpos[c] - qpos[qb] + middle)
            scores[c * block : (c + 1) * block, t * span : (t + 1) * span] = raw
            tops[t] = jnp.maximum(tops[t], jnp.max(raw.reshape(block // 8, 8, span), axis=0))
    tops = [jnp.max(top, axis=0, keepdims=True) for top in tops]
    for c in range(2 * pieces):
        for t in range(len(tiles)):
            part = (slice(c * block, (c + 1) * block), slice(t * span, (t + 1) * span))
            probs[part] = jnp.exp(scores[part] - tops[t]).astype(BF16)
    out_t = mm(v_t[...], probs[...])
    total = out_t[width : width + 1, :]
    out_t = out_t[:width, :] / total
    out = diagonal_heads(out_t, heads).T
    ctx_ref[...] = out.astype(BF16)
    ctx32_ref[...] = out
    lse_ref[0] = jnp.concatenate(tops, axis=1) + jnp.log(total)


def attend_backward_kernel(pieces, heads, qpos, kpos, q_ref, d_ref, ctx_ref, lse_ref, line_ref, *refs):
    k_refs = refs[:pieces]
    v_refs = refs[pieces : 2 * pieces]
    dq_ref = refs[2 * pieces]
    dkv_refs = refs[2 * pieces + 1 : 3 * pieces + 1]
    line_grad, skew, skew_grad, query, error, probs, d_scores, k_t = refs[3 * pieces + 1 :]
    rows, width = q_ref.shape
    block = rows // 2
    chunks = skew.shape[1] // SUB
    middle = skew.shape[1] // 2
    scale = (width // heads) ** (-0.5)
    size = width // heads
    tiles = column_tiles(heads, rows // SUB)
    span = 2 * SUB
    build_skew(line_ref, skew, heads, chunks)
    skew_grad[...] = jnp.zeros_like(skew_grad)
    for p in range(pieces):
        k_t[:, p * rows : (p + 1) * rows] = k_refs[p][0].T
    query[...] = stack_heads(q_ref[...], heads, scale)
    error[...] = stack_heads(d_ref[...], heads, 1.0)
    weighed = (d_ref[...].astype(F32) * ctx_ref[...]).T
    dot_sum = jnp.concatenate(
        [jnp.sum(weighed[h * size : (h + 1) * size], axis=0, keepdims=True) for h in range(heads)],
        axis=1,
    )
    lse = lse_ref[0]
    for c in range(2 * pieces):
        part = slice((c % 2) * block, (c % 2 + 1) * block)
        here = slice(c * block, (c + 1) * block)
        keys = k_refs[c // 2][0, part, :]
        values = v_refs[c // 2][0, part, :]
        for t, tile in enumerate(tiles):
            cols = slice(t * span, (t + 1) * span)
            raw = mm_nt(keys, query[cols, :])
            bias = tile_bias(skew, tile, block, lambda qb: kpos[c] - qpos[qb] + middle)
            prob = jnp.exp(raw + bias - lse[:, cols])
            d_score = prob * (mm_nt(values, error[cols, :]) - dot_sum[:, cols])
            probs[c % 2, :, cols] = prob.astype(BF16)
            d_scores[here, cols] = d_score.astype(BF16)
            for i, (h, qb) in enumerate(tile):
                offset = pl.multiple_of(kpos[c] - qpos[qb] + middle, SUB)
                skew_grad[h, pl.ds(offset, block), :] += d_score[:, i * SUB : (i + 1) * SUB]
        dkv_refs[c // 2][0, part, :] = mm(d_scores[here, :], query[...]).astype(BF16)
        dkv_refs[c // 2][1, part, :] = mm(probs[c % 2], error[...]).astype(BF16)
    dq_t = mm(k_t[...], d_scores[...])
    dq_ref[...] = (diagonal_heads(dq_t, heads).T * scale).astype(BF16)
    line_grad[...] = jnp.zeros_like(line_grad)
    for h in range(heads):
        for c in range(chunks):
            block_grad = skew_grad[h, SUB * c : SUB * (c + 1), :]
            value = jnp.concatenate([jnp.zeros_like(block_grad), block_grad], axis=1)
            half = SUB // 2
            while half >= 8:
                value = value[:half] + pltpu.roll(value[half:], 2 * SUB - half, 1)
                half //= 2
            at = SUB * (chunks - 1 - c)
            line_grad[0, h, :, at : at + 2 * SUB] += value


def attention_specs(rows, width, pieces, deltas, line_shape):
    whole_q = pl.BlockSpec((rows, width), lambda j, *_: (0, j))
    line = pl.BlockSpec((1,) + line_shape[1:], lambda j, *_: (j, 0, 0))
    keys, values = [], []
    for p in range(pieces):
        keys.append(pl.BlockSpec((1, rows, width), lambda j, *_, d=deltas[p]: (0, 0, j ^ d)))
        values.append(pl.BlockSpec((1, rows, width), lambda j, *_, d=deltas[p]: (1, 0, j ^ d)))
    return (whole_q, line, keys, values)


def attend_forward(query, pairs, deltas, line, qpos, kpos):
    rows = query.shape[0]
    groups, heads = line.shape[0], line.shape[1]
    width = query.shape[1] // groups
    pieces = len(pairs)
    table = line.shape[2] - SUB
    whole_q, line_spec, keys, values = attention_specs(rows, width, pieces, deltas, line.shape)
    return pl.pallas_call(
        functools.partial(attend_forward_kernel, pieces, heads),
        out_shape=(
            jax.ShapeDtypeStruct(query.shape, BF16),
            jax.ShapeDtypeStruct((groups, 1, heads * rows), F32),
            jax.ShapeDtypeStruct(query.shape, F32),
        ),
        grid_spec=pltpu.PrefetchScalarGridSpec(
            num_scalar_prefetch=2,
            grid=(groups,),
            in_specs=[whole_q, line_spec] + keys + values,
            out_specs=(
                whole_q,
                pl.BlockSpec((1, 1, heads * rows), lambda j, *_: (j, 0, 0)),
                whole_q,
            ),
            scratch_shapes=[
                pltpu.VMEM((heads, table, SUB), F32),
                pltpu.VMEM((heads * rows, width), BF16),
                pltpu.VMEM((pieces * rows, heads * rows), F32),
                pltpu.VMEM((pieces * rows, heads * rows), BF16),
                pltpu.VMEM((width + 16, pieces * rows), BF16),
            ],
        ),
        name="attend_forward",
    )(qpos, kpos, query, line, *pairs, *pairs)


def attend_backward(query, d_context, lse, context, pairs, deltas, line, qpos, kpos):
    rows = query.shape[0]
    groups, heads = line.shape[0], line.shape[1]
    width = query.shape[1] // groups
    pieces = len(pairs)
    table = line.shape[2] - SUB
    whole_q, line_spec, keys, values = attention_specs(rows, width, pieces, deltas, line.shape)
    lse_spec = pl.BlockSpec((1, 1, heads * rows), lambda j, *_: (j, 0, 0))
    pair_specs = [
        pl.BlockSpec((2, rows, width), lambda j, *_, d=deltas[p]: (0, 0, j ^ d))
        for p in range(pieces)
    ]
    return pl.pallas_call(
        functools.partial(attend_backward_kernel, pieces, heads),
        out_shape=(
            (jax.ShapeDtypeStruct(query.shape, BF16),)
            + tuple(jax.ShapeDtypeStruct(pairs[0].shape, BF16) for _ in range(pieces))
            + (jax.ShapeDtypeStruct((groups, heads, 8, line.shape[2]), F32),)
        ),
        grid_spec=pltpu.PrefetchScalarGridSpec(
            num_scalar_prefetch=2,
            grid=(groups,),
            in_specs=[whole_q, whole_q, whole_q, lse_spec, line_spec] + keys + values,
            out_specs=(
                (whole_q,)
                + tuple(pair_specs)
                + (pl.BlockSpec((1, heads, 8, line.shape[2]), lambda j, *_: (j, 0, 0, 0)),)
            ),
            scratch_shapes=[
                pltpu.VMEM((heads, table, SUB), F32),
                pltpu.VMEM((heads, table, SUB), F32),
                pltpu.VMEM((heads * rows, width), BF16),
                pltpu.VMEM((heads * rows, width), BF16),
                pltpu.VMEM((2, rows // 2, heads * rows), BF16),
                pltpu.VMEM((pieces * rows, heads * rows), BF16),
                pltpu.VMEM((width, pieces * rows), BF16),
            ],
        ),
        name="attend_backward",
    )(qpos, kpos, query, d_context, context, lse, line, *pairs, *pairs)


def body(
    block_input,
    out_cotangent,
    early_up,
    early_down,
    attention_in,
    attention_out,
    relative_bias,
    pointwise_in,
    depthwise,
    batch_norm,
    pointwise_out,
    late_up,
    late_down,
    norm_gains,
):
    dp_n, mp_n = lax.axis_size("dp"), lax.axis_size("mp")
    held_rows = block_input.shape[1]
    features = block_input.shape[2]
    block = held_rows // mp_n
    rows = 2 * block
    batch_rows = held_rows * dp_n
    batch = lax.axis_index("dp") % 2
    place = lax.axis_index("mp")
    shard_rows, part = early_up.shape
    heads, table_part = relative_bias.shape
    table_n = table_part * dp_n
    channel_part, kernel = depthwise.shape
    margin = (kernel - 1) // 2
    order_a, order_b = full_order()
    kept = kept_deltas()
    deltas = kept + [delta ^ 1 for delta in kept]

    def exchanged(value):
        mine = lax.dynamic_slice_in_dim(value, place * block, block, 1)
        own = lax.dynamic_index_in_dim(mine, batch, 0, keepdims=False)
        away = lax.dynamic_index_in_dim(mine, 1 - batch, 0, keepdims=False)
        return jnp.concatenate([own, flip_pair(away, "dp", 0)], axis=0).astype(F32)

    small = jnp.concatenate(
        [
            relative_bias.reshape(-1),
            depthwise.reshape(-1),
            batch_norm.reshape(-1),
            norm_gains.reshape(-1),
        ]
    )
    small_n = small.shape[0]
    small_rows = -(-small_n // (8 * part)) * 8
    small = jnp.pad(small, (0, small_rows * part - small_n)).reshape(small_rows, part)
    early = gather_groups(jnp.concatenate([early_up, small], axis=0), order_a)
    early_u = tuple(
        side[:, :, :shard_rows].reshape(side.shape[0], features, part) for side in early
    )
    early_d = tuple(
        side.reshape(side.shape[0], features, part)
        for side in gather_groups(early_down.T, order_b)
    )
    start = exchanged(block_input)

    tiny = jnp.concatenate(
        [side[:, :, shard_rows:].reshape(side.shape[0], dp_n, -1) for side in early], axis=0
    )
    tiny = jnp.stack([tiny[deltas.index(j)] for j in range(mp_n)]).astype(F32)
    ends = [heads * table_part, heads * table_part + channel_part * kernel]
    ends.append(ends[1] + 2 * channel_part)
    ends.append(small_n)
    bias_table = (
        tiny[:, :, : ends[0]]
        .reshape(mp_n, dp_n, heads, table_part)
        .transpose(0, 2, 1, 3)
        .reshape(mp_n, heads, table_n)
    )
    taps = tiny[:, :, ends[0] : ends[1]].reshape(mp_n * dp_n * channel_part, kernel)
    bn_both = (
        tiny[:, :, ends[1] : ends[2]]
        .reshape(mp_n, dp_n, 2, channel_part)
        .transpose(2, 0, 1, 3)
        .reshape(2, mp_n * dp_n * channel_part)
    )
    bn_gain, bn_shift = bn_both[0:1], bn_both[1:2]
    gains = (
        tiny[0, :, ends[2] : ends[3]].reshape(dp_n, 5, shard_rows).transpose(1, 0, 2).reshape(5, features)
    )
    gain = [gains[i : i + 1] for i in range(5)]
    line = jnp.concatenate(
        [
            jnp.zeros((mp_n, heads, 1), F32),
            jnp.flip(bias_table[:, :, 1:], axis=2),
            jnp.zeros((mp_n, heads, SUB), F32),
        ],
        axis=2,
    )

    middle_shard = jnp.concatenate(
        [
            attention_in[0],
            attention_in[1],
            attention_in[2],
            attention_out.T,
            pointwise_in[0],
            pointwise_in[1],
            pointwise_out.T,
        ],
        axis=1,
    )
    head_width = attention_out.shape[0]
    channels = mp_n * head_width
    middle = gather_groups(middle_shard, order_b)
    middle = [
        side[g].reshape(features, middle_shard.shape[1])
        for side in middle
        for g in range(side.shape[0])
    ]

    def columns(index):
        return jnp.concatenate(
            [
                middle[deltas.index(j)][:, index * head_width : (index + 1) * head_width]
                for j in range(mp_n)
            ],
            axis=1,
        )

    w_qkv = jnp.stack([columns(0), columns(1), columns(2)])
    w_out_t = columns(3)
    w_pw = jnp.stack([columns(4), columns(5)])
    w_pw_out_t = columns(6)
    late = gather_groups(jnp.concatenate([late_up, late_down.T], axis=1), order_a)
    late = [side.reshape(side.shape[0], features, 2 * part) for side in late]
    late_u = tuple(side[:, :, :part] for side in late)
    late_d = tuple(side[:, :, part:] for side in late)

    half_of_slot = jnp.stack([batch, 1 - batch]).astype(jnp.int32)
    sub_n = block // SUB
    qpos = (
        half_of_slot[:, None] * held_rows
        + place * block
        + SUB * jnp.arange(sub_n, dtype=jnp.int32)[None, :]
    ).reshape(-1)
    kpos = jnp.stack(
        [half_of_slot[r] * held_rows + (place ^ delta) * block for delta in deltas for r in (0, 1)]
    )
    after_first = ffn_forward(start, gain[0], early_u, early_d)
    second_n, second_inv = normed_of(after_first)
    second_act = (second_n * gain[1]).astype(BF16)
    projected = jnp.einsum("td,idk->itk", second_act, w_qkv, preferred_element_type=F32).astype(BF16)
    query = projected[0]
    pairs = [projected[1:]]
    for bit in range(bits_of("mp") - 1, -1, -1):
        pairs = pairs + [flip_pair(pair, "mp", bit) for pair in pairs]
    narrow = head_width < SUB
    shifts = [0] * len(deltas) if narrow else deltas
    if narrow:
        pairs = [swap_groups(pair, mp_n, delta) for pair, delta in zip(pairs, deltas)]
        line = line.reshape(channels // SUB, -1, line.shape[2])
    context, lse, context_wide = attend_forward(query, pairs, shifts, line, qpos, kpos)
    after_second = after_first + mm_nt(context, w_out_t)
    third_n, third_inv = normed_of(after_second)
    third_act = (third_n * gain[2]).astype(BF16)
    glu_pre = jnp.einsum("td,idc->itc", third_act, w_pw, preferred_element_type=F32)
    gate_sig = jax.nn.sigmoid(glu_pre[1])
    glu = (glu_pre[0] * gate_sig).astype(BF16).reshape(2, block, channels)
    edge = margin + 1
    before, after = edge_rows(glu[:, :edge], glu[:, block - edge :], half_of_slot)
    extended = jnp.concatenate([before[:, 1:], glu, after[:, :margin]], axis=1).astype(F32)
    conv = jnp.zeros((2, block, channels), F32)
    for tap in range(kernel):
        conv = conv + taps[:, tap] * extended[:, tap : tap + block]
    conv = conv.reshape(rows, channels)
    sums = channel_total(
        jnp.stack([jnp.sum(conv, axis=0), jnp.sum(conv * conv, axis=0)])
    )
    bmean = sums[0:1] / batch_rows
    bvar = sums[1:2] / batch_rows - bmean * bmean
    binv = lax.rsqrt(bvar + EPS)
    white = (conv - bmean) * binv
    bn_pre = bn_gain * white + bn_shift
    conv_act = jax.nn.silu(bn_pre).astype(BF16)
    after_third = after_second + mm_nt(conv_act, w_pw_out_t)
    after_fourth = ffn_forward(after_third, gain[3], late_u, late_d)
    fifth_n, fifth_inv = normed_of(after_fourth)
    final_rows = (fifth_n * gain[4]).astype(BF16)

    upstream = exchanged(out_cotangent)
    d_fourth, gain_four = norm_back(fifth_n, fifth_inv, gain[4], upstream)
    d_third, glu_a, glu_b, gld_a, gld_b, gain_three = ffn_backward(
        after_third, d_fourth, gain[3], late_u, late_d
    )

    def by_dp(value):
        return value.reshape(value.shape[0], dp_n, shard_rows, value.shape[2])

    own_late = scatter_groups(
        by_dp(jnp.concatenate([glu_a, gld_a], axis=2)),
        by_dp(jnp.concatenate([glu_b, gld_b], axis=2)),
        order_a,
    )
    conv_err = d_third.astype(BF16)
    grad_pw_out_t = mm(conv_err.T, conv_act)
    d_pre = mm(conv_err, w_pw_out_t) * swish_grad(bn_pre)
    local_sums = jnp.stack([jnp.sum(d_pre, axis=0), jnp.sum(d_pre * white, axis=0)])
    sums = channel_total(local_sums)
    d_conv = (
        binv * bn_gain * (d_pre - sums[0:1] / batch_rows - white * sums[1:2] / batch_rows)
    ).reshape(2, block, channels)
    before, after = edge_rows(d_conv[:, :edge], d_conv[:, block - edge :], half_of_slot)
    d_extended = jnp.concatenate([before[:, 1:], d_conv, after[:, :margin]], axis=1)
    d_glu = jnp.zeros((2, block, channels), F32)
    tap_grads = []
    for tap in range(kernel):
        d_glu = d_glu + taps[:, tap] * d_extended[:, kernel - 1 - tap : kernel - 1 - tap + block]
        tap_grads.append(jnp.sum(extended[:, tap : tap + block] * d_conv, axis=(0, 1)))
    grad_taps = jnp.stack(tap_grads, axis=1)
    d_glu = d_glu.reshape(rows, channels)
    d_lin = (d_glu * gate_sig).astype(BF16)
    d_gate = (d_glu * glu_pre[0] * gate_sig * (1.0 - gate_sig)).astype(BF16)
    d_both = jnp.stack([d_lin, d_gate])
    grad_pw = jnp.einsum("td,itc->idc", third_act, d_both, preferred_element_type=F32)
    back, gain_two = norm_back(
        third_n,
        third_inv,
        gain[2],
        jnp.einsum("itc,idc->td", d_both, w_pw, preferred_element_type=F32),
    )
    d_second = d_third + back
    att_err = d_second.astype(BF16)
    grad_out_t = mm(att_err.T, context)
    d_context = mm(att_err, w_out_t).astype(BF16)

    def group_pack(parts):
        parts = [value.astype(BF16) for value in parts]

        def of(delta):
            return jnp.concatenate(
                [value[:, delta * head_width : (delta + 1) * head_width] for value in parts], axis=1
            )

        half = len(kept)
        return tuple(
            by_dp(jnp.stack([of(delta) for delta in side]))
            for side in (deltas[:half], deltas[half:])
        )

    own_middle = scatter_groups(
        *group_pack([grad_out_t, grad_pw[0], grad_pw[1], grad_pw_out_t]), order_b
    )
    grads = attend_backward(query, d_context, lse, context_wide, pairs, shifts, line, qpos, kpos)
    d_query, line_grad = grads[0], grads[-1].reshape(mp_n, heads, 8, line.shape[2])
    d_pairs = dict(zip(deltas, grads[1:-1]))
    if narrow:
        d_pairs = {delta: swap_groups(value, mp_n, delta) for delta, value in d_pairs.items()}
    for bit in range(bits_of("mp")):
        for delta in [d for d in d_pairs if d >> bit & 1]:
            other = flip_pair(d_pairs.pop(delta), "mp", bit)
            home = delta ^ 1 << bit
            d_pairs[home] = (d_pairs[home].astype(F32) + other.astype(F32)).astype(BF16)
    stacked = jnp.concatenate([d_query[None], d_pairs[0]], axis=0)
    grad_qkv = jnp.einsum("td,itk->idk", second_act, stacked, preferred_element_type=F32)
    back, gain_one = norm_back(
        second_n,
        second_inv,
        gain[1],
        jnp.einsum("itk,idk->td", stacked, w_qkv, preferred_element_type=F32),
    )
    own_qkv = scatter_groups(*group_pack([grad_qkv[0], grad_qkv[1], grad_qkv[2]]), order_b)
    d_first = d_second + back
    d_start, geu_a, geu_b, ged_a, ged_b, gain_zero = ffn_backward(
        start, d_first, gain[0], early_u, early_d
    )

    width = table_n + SUB
    lines = jnp.pad(line_grad, ((0, 0), (0, 0), (0, 0), (0, 8)))
    line_total = sum(lines[:, :, row, row : row + width] for row in range(8))
    grad_table = jnp.concatenate(
        [jnp.zeros((mp_n, heads, 1), F32), jnp.flip(line_total[:, :, 1:table_n], axis=2)], axis=2
    )
    grad_gains = jnp.concatenate([gain_zero, gain_one, gain_two, gain_three, gain_four], axis=0)
    tiny = jnp.concatenate(
        [
            grad_table.reshape(mp_n, heads, dp_n, table_part)
            .transpose(0, 2, 1, 3)
            .reshape(mp_n, dp_n, heads * table_part),
            grad_taps.reshape(mp_n, dp_n, channel_part * kernel),
            local_sums[::-1]
            .reshape(2, mp_n, dp_n, channel_part)
            .transpose(1, 2, 0, 3)
            .reshape(mp_n, dp_n, 2 * channel_part),
            jnp.broadcast_to(
                grad_gains.reshape(5, dp_n, shard_rows)
                .transpose(1, 0, 2)
                .reshape(1, dp_n, 5 * shard_rows),
                (mp_n, dp_n, 5 * shard_rows),
            ),
            jnp.zeros((mp_n, dp_n, small_rows * part - small_n), F32),
        ],
        axis=2,
    ).astype(BF16)
    tiny = jnp.stack([tiny[delta] for delta in deltas]).reshape(mp_n, dp_n, small_rows, part)
    half = len(kept)
    own_early_u = scatter_groups(
        jnp.concatenate([by_dp(geu_a), tiny[:half]], axis=2),
        jnp.concatenate([by_dp(geu_b), tiny[half:]], axis=2),
        order_a,
    )
    own_early_d = scatter_groups(by_dp(ged_a), by_dp(ged_b), order_b)
    tiny = own_early_u[shard_rows:].reshape(-1)

    def returned(value):
        own, away = value[:block], value[block:]
        other = flip_pair(away, "dp", 0)
        first = batch == 0
        return jnp.stack([jnp.where(first, own, other), jnp.where(first, other, own)])

    def middle_part(value, index):
        return value[:, index * head_width : (index + 1) * head_width]

    return (
        returned(final_rows),
        returned(d_start),
        own_early_u[:shard_rows],
        own_early_d.T,
        jnp.stack([middle_part(own_qkv, i) for i in range(3)]),
        middle_part(own_middle, 0).T,
        tiny[: ends[0]].reshape(heads, table_part),
        jnp.stack([middle_part(own_middle, 1), middle_part(own_middle, 2)]),
        tiny[ends[0] : ends[1]].reshape(channel_part, kernel),
        tiny[ends[1] : ends[2]].reshape(2, channel_part),
        middle_part(own_middle, 3).T,
        own_late[:, :part],
        own_late[:, part:].T,
        tiny[ends[2] : ends[3]].reshape(5, shard_rows),
    )


def solution(mesh):
    placed = (
        P(None, "dp", None),
        P(None, "dp", None),
        P("dp", "mp"),
        P("mp", "dp"),
        P(None, "dp", "mp"),
        P("mp", "dp"),
        P("mp", "dp"),
        P(None, "dp", "mp"),
        P(("mp", "dp"), None),
        P(None, ("mp", "dp")),
        P("mp", "dp"),
        P("dp", "mp"),
        P("mp", "dp"),
        P(None, "dp"),
    )
    returned = (P(None, ("dp", "mp"), None), P(None, ("dp", "mp"), None)) + placed[2:]
    return jax.shard_map(body, mesh=mesh, in_specs=placed, out_specs=returned, check_vma=False)
```

```python
import functools

import jax
import jax.numpy as jnp
from jax import lax
from jax.experimental import pallas as pl
from jax.experimental.pallas import tpu as pltpu
from jax.sharding import PartitionSpec as P

EPS = 1e-05
BF16 = jnp.bfloat16
F32 = jnp.float32
SUB = 128
NT = (((1,), (1,)), ((), ()))


def flip_pair(value, axis, bit):
    return lax.ppermute(value, axis, [(i, i ^ 1 << bit) for i in range(lax.axis_size(axis))])


def bits_of(axis):
    return (lax.axis_size(axis) - 1).bit_length()


def own_bit(axis, bit):
    return lax.shift_right_logical(lax.axis_index(axis), bit) & 1


def full_order():
    dp_bits, mp_bits = bits_of("dp"), bits_of("mp")
    dp_high = [("dp", bit) for bit in range(dp_bits - 1, 0, -1)]
    mp_high = [("mp", bit) for bit in range(mp_bits - 1, 0, -1)]
    first = dp_high + [("dp", 0)] + mp_high + [("mp", 0)]
    second = dp_high + mp_high + [("dp", 0)] + [("mp", 0)]
    return (first, second)


def tied(value, other):
    return lax.optimization_barrier((value, other))[0]


def gather_groups(shard, order):
    held = {0: shard}
    for axis, bit in order:
        for delta in list(held):
            own = held[delta]
            other = flip_pair(own, axis, bit)
            if axis == "mp":
                held[delta ^ 1 << bit] = other
            else:
                first = own_bit(axis, bit) == 0
                held[delta] = jnp.concatenate(
                    [jnp.where(first, own, other), jnp.where(first, other, own)], axis=0
                )
    return held


def scatter_groups(parts, order):
    parts = dict(parts)
    total = None
    for axis, bit in reversed(order):
        if axis == "mp":
            for delta in [d for d in parts if d >> bit & 1]:
                other = flip_pair(parts.pop(delta), axis, bit)
                home = delta ^ 1 << bit
                parts[home] = (parts[home].astype(F32) + other.astype(F32)).astype(BF16)
        else:
            mine = own_bit(axis, bit)
            for delta in parts:
                half = parts[delta].shape[0] // 2
                send = lax.dynamic_slice_in_dim(parts[delta], (1 - mine) * half, half, 0)
                keep = lax.dynamic_slice_in_dim(parts[delta], mine * half, half, 0)
                total = keep.astype(F32) + flip_pair(send, axis, bit).astype(F32)
                parts[delta] = total.astype(BF16)
    return total


def reversed_blocks(count):
    bits = (count - 1).bit_length()
    return [int(format(i, "b").zfill(bits)[::-1], 2) if bits else 0 for i in range(count)]


def block_swap(features, count, dtype):
    row = lax.broadcasted_iota(jnp.int32, (features, features), 0)
    col = lax.broadcasted_iota(jnp.int32, (features, features), 1)
    size = features // count
    block, image = col // size, jnp.zeros_like(col)
    for bit in range((count - 1).bit_length()):
        image = image * 2 + (block >> bit & 1)
    return (row == image * size + col % size).astype(dtype)


def lane_flip(dtype):
    row = lax.broadcasted_iota(jnp.int32, (SUB, SUB), 0)
    col = lax.broadcasted_iota(jnp.int32, (SUB, SUB), 1)
    return (row + col == SUB - 1).astype(dtype)


def regroup(parts, widths, count):
    if count == 1:
        return parts
    joined = []
    for start in range(0, len(parts), count):
        pieces, at = [], 0
        for width in widths:
            pieces += [part[:, at : at + width] for part in parts[start : start + count]]
            at += width
        joined.append(jnp.concatenate(pieces, axis=1))
    return joined


def ungroup(parts, widths, count):
    if count == 1:
        return parts
    split = []
    for part in parts:
        for i in range(count):
            pieces, at = [], 0
            for width in widths:
                pieces.append(part[:, at + i * width : at + (i + 1) * width])
                at += width * count
            split.append(jnp.concatenate(pieces, axis=1))
    return split


def swap_groups(value, groups, delta):
    width = value.shape[-1] // groups
    parts = [value[..., (g ^ delta) * width : ((g ^ delta) + 1) * width] for g in range(groups)]
    return jnp.concatenate(parts, axis=-1)


def absolute_groups(value, groups):
    for bit in range((groups - 1).bit_length()):
        value = jnp.where(own_bit("mp", bit) == 0, value, swap_groups(value, groups, 1 << bit))
    return value


def channel_total(sums):
    groups = lax.axis_size("mp")
    for bit in range(bits_of("mp")):
        sums = sums + swap_groups(flip_pair(sums, "mp", bit), groups, 1 << bit)
    for bit in range(1, bits_of("dp")):
        sums = sums + flip_pair(sums, "dp", bit)
    return sums


def edge_rows(first_rows, last_rows, half_of_slot):
    groups = lax.axis_size("mp")
    place = lax.axis_index("mp")
    up = [(i, (i + 1) % groups) for i in range(groups)]
    down = [(i, (i - 1) % groups) for i in range(groups)]
    before = lax.ppermute(absolute_groups(last_rows, groups), "mp", up)
    after = lax.ppermute(absolute_groups(first_rows, groups), "mp", down)
    before = absolute_groups(before, groups)
    after = absolute_groups(after, groups)
    second = half_of_slot[:, None, None] == 1
    nothing = jnp.zeros_like(before)
    before = jnp.where(place == 0, jnp.where(second, before[::-1], nothing), before)
    after = jnp.where(place == groups - 1, jnp.where(second, nothing, after[::-1]), after)
    return (before, after)


def swish_grad(value):
    logistic = jax.nn.sigmoid(value)
    return logistic * (1.0 + value * (1.0 - logistic))


def normed_of(value):
    centred = value - jnp.mean(value, axis=-1, keepdims=True)
    inverse = lax.rsqrt(jnp.mean(centred * centred, axis=-1, keepdims=True) + EPS)
    return (centred * inverse, inverse)


def norm_back(normed, inverse, gain, upstream):
    scaled = upstream * gain
    inner = (
        scaled
        - jnp.mean(scaled, axis=-1, keepdims=True)
        - normed * jnp.mean(scaled * normed, axis=-1, keepdims=True)
    )
    return (inverse * inner, jnp.sum(upstream * normed, axis=0, keepdims=True))


def mm(left, right):
    return jnp.dot(left, right, preferred_element_type=F32)


def mm_nt(left, right):
    return lax.dot_general(left, right, NT, preferred_element_type=F32)


def call_kernel(kernel, outs, name, *inputs):
    return pl.pallas_call(
        kernel, out_shape=[jax.ShapeDtypeStruct(shape, dtype) for shape, dtype in outs], name=name
    )(*inputs)


def column_join(refs, index):
    return jnp.concatenate([ref[:, index * SUB : (index + 1) * SUB] for ref in refs], axis=1)


def ffn_forward_kernel(groups, v_ref, gain_ref, *refs):
    ups, downs, out_ref = refs[:groups], refs[groups : 2 * groups], refs[-1]
    value = v_ref[...]
    normed, _ = normed_of(value)
    active = (normed * gain_ref[...]).astype(BF16)
    total = jnp.zeros_like(value)
    for up_ref, down_ref in zip(ups, downs):
        pre = mm(active, up_ref[...])
        hidden = (pre * jax.nn.sigmoid(pre)).astype(BF16)
        total += mm_nt(hidden, down_ref[...])
    out_ref[...] = value + 0.5 * total


def ffn_backward_kernel(groups, v_ref, d_ref, gain_ref, *refs):
    ups, downs = refs[:groups], refs[groups : 2 * groups]
    out_ref, gg_ref = refs[2 * groups : 2 * groups + 2]
    gus, gds = refs[2 * groups + 2 : 3 * groups + 2], refs[3 * groups + 2 :]
    normed, inverse = normed_of(v_ref[...])
    upstream = d_ref[...]
    active = (normed * gain_ref[...]).astype(BF16)
    error = (0.5 * upstream).astype(BF16)
    active_t = active.T
    error_t = error.T
    total = jnp.zeros_like(upstream)
    for up_ref, down_ref, gu_ref, gd_ref in zip(ups, downs, gus, gds):
        pre = mm(active, up_ref[...])
        logistic = jax.nn.sigmoid(pre)
        hidden = (pre * logistic).astype(BF16)
        gd_ref[...] = mm(error_t, hidden).astype(BF16)
        d_hidden = mm(error, down_ref[...])
        d_pre = (d_hidden * (logistic * (1.0 + pre * (1.0 - logistic)))).astype(BF16)
        gu_ref[...] = mm(active_t, d_pre).astype(BF16)
        total += mm_nt(d_pre, up_ref[...])
    back, grad_gain = norm_back(normed, inverse, gain_ref[...], total)
    out_ref[...] = upstream + back
    gg_ref[...] = grad_gain


def project_kernel(groups, v_ref, gain_ref, *refs):
    weights, q_ref = refs[:groups], refs[groups]
    pair_refs = refs[groups + 1 :]
    normed, _ = normed_of(v_ref[...])
    active = (normed * gain_ref[...]).astype(BF16)
    q_ref[...] = mm(active, column_join(weights, 0)).astype(BF16)
    width = q_ref.shape[1] // len(pair_refs)
    for i in (0, 1):
        projected = mm(active, column_join(weights, i + 1)).astype(BF16)
        for h, pair_ref in enumerate(pair_refs):
            pair_ref[i] = projected[:, h * width : (h + 1) * width]


def project_backward_kernel(groups, halves, v_ref, d_ref, gain_ref, *refs):
    weights, smalls = refs[:groups], refs[groups : 2 * groups]
    dqs = refs[2 * groups : 2 * groups + halves]
    pairs = refs[2 * groups + halves : 2 * groups + 2 * halves]
    out_ref, gg_ref = refs[2 * groups + 2 * halves : 2 * groups + 2 * halves + 2]
    grads = refs[2 * groups + 2 * halves + 2 :]
    normed, inverse = normed_of(v_ref[...])
    active_t = (normed * gain_ref[...]).astype(BF16).T
    total = jnp.zeros_like(d_ref[...])
    for i in range(3):
        parts = [ref[...] for ref in dqs] if i == 0 else [ref[i - 1] for ref in pairs]
        error = jnp.concatenate(parts, axis=1) if halves > 1 else parts[0]
        total += mm_nt(error, column_join(weights, i))
        grad = mm(active_t, error).astype(BF16)
        for g, grad_ref in enumerate(grads):
            grad_ref[:, i * SUB : (i + 1) * SUB] = grad[:, g * SUB : (g + 1) * SUB]
    for small_ref, grad_ref in zip(smalls, grads):
        grad_ref[:, 3 * SUB :] = small_ref[...]
    back, grad_gain = norm_back(normed, inverse, gain_ref[...], total)
    out_ref[...] = d_ref[...] + back
    gg_ref[...] = grad_gain


def middle_kernel(groups, halves, v_ref, gain_ref, *refs):
    weights, contexts = refs[:groups], refs[groups : groups + halves]
    out_ref, lin_ref, sig_ref, glu_ref = refs[groups + halves :]
    parts = [ref[...] for ref in contexts]
    context = jnp.concatenate(parts, axis=1) if halves > 1 else parts[0]
    value = v_ref[...] + mm_nt(context, column_join(weights, 0))
    out_ref[...] = value
    normed, _ = normed_of(value)
    active = (normed * gain_ref[...]).astype(BF16)
    lin = mm(active, column_join(weights, 1))
    gate = jax.nn.sigmoid(mm(active, column_join(weights, 2)))
    lin_ref[...] = lin
    sig_ref[...] = gate
    glu_ref[...] = (lin * gate).astype(BF16)


def middle_backward_kernel(groups, halves, dglu_ref, lin_ref, sig_ref, v_ref, d_ref, gain_ref, *refs):
    weights, contexts = refs[:groups], refs[groups : groups + halves]
    out_ref, gg_ref, dctx_ref = refs[groups + halves : groups + halves + 3]
    grads = refs[groups + halves + 3 :]
    d_glu, lin, gate = dglu_ref[...], lin_ref[...], sig_ref[...]
    d_lin = (d_glu * gate).astype(BF16)
    d_gate = (d_glu * lin * gate * (1.0 - gate)).astype(BF16)
    normed, inverse = normed_of(v_ref[...])
    active_t = (normed * gain_ref[...]).astype(BF16).T
    total = mm_nt(d_lin, column_join(weights, 1)) + mm_nt(d_gate, column_join(weights, 2))
    back, grad_gain = norm_back(normed, inverse, gain_ref[...], total)
    value = d_ref[...] + back
    out_ref[...] = value
    gg_ref[...] = grad_gain
    error = value.astype(BF16)
    dctx_ref[...] = mm(error, column_join(weights, 0)).astype(BF16)
    parts = [ref[...] for ref in contexts]
    context = jnp.concatenate(parts, axis=1) if halves > 1 else parts[0]
    for i, grad in enumerate((mm(error.T, context), mm(active_t, d_lin), mm(active_t, d_gate))):
        rounded = grad.astype(BF16)
        for g, grad_ref in enumerate(grads):
            grad_ref[:, i * SUB : (i + 1) * SUB] = rounded[:, g * SUB : (g + 1) * SUB]


def turn_kernel(groups, conv_ref, bn_ref, v_ref, up_ref, gains_ref, *refs):
    weights = refs[:groups]
    final_ref, out_ref, dpre_ref, gg_ref, sums_ref = refs[groups : groups + 5]
    grads, pres = refs[groups + 5 : -1], refs[-1]
    part = pres.shape[2]
    top, bottom = slice(4 * SUB, 4 * SUB + part), slice(4 * SUB + part, 4 * SUB + 2 * part)
    gain_three, gain_four = gains_ref[3:4], gains_ref[4:5]
    white = (conv_ref[...] - bn_ref[0:1]) * bn_ref[1:2]
    bn_pre = bn_ref[2:3] * white + bn_ref[3:4]
    activated = (bn_pre * jax.nn.sigmoid(bn_pre)).astype(BF16)
    outward = column_join(weights, 3)
    third = v_ref[...] + mm_nt(activated, outward)
    normed, inverse = normed_of(third)
    active = (normed * gain_three).astype(BF16)
    total = jnp.zeros_like(third)
    for g, weight in enumerate(weights):
        pre = mm(active, weight[:, top])
        pres[g] = pre
        total += mm_nt((pre * jax.nn.sigmoid(pre)).astype(BF16), weight[:, bottom])
    last_normed, last_inverse = normed_of(third + 0.5 * total)
    final_ref[...] = (last_normed * gain_four).astype(BF16)
    fourth, grad_four = norm_back(last_normed, last_inverse, gain_four, up_ref[...])
    error = (0.5 * fourth).astype(BF16)
    active_t = active.T
    error_t = error.T
    total = jnp.zeros_like(third)
    for g, (weight, grad_ref) in enumerate(zip(weights, grads)):
        pre = pres[g]
        logistic = jax.nn.sigmoid(pre)
        hidden = (pre * logistic).astype(BF16)
        grad_ref[:, SUB + part :] = mm(error_t, hidden).astype(BF16)
        d_hidden = mm(error, weight[:, bottom])
        d_pre = (d_hidden * (logistic * (1.0 + pre * (1.0 - logistic)))).astype(BF16)
        grad_ref[:, SUB : SUB + part] = mm(active_t, d_pre).astype(BF16)
        total += mm_nt(d_pre, weight[:, top])
    back, grad_three = norm_back(normed, inverse, gain_three, total)
    value = fourth + back
    out_ref[...] = value
    gg_ref[0:1] = grad_three
    gg_ref[1:2] = grad_four
    error = value.astype(BF16)
    grad = mm(error.T, activated).astype(BF16)
    for g, grad_ref in enumerate(grads):
        grad_ref[:, :SUB] = grad[:, g * SUB : (g + 1) * SUB]
    d_pre = mm(error, outward) * swish_grad(bn_pre)
    dpre_ref[...] = d_pre
    sums_ref[0:1] = jnp.sum(d_pre, axis=0, keepdims=True)
    sums_ref[1:2] = jnp.sum(d_pre * white, axis=0, keepdims=True)


def build_skew(line_ref, skew, heads, chunks):
    for h in range(heads):
        for c in range(chunks):
            window = jnp.concatenate(
                [line_ref[0, h, c + 1 : c + 2, :], line_ref[0, h, c : c + 1, :]], axis=1
            )
            window = jnp.broadcast_to(window, (SUB, 2 * SUB))
            rolled = pltpu.roll(window, 1, 1, stride=1, stride_axis=0)
            skew[h, SUB * c : SUB * (c + 1), :] = rolled[:, SUB:]


def stack_heads(rows, heads, factor):
    lane = lax.broadcasted_iota(jnp.int32, rows.shape, 1)
    size = rows.shape[1] // heads
    return jnp.concatenate(
        [
            rows * jnp.where((lane >= h * size) & (lane < (h + 1) * size), factor, 0.0).astype(BF16)
            for h in range(heads)
        ],
        axis=0,
    )


def diagonal_heads(value, heads):
    size, columns = value.shape[0] // heads, value.shape[1] // heads
    parts = [
        value[h * size : (h + 1) * size, h * columns : (h + 1) * columns] for h in range(heads)
    ]
    return jnp.concatenate(parts, axis=0)


def tile_bias(skew, columns, block, offset_of):
    parts = [
        skew[h, pl.ds(pl.multiple_of(offset_of(qb), SUB), block), :] for h, qb in columns
    ]
    return jnp.concatenate(parts, axis=1)


def column_tiles(heads, steps):
    columns = [(h, qb) for h in range(heads) for qb in range(steps)]
    return [columns[i : i + 2] for i in range(0, len(columns), 2)]


def attend_forward_kernel(pieces, heads, qpos, kpos, q_ref, line_ref, *refs):
    k_refs = refs[:pieces]
    v_refs = refs[pieces : 2 * pieces]
    ctx_ref, lse_ref, ctx32_ref, skew, query, scores, probs, v_t = refs[2 * pieces :]
    rows, width = q_ref.shape
    block = rows // 2
    chunks = skew.shape[1] // SUB
    middle = skew.shape[1] // 2
    tiles = column_tiles(heads, rows // SUB)
    span = 2 * SUB
    build_skew(line_ref, skew, heads, chunks)
    for p in range(pieces):
        v_t[:width, p * rows : (p + 1) * rows] = v_refs[p][0].T
    v_t[width:, :] = jnp.ones_like(v_t[width:, :])
    query[...] = stack_heads(q_ref[...], heads, (width // heads) ** (-0.5))
    tops = [jnp.full((8, span), -jnp.inf, F32) for _ in tiles]
    for c in range(2 * pieces):
        keys = k_refs[c // 2][0, (c % 2) * block : (c % 2 + 1) * block, :]
        for t, tile in enumerate(tiles):
            raw = mm_nt(keys, query[t * span : (t + 1) * span, :])
            raw = raw + tile_bias(skew, tile, block, lambda qb: kpos[c] - qpos[qb] + middle)
            scores[c * block : (c + 1) * block, t * span : (t + 1) * span] = raw
            tops[t] = jnp.maximum(tops[t], jnp.max(raw.reshape(block // 8, 8, span), axis=0))
    tops = [jnp.max(top, axis=0, keepdims=True) for top in tops]
    for c in range(2 * pieces):
        for t in range(len(tiles)):
            part = (slice(c * block, (c + 1) * block), slice(t * span, (t + 1) * span))
            probs[part] = jnp.exp(scores[part] - tops[t]).astype(BF16)
    out_t = mm(v_t[...], probs[...])
    total = out_t[width : width + 1, :]
    out_t = out_t[:width, :] / total
    out = diagonal_heads(out_t, heads).T
    ctx_ref[...] = out.astype(BF16)
    ctx32_ref[...] = out
    lse_ref[0] = jnp.concatenate(tops, axis=1) + jnp.log(total)


def attend_backward_kernel(pieces, heads, qpos, kpos, q_ref, d_ref, ctx_ref, lse_ref, line_ref, *refs):
    k_refs = refs[:pieces]
    v_refs = refs[pieces : 2 * pieces]
    dq_ref = refs[2 * pieces]
    dkv_refs = refs[2 * pieces + 1 : 3 * pieces + 1]
    line_grad, skew, skew_grad, query, error, probs, d_scores, k_t = refs[3 * pieces + 1 :]
    rows, width = q_ref.shape
    block = rows // 2
    chunks = skew.shape[1] // SUB
    middle = skew.shape[1] // 2
    scale = (width // heads) ** (-0.5)
    size = width // heads
    tiles = column_tiles(heads, rows // SUB)
    span = 2 * SUB
    build_skew(line_ref, skew, heads, chunks)
    skew_grad[...] = jnp.zeros_like(skew_grad)
    for p in range(pieces):
        k_t[:, p * rows : (p + 1) * rows] = k_refs[p][0].T
    query[...] = stack_heads(q_ref[...], heads, scale)
    error[...] = stack_heads(d_ref[...], heads, 1.0)
    weighed = (d_ref[...].astype(F32) * ctx_ref[...]).T
    dot_sum = jnp.concatenate(
        [jnp.sum(weighed[h * size : (h + 1) * size], axis=0, keepdims=True) for h in range(heads)],
        axis=1,
    )
    lse = lse_ref[0]
    for c in range(2 * pieces):
        part = slice((c % 2) * block, (c % 2 + 1) * block)
        here = slice(c * block, (c + 1) * block)
        keys = k_refs[c // 2][0, part, :]
        values = v_refs[c // 2][0, part, :]
        for t, tile in enumerate(tiles):
            cols = slice(t * span, (t + 1) * span)
            raw = mm_nt(keys, query[cols, :])
            bias = tile_bias(skew, tile, block, lambda qb: kpos[c] - qpos[qb] + middle)
            prob = jnp.exp(raw + bias - lse[:, cols])
            d_score = prob * (mm_nt(values, error[cols, :]) - dot_sum[:, cols])
            probs[c % 2, :, cols] = prob.astype(BF16)
            d_scores[here, cols] = d_score.astype(BF16)
            for i, (h, qb) in enumerate(tile):
                offset = pl.multiple_of(kpos[c] - qpos[qb] + middle, SUB)
                skew_grad[h, pl.ds(offset, block), :] += d_score[:, i * SUB : (i + 1) * SUB]
        dkv_refs[c // 2][0, part, :] = mm(d_scores[here, :], query[...]).astype(BF16)
        dkv_refs[c // 2][1, part, :] = mm(probs[c % 2], error[...]).astype(BF16)
    dq_t = mm(k_t[...], d_scores[...])
    dq_ref[...] = (diagonal_heads(dq_t, heads).T * scale).astype(BF16)
    line_grad[...] = jnp.zeros_like(line_grad)
    for h in range(heads):
        for c in range(chunks):
            block_grad = skew_grad[h, SUB * c : SUB * (c + 1), :]
            value = jnp.concatenate([jnp.zeros_like(block_grad), block_grad], axis=1)
            half = SUB // 2
            while half >= 1:
                value = value[:half] + pltpu.roll(value[half:], 2 * SUB - half, 1)
                half //= 2
            value = pltpu.roll(value, 2 * SUB - 1, 1)
            line_grad[0, h, c + 1 : c + 2, :] += value[:, :SUB]
            line_grad[0, h, c : c + 1, :] += value[:, SUB:]


def attention_specs(rows, first, pieces, shifts, line_shape):
    whole_q = pl.BlockSpec((rows, SUB), lambda j, *_: (0, j + first))
    own = pl.BlockSpec((rows, SUB), lambda j, *_: (0, j))
    line = pl.BlockSpec((1,) + line_shape[1:], lambda j, *_: (j + first, 0, 0, 0))
    keys, values = [], []
    for p in range(pieces):
        keys.append(pl.BlockSpec((1, rows, SUB), lambda j, *_, d=shifts[p]: (0, 0, j ^ d)))
        values.append(pl.BlockSpec((1, rows, SUB), lambda j, *_, d=shifts[p]: (1, 0, j ^ d)))
    return (whole_q, own, line, keys, values)


def attend_forward(query, pairs, shifts, line, first, qpos, kpos):
    rows = query.shape[0]
    heads = line.shape[1]
    groups = pairs[0].shape[2] // SUB
    pieces = len(pairs)
    table = (line.shape[2] - 1) * SUB
    whole_q, own, line_spec, keys, values = attention_specs(rows, first, pieces, shifts, line.shape)
    return pl.pallas_call(
        functools.partial(attend_forward_kernel, pieces, heads),
        out_shape=(
            jax.ShapeDtypeStruct((rows, groups * SUB), BF16),
            jax.ShapeDtypeStruct((groups, 1, heads * rows), F32),
            jax.ShapeDtypeStruct((rows, groups * SUB), F32),
        ),
        grid_spec=pltpu.PrefetchScalarGridSpec(
            num_scalar_prefetch=2,
            grid=(groups,),
            in_specs=[whole_q, line_spec] + keys + values,
            out_specs=(
                own,
                pl.BlockSpec((1, 1, heads * rows), lambda j, *_: (j, 0, 0)),
                own,
            ),
            scratch_shapes=[
                pltpu.VMEM((heads, table, SUB), F32),
                pltpu.VMEM((heads * rows, SUB), BF16),
                pltpu.VMEM((pieces * rows, heads * rows), F32),
                pltpu.VMEM((pieces * rows, heads * rows), BF16),
                pltpu.VMEM((SUB + 16, pieces * rows), BF16),
            ],
        ),
        name="attend_forward",
    )(qpos, kpos, query, line, *pairs, *pairs)


def attend_backward(query, d_context, lse, context, pairs, shifts, line, first, qpos, kpos):
    rows = query.shape[0]
    heads = line.shape[1]
    groups = pairs[0].shape[2] // SUB
    pieces = len(pairs)
    table = (line.shape[2] - 1) * SUB
    whole_q, own, line_spec, keys, values = attention_specs(rows, first, pieces, shifts, line.shape)
    lse_spec = pl.BlockSpec((1, 1, heads * rows), lambda j, *_: (j, 0, 0))
    pair_specs = [
        pl.BlockSpec((2, rows, SUB), lambda j, *_, d=shifts[p]: (0, 0, j ^ d))
        for p in range(pieces)
    ]
    return pl.pallas_call(
        functools.partial(attend_backward_kernel, pieces, heads),
        out_shape=(
            (jax.ShapeDtypeStruct((rows, groups * SUB), BF16),)
            + tuple(jax.ShapeDtypeStruct(pairs[0].shape, BF16) for _ in range(pieces))
            + (jax.ShapeDtypeStruct((groups,) + line.shape[1:], F32),)
        ),
        grid_spec=pltpu.PrefetchScalarGridSpec(
            num_scalar_prefetch=2,
            grid=(groups,),
            in_specs=[whole_q, whole_q, own, lse_spec, line_spec] + keys + values,
            out_specs=(
                (own,)
                + tuple(pair_specs)
                + (pl.BlockSpec((1,) + line.shape[1:], lambda j, *_: (j, 0, 0, 0)),)
            ),
            scratch_shapes=[
                pltpu.VMEM((heads, table, SUB), F32),
                pltpu.VMEM((heads, table, SUB), F32),
                pltpu.VMEM((heads * rows, SUB), BF16),
                pltpu.VMEM((heads * rows, SUB), BF16),
                pltpu.VMEM((2, rows // 2, heads * rows), BF16),
                pltpu.VMEM((pieces * rows, heads * rows), BF16),
                pltpu.VMEM((SUB, pieces * rows), BF16),
            ],
        ),
        name="attend_backward",
    )(qpos, kpos, query, d_context, context, lse, line, *pairs, *pairs)


def body(
    block_input,
    out_cotangent,
    early_up,
    early_down,
    attention_in,
    attention_out,
    relative_bias,
    pointwise_in,
    depthwise,
    batch_norm,
    pointwise_out,
    late_up,
    late_down,
    norm_gains,
):
    dp_n, mp_n = lax.axis_size("dp"), lax.axis_size("mp")
    held_rows, features = block_input.shape[1:]
    block = held_rows // mp_n
    rows = 2 * block
    batch_rows = held_rows * dp_n
    batch = lax.axis_index("dp") % 2
    place = lax.axis_index("mp")
    shard_rows, part = early_up.shape
    heads, table_part = relative_bias.shape
    channel_part, kernel = depthwise.shape
    head_width = attention_out.shape[0]
    channels = mp_n * head_width
    margin = (kernel - 1) // 2
    order_a, order_b = full_order()
    fold = max(1, SUB // head_width)
    groups = mp_n // fold
    blocks = reversed_blocks(dp_n)
    swap_blocks = block_swap(features, dp_n, BF16)

    def exchanged(value):
        mine = lax.dynamic_slice_in_dim(value, place * block, block, 1)
        own = lax.dynamic_index_in_dim(mine, batch, 0, keepdims=False)
        away = lax.dynamic_index_in_dim(mine, 1 - batch, 0, keepdims=False)
        return mm(jnp.concatenate([own, flip_pair(away, "dp", 0)], axis=0), swap_blocks)

    def listed(parts, widths):
        return regroup([parts[delta] for delta in range(mp_n)], widths, fold)

    def unlisted(parts, widths):
        return dict(enumerate(ungroup(list(parts), widths, fold)))

    bias_rows = heads * table_part // SUB
    tap_n = kernel + 2
    small = jnp.concatenate(
        [
            relative_bias.reshape(bias_rows, SUB),
            jnp.pad(
                jnp.concatenate([depthwise, batch_norm.T], axis=1),
                ((0, shard_rows - bias_rows - channel_part), (0, SUB - tap_n)),
            ),
        ],
        axis=0,
    )
    gain_held = norm_gains[None]
    for bit in range(bits_of("dp") - 1, -1, -1):
        other = flip_pair(gain_held, "dp", bit)
        first = own_bit("dp", bit) == 0
        gain_held = jnp.concatenate(
            [jnp.where(first, gain_held, other), jnp.where(first, other, gain_held)], axis=0
        )
    gains = gain_held.transpose(1, 0, 2).reshape(5, features).astype(F32)
    gain = [gains[i : i + 1] for i in range(5)]
    early_u = gather_groups(early_up, order_a)
    early_d = gather_groups(early_down.T, order_b)
    start = exchanged(block_input)
    pair_widths = [head_width] * 3
    att_held = gather_groups(
        jnp.concatenate([attention_in[0], attention_in[1], attention_in[2], small], axis=1), order_a
    )
    rest_widths = [head_width] * 4 + [part] * 2
    rest_shard = jnp.concatenate(
        [
            attention_out.T,
            pointwise_in[0],
            pointwise_in[1],
            pointwise_out.T,
            late_up,
            late_down.T,
        ],
        axis=1,
    )
    rest = listed(gather_groups(tied(rest_shard, early_u[0]), order_b), rest_widths)
    if fold == 1:
        att = [att_held[delta] for delta in range(mp_n)]
    else:
        att = listed({d: value[:, : 3 * head_width] for d, value in att_held.items()}, pair_widths)
    tiny = jnp.stack([att_held[delta][:, 3 * head_width :] for delta in range(mp_n)])
    tiny = tiny.reshape(mp_n, dp_n, shard_rows, SUB)[:, jnp.array(blocks)]
    line = (
        tiny[:, :, :bias_rows]
        .reshape(mp_n, dp_n, heads, table_part // SUB, SUB)
        .transpose(0, 2, 1, 3, 4)
        .reshape(mp_n, heads, dp_n * table_part // SUB, SUB)
    )
    line = jnp.einsum("ghcl,lk->ghck", line, lane_flip(BF16), preferred_element_type=F32)
    line = jnp.pad(line, ((0, 0), (0, 0), (1, 0), (0, 0)))
    line = line.reshape(groups, heads * fold, line.shape[2], SUB)
    taps = (
        tiny[:, :, bias_rows : bias_rows + channel_part, :tap_n].reshape(channels, tap_n).T.astype(F32)
    )

    half_of_slot = jnp.stack([batch, 1 - batch]).astype(jnp.int32)
    kept = [0]
    for bit in range(bits_of("mp") - 1, -1, -1):
        kept = kept + [delta ^ 1 << bit for delta in kept]
    qpos = (
        half_of_slot[:, None] * held_rows
        + place * block
        + SUB * jnp.arange(block // SUB, dtype=jnp.int32)[None, :]
    ).reshape(-1)
    kpos = jnp.stack(
        [half_of_slot[r] * held_rows + (place ^ delta) * block for delta in kept for r in (0, 1)]
    )
    wide = (rows, channels)
    halves = 2 if fold == 1 and mp_n >= 4 else 1
    local = groups // halves
    up_list = [early_u[delta] for delta in range(mp_n)]
    down_list = [early_d[delta] for delta in range(mp_n)]
    (after_first,) = call_kernel(
        functools.partial(ffn_forward_kernel, mp_n),
        [((rows, features), F32)],
        "ffn_forward",
        start,
        gain[0],
        *up_list,
        *down_list,
    )
    query, *pair_halves = call_kernel(
        functools.partial(project_kernel, groups),
        [(wide, BF16)] + [((2, rows, local * SUB), BF16)] * halves,
        "project",
        after_first,
        gain[1],
        *att,
    )
    top_bit = bits_of("mp") - 1
    held_pairs = []
    for h in range(halves):
        pieces = [pair_halves[h]]
        pieces.append(flip_pair(pair_halves[halves - 1 - h], "mp", top_bit))
        for bit in range(top_bit - 1, -1, -1):
            pieces = pieces + [flip_pair(piece, "mp", bit) for piece in pieces]
        if fold > 1:
            pieces = [swap_groups(piece, mp_n, delta) for piece, delta in zip(pieces, kept)]
        held_pairs.append(pieces)
    shifts = [delta & (local - 1) if fold == 1 else 0 for delta in kept]
    attended = [
        attend_forward(query, held_pairs[h], shifts, line, h * local, qpos, kpos)
        for h in range(halves)
    ]
    contexts = [item[0] for item in attended]
    after_second, lin, gate_sig, glu = call_kernel(
        functools.partial(middle_kernel, groups, halves),
        [((rows, features), F32), (wide, F32), (wide, F32), (wide, BF16)],
        "middle",
        after_first,
        gain[2],
        *rest,
        *contexts,
    )
    glu = glu.reshape(2, block, channels)
    edge = margin + 1
    before, after = edge_rows(glu[:, :edge], glu[:, block - edge :], half_of_slot)
    extended = jnp.concatenate([before[:, 1:], glu, after[:, :margin]], axis=1).astype(F32)
    conv = jnp.zeros((2, block, channels), F32)
    for tap in range(kernel):
        conv = conv + taps[tap] * extended[:, tap : tap + block]
    conv = conv.reshape(rows, channels)
    sums = channel_total(jnp.stack([jnp.sum(conv, axis=0), jnp.sum(conv * conv, axis=0)]))
    bmean = sums[0:1] / batch_rows
    binv = lax.rsqrt(sums[1:2] / batch_rows - bmean * bmean + EPS)
    bn_rows = jnp.concatenate([bmean, binv, taps[kernel:]], axis=0)

    wide_part = part * fold
    turn_widths = [head_width, part, part]
    final_rows, d_third, d_pre, gg_last, local_sums, *turn_grads = pl.pallas_call(
        functools.partial(turn_kernel, groups),
        out_shape=[
            jax.ShapeDtypeStruct((rows, features), BF16),
            jax.ShapeDtypeStruct((rows, features), F32),
            jax.ShapeDtypeStruct(wide, F32),
            jax.ShapeDtypeStruct((2, features), F32),
            jax.ShapeDtypeStruct((2, channels), F32),
        ]
        + [jax.ShapeDtypeStruct((features, SUB + 2 * wide_part), BF16)] * groups,
        scratch_shapes=[pltpu.VMEM((groups, rows, wide_part), F32)],
        name="turn",
    )(conv, bn_rows, after_second, exchanged(out_cotangent), gains, *rest)
    own_turn = scatter_groups(unlisted(turn_grads, turn_widths), order_a)

    sums = channel_total(local_sums)
    white = (conv - bmean) * binv
    d_conv = (
        binv * bn_rows[2:3] * (d_pre - sums[0:1] / batch_rows - white * sums[1:2] / batch_rows)
    ).reshape(2, block, channels)
    before, after = edge_rows(d_conv[:, :edge], d_conv[:, block - edge :], half_of_slot)
    d_extended = jnp.concatenate([before[:, 1:], d_conv, after[:, :margin]], axis=1)
    d_glu = jnp.zeros((2, block, channels), F32)
    tap_grads = []
    for tap in range(kernel):
        d_glu = d_glu + taps[tap] * d_extended[:, kernel - 1 - tap : kernel - 1 - tap + block]
        tap_grads.append(jnp.sum(extended[:, tap : tap + block] * d_conv, axis=(0, 1)))
    tap_grads = jnp.stack(tap_grads + [local_sums[1], local_sums[0]])
    d_second, gain_two, d_context, *middle_grads = call_kernel(
        functools.partial(middle_backward_kernel, groups, halves),
        [((rows, features), F32), (gain[2].shape, F32), (wide, BF16)]
        + [((features, 3 * SUB), BF16)] * groups,
        "middle_backward",
        d_glu.reshape(rows, channels),
        lin,
        gate_sig,
        after_second,
        d_third,
        gain[2],
        *rest,
        *contexts,
    )
    own_middle = scatter_groups(unlisted(middle_grads, pair_widths), order_b)
    d_queries, kept_pairs, sent_pairs, line_grads = [], [], [], []
    for h in range(halves):
        grads = attend_backward(
            query, d_context, attended[h][1], attended[h][2], held_pairs[h], shifts, line,
            h * local, qpos, kpos,
        )
        d_queries.append(grads[0])
        line_grads.append(grads[-1])
        pieces = dict(zip(kept, grads[1:-1]))
        if fold > 1:
            pieces = {delta: swap_groups(value, mp_n, delta) for delta, value in pieces.items()}
        for bit in range(top_bit):
            for delta in [d for d in pieces if d >> bit & 1]:
                other = flip_pair(pieces.pop(delta), "mp", bit)
                home = delta ^ 1 << bit
                pieces[home] = (pieces[home].astype(F32) + other.astype(F32)).astype(BF16)
        kept_pairs.append(pieces[0])
        sent_pairs.append(flip_pair(pieces[1 << top_bit], "mp", top_bit))
    d_pairs = [
        (kept_pairs[h].astype(F32) + sent_pairs[halves - 1 - h].astype(F32)).astype(BF16)
        for h in range(halves)
    ]
    line_grad = jnp.concatenate(line_grads, axis=0)[:, :, 1:].reshape(mp_n, heads, -1, SUB)
    line_grad = jnp.einsum(
        "ghcl,lk->ghck", line_grad, lane_flip(F32), precision=lax.Precision.HIGHEST
    )
    order = jnp.array(blocks)
    tiny = jnp.concatenate(
        [
            line_grad.reshape(mp_n, heads, dp_n, table_part // SUB, SUB)
            .transpose(0, 2, 1, 3, 4)
            .reshape(mp_n, dp_n, bias_rows, SUB)[:, order],
            jnp.pad(
                tap_grads.T.reshape(mp_n, dp_n, channel_part, tap_n)[:, order],
                (
                    (0, 0),
                    (0, 0),
                    (0, shard_rows - bias_rows - channel_part),
                    (0, SUB - tap_n),
                ),
            ),
        ],
        axis=2,
    ).astype(BF16)
    tiny = tiny.reshape(mp_n, features, SUB)
    smalls = [tiny[g] for g in range(groups)]
    d_first, gain_one, *att_grads = call_kernel(
        functools.partial(project_backward_kernel, groups, halves),
        [((rows, features), F32), (gain[1].shape, F32)] + [((features, 4 * SUB), BF16)] * groups,
        "project_backward",
        after_first,
        d_second,
        gain[1],
        *att,
        *smalls,
        *d_queries,
        *d_pairs,
    )
    if fold > 1:
        att_grads = ungroup([grad[:, : 3 * SUB] for grad in att_grads], pair_widths, fold)
        att_grads = [jnp.concatenate([g, t], axis=1) for g, t in zip(att_grads, tiny)]
    own_att = scatter_groups(dict(enumerate(att_grads)), order_b)
    weight = ((features, part), BF16)
    d_start, gain_zero, *early_grads = call_kernel(
        functools.partial(ffn_backward_kernel, mp_n),
        [((rows, features), F32), (gain[0].shape, F32)] + [weight] * (2 * mp_n),
        "ffn_backward",
        start,
        d_first,
        gain[0],
        *up_list,
        *down_list,
    )
    own_up = scatter_groups(dict(enumerate(early_grads[:mp_n])), order_a)
    own_down = scatter_groups(dict(enumerate(early_grads[mp_n:])), order_b)
    gg = jnp.concatenate([gain_zero, gain_one, gain_two, gg_last], axis=0)
    for bit in range(bits_of("mp")):
        gg = gg + flip_pair(gg, "mp", bit)
    gg = gg.reshape(5, dp_n, shard_rows).transpose(1, 0, 2)
    for bit in range(bits_of("dp")):
        half = gg.shape[0] // 2
        mine = own_bit("dp", bit)
        send = lax.dynamic_slice_in_dim(gg, (1 - mine) * half, half, 0)
        gg = lax.dynamic_slice_in_dim(gg, mine * half, half, 0) + flip_pair(send, "dp", bit)

    def returned(value):
        own, away = value[:block], value[block:]
        other = flip_pair(away, "dp", 0)
        first = batch == 0
        return jnp.stack([jnp.where(first, own, other), jnp.where(first, other, own)])

    def columns(value, index):
        return value[:, index * head_width : (index + 1) * head_width]

    tail = own_att[:, 3 * head_width :]
    per_channel = tail[bias_rows : bias_rows + channel_part]
    natural = jnp.dot(d_start, swap_blocks.astype(F32), precision=lax.Precision.HIGHEST)
    return (
        returned(mm(final_rows, swap_blocks).astype(BF16)),
        returned(natural),
        own_up,
        own_down.T,
        jnp.stack([columns(own_att, i) for i in range(3)]),
        columns(own_middle, 0).T,
        tail[:bias_rows].reshape(heads, table_part),
        jnp.stack([columns(own_middle, 1), columns(own_middle, 2)]),
        per_channel[:, :kernel],
        per_channel[:, kernel:tap_n].T,
        columns(own_turn, 0).T,
        own_turn[:, head_width : head_width + part],
        own_turn[:, head_width + part :].T,
        gg[0],
    )


def solution(mesh):
    placed = (
        P(None, "dp", None),
        P(None, "dp", None),
        P("dp", "mp"),
        P("mp", "dp"),
        P(None, "dp", "mp"),
        P("mp", "dp"),
        P("mp", "dp"),
        P(None, "dp", "mp"),
        P(("mp", "dp"), None),
        P(None, ("mp", "dp")),
        P("mp", "dp"),
        P("dp", "mp"),
        P("mp", "dp"),
        P(None, "dp"),
    )
    returned = (P(None, ("dp", "mp"), None), P(None, ("dp", "mp"), None)) + placed[2:]
    return jax.shard_map(body, mesh=mesh, in_specs=placed, out_specs=returned, check_vma=False)
```

```python
import functools

import jax
import jax.numpy as jnp
from jax import lax
from jax.experimental import pallas as pl
from jax.experimental.pallas import tpu as pltpu
from jax.sharding import PartitionSpec as P


EPS = 1e-05
BF16 = jnp.bfloat16
F32 = jnp.float32
SUB = 128
NT = (((1,), (1,)), ((), ()))


def flip_pair(value, axis, bit):
    return lax.ppermute(value, axis, [(i, i ^ 1 << bit) for i in range(lax.axis_size(axis))])


def bits_of(axis):
    return (lax.axis_size(axis) - 1).bit_length()


def own_bit(axis, bit):
    return lax.shift_right_logical(lax.axis_index(axis), bit) & 1


def full_order():
    dp_bits, mp_bits = bits_of("dp"), bits_of("mp")
    dp_high = [("dp", bit) for bit in range(dp_bits - 1, 0, -1)]
    mp_high = [("mp", bit) for bit in range(mp_bits - 1, 0, -1)]
    first = dp_high + [("dp", 0)] + mp_high + [("mp", 0)]
    second = dp_high + mp_high + [("dp", 0)] + [("mp", 0)]
    return (first, second)


def tied(value, other):
    return lax.optimization_barrier((value, other))[0]


def gather_groups(shard, order):
    held = {0: shard}
    for axis, bit in order:
        for delta in list(held):
            own = held[delta]
            other = flip_pair(own, axis, bit)
            if axis == "mp":
                held[delta ^ 1 << bit] = other
            else:
                held[delta] = jnp.concatenate([own, other], axis=0)
    return held


def scatter_groups(parts, order, marks=None):
    parts = dict(parts)
    total = None
    for axis, bit in reversed(order):
        if axis == "mp":
            for delta in [d for d in parts if d >> bit & 1]:
                other = flip_pair(parts.pop(delta), axis, bit)
                home = delta ^ 1 << bit
                parts[home] = (parts[home].astype(F32) + other.astype(F32)).astype(BF16)
        else:
            for delta in parts:
                half = parts[delta].shape[0] // 2
                keep, send = parts[delta][:half], parts[delta][half:]
                other = flip_pair(send, axis, bit)
                total = keep.astype(F32) + other.astype(F32)
                parts[delta] = total.astype(BF16)
        if marks is not None:
            marks.append(dict(parts))
    return total


def reversed_blocks(count):
    bits = (count - 1).bit_length()
    return [int(format(i, "b").zfill(bits)[::-1], 2) if bits else 0 for i in range(count)]


def block_choice(features, count, dtype):
    row = lax.broadcasted_iota(jnp.int32, (features, features), 0)
    col = lax.broadcasted_iota(jnp.int32, (features, features), 1)
    size = features // count
    block, image = col // size, jnp.zeros_like(col)
    for bit in range((count - 1).bit_length()):
        image = image * 2 + (block >> bit & 1)
    image = image ^ lax.axis_index("dp")
    return (row == image * size + col % size).astype(dtype)


def lane_flip(dtype):
    row = lax.broadcasted_iota(jnp.int32, (SUB, SUB), 0)
    col = lax.broadcasted_iota(jnp.int32, (SUB, SUB), 1)
    return (row + col == SUB - 1).astype(dtype)


def regroup(parts, widths, count):
    if count == 1:
        return parts
    joined = []
    for start in range(0, len(parts), count):
        pieces, at = [], 0
        for width in widths:
            pieces += [part[:, at : at + width] for part in parts[start : start + count]]
            at += width
        joined.append(jnp.concatenate(pieces, axis=1))
    return joined


def ungroup(parts, widths, count):
    if count == 1:
        return parts
    split = []
    for part in parts:
        for i in range(count):
            pieces, at = [], 0
            for width in widths:
                pieces.append(part[:, at + i * width : at + (i + 1) * width])
                at += width * count
            split.append(jnp.concatenate(pieces, axis=1))
    return split


def swap_groups(value, groups, delta):
    width = value.shape[-1] // groups
    parts = [value[..., (g ^ delta) * width : ((g ^ delta) + 1) * width] for g in range(groups)]
    return jnp.concatenate(parts, axis=-1)


def absolute_groups(value, groups):
    for bit in range((groups - 1).bit_length()):
        value = jnp.where(own_bit("mp", bit) == 0, value, swap_groups(value, groups, 1 << bit))
    return value


def channel_total(sums):
    groups = lax.axis_size("mp")
    for bit in range(bits_of("mp")):
        sums = sums + swap_groups(flip_pair(sums, "mp", bit), groups, 1 << bit)
    for bit in range(1, bits_of("dp")):
        sums = sums + flip_pair(sums, "dp", bit)
    return sums


def edge_rows(first_rows, last_rows, half_of_slot):
    groups = lax.axis_size("mp")
    place = lax.axis_index("mp")
    up = [(i, (i + 1) % groups) for i in range(groups)]
    down = [(i, (i - 1) % groups) for i in range(groups)]
    before = lax.ppermute(absolute_groups(last_rows, groups), "mp", up)
    after = lax.ppermute(absolute_groups(first_rows, groups), "mp", down)
    before = absolute_groups(before, groups)
    after = absolute_groups(after, groups)
    second = half_of_slot[:, None, None] == 1
    nothing = jnp.zeros_like(before)
    before = jnp.where(place == 0, jnp.where(second, before[::-1], nothing), before)
    after = jnp.where(place == groups - 1, jnp.where(second, nothing, after[::-1]), after)
    return (before, after)


def swish_grad(value):
    logistic = jax.nn.sigmoid(value)
    return logistic * (1.0 + value * (1.0 - logistic))


def normed_of(value):
    centred = value - jnp.mean(value, axis=-1, keepdims=True)
    inverse = lax.rsqrt(jnp.mean(centred * centred, axis=-1, keepdims=True) + EPS)
    return (centred * inverse, inverse)


def norm_back(normed, inverse, gain, upstream):
    scaled = upstream * gain
    inner = (
        scaled
        - jnp.mean(scaled, axis=-1, keepdims=True)
        - normed * jnp.mean(scaled * normed, axis=-1, keepdims=True)
    )
    return (inverse * inner, jnp.sum(upstream * normed, axis=0, keepdims=True))


def mm(left, right):
    return jnp.dot(left, right, preferred_element_type=F32)


def mm_nt(left, right):
    return lax.dot_general(left, right, NT, preferred_element_type=F32)


def call_kernel(kernel, outs, *inputs):
    return pl.pallas_call(
        kernel, out_shape=[jax.ShapeDtypeStruct(shape, dtype) for shape, dtype in outs]
    )(*inputs)


def column_join(refs, index):
    return jnp.concatenate([ref[:, index * SUB : (index + 1) * SUB] for ref in refs], axis=1)


def ffn_forward_kernel(groups, v_ref, gain_ref, *refs):
    ups, downs, out_ref = refs[:groups], refs[groups : 2 * groups], refs[-1]
    value = v_ref[...]
    normed, _ = normed_of(value)
    active = (normed * gain_ref[...]).astype(BF16)
    total = jnp.zeros_like(value)
    for up_ref, down_ref in zip(ups, downs):
        pre = mm(active, up_ref[...])
        hidden = (pre * jax.nn.sigmoid(pre)).astype(BF16)
        total += mm_nt(hidden, down_ref[...])
    out_ref[...] = value + 0.5 * total


def ffn_backward_kernel(groups, v_ref, d_ref, gain_ref, one_ref, two_ref, last_ref, *refs):
    ups, downs = refs[:groups], refs[groups : 2 * groups]
    out_ref = refs[2 * groups]
    gus, gds = refs[2 * groups + 1 : 3 * groups + 1], refs[3 * groups + 1 :]
    part = ups[0].shape[1]
    normed, inverse = normed_of(v_ref[...])
    upstream = d_ref[...]
    active = (normed * gain_ref[...]).astype(BF16)
    error = (0.5 * upstream).astype(BF16)
    active_t = active.T
    error_t = error.T
    total = jnp.zeros_like(upstream)
    for up_ref, down_ref, gu_ref, gd_ref in zip(ups, downs, gus, gds):
        pre = mm(active, up_ref[...])
        logistic = jax.nn.sigmoid(pre)
        hidden = (pre * logistic).astype(BF16)
        gd_ref[:, :part] = mm(error_t, hidden).astype(BF16)
        d_hidden = mm(error, down_ref[...])
        d_pre = (d_hidden * (logistic * (1.0 + pre * (1.0 - logistic)))).astype(BF16)
        gu_ref[...] = mm(active_t, d_pre).astype(BF16)
        total += mm_nt(d_pre, up_ref[...])
    back, grad_gain = norm_back(normed, inverse, gain_ref[...], total)
    out_ref[...] = upstream + back
    known = [grad_gain, one_ref[...], two_ref[...], last_ref[...]]
    count = sum(value.shape[0] for value in known)
    known.append(jnp.zeros((SUB - count, upstream.shape[1]), F32))
    columns = jnp.concatenate(known, axis=0).T.astype(BF16)
    for gd_ref in gds:
        gd_ref[:, part:] = columns


def project_kernel(groups, v_ref, gain_ref, *refs):
    weights, q_ref = refs[:groups], refs[groups]
    pair_refs = refs[groups + 1 :]
    normed, _ = normed_of(v_ref[...])
    active = (normed * gain_ref[...]).astype(BF16)
    q_ref[...] = mm(active, column_join(weights, 0)).astype(BF16)
    width = q_ref.shape[1] // len(pair_refs)
    for i in (0, 1):
        projected = mm(active, column_join(weights, i + 1)).astype(BF16)
        for h, pair_ref in enumerate(pair_refs):
            pair_ref[i] = projected[:, h * width : (h + 1) * width]


def project_backward_kernel(groups, halves, v_ref, d_ref, gain_ref, *refs):
    weights, smalls = refs[:groups], refs[groups : 2 * groups]
    dqs = refs[2 * groups : 2 * groups + halves]
    pairs = refs[2 * groups + halves : 2 * groups + 2 * halves]
    out_ref, gg_ref = refs[2 * groups + 2 * halves : 2 * groups + 2 * halves + 2]
    grads = refs[2 * groups + 2 * halves + 2 :]
    normed, inverse = normed_of(v_ref[...])
    active_t = (normed * gain_ref[...]).astype(BF16).T
    total = jnp.zeros_like(d_ref[...])
    for i in range(3):
        parts = [ref[...] for ref in dqs] if i == 0 else [ref[i - 1] for ref in pairs]
        error = jnp.concatenate(parts, axis=1) if halves > 1 else parts[0]
        total += mm_nt(error, column_join(weights, i))
        grad = mm(active_t, error).astype(BF16)
        for g, grad_ref in enumerate(grads):
            grad_ref[:, i * SUB : (i + 1) * SUB] = grad[:, g * SUB : (g + 1) * SUB]
    for small_ref, grad_ref in zip(smalls, grads):
        grad_ref[:, 3 * SUB :] = small_ref[...]
    back, grad_gain = norm_back(normed, inverse, gain_ref[...], total)
    out_ref[...] = d_ref[...] + back
    gg_ref[...] = grad_gain


def middle_kernel(groups, halves, v_ref, gain_ref, *refs):
    weights, contexts = refs[:groups], refs[groups : groups + halves]
    out_ref, lin_ref, sig_ref, glu_ref = refs[groups + halves :]
    parts = [ref[...] for ref in contexts]
    context = jnp.concatenate(parts, axis=1) if halves > 1 else parts[0]
    value = v_ref[...] + mm_nt(context, column_join(weights, 0))
    out_ref[...] = value
    normed, _ = normed_of(value)
    active = (normed * gain_ref[...]).astype(BF16)
    lin = mm(active, column_join(weights, 1))
    gate = jax.nn.sigmoid(mm(active, column_join(weights, 2)))
    lin_ref[...] = lin
    sig_ref[...] = gate
    glu_ref[...] = (lin * gate).astype(BF16)


def middle_backward_kernel(groups, halves, dglu_ref, lin_ref, sig_ref, v_ref, d_ref, gain_ref, *refs):
    weights, contexts = refs[:groups], refs[groups : groups + halves]
    out_ref, gg_ref, dctx_ref = refs[groups + halves : groups + halves + 3]
    grads = refs[groups + halves + 3 :]
    d_glu, lin, gate = dglu_ref[...], lin_ref[...], sig_ref[...]
    d_lin = (d_glu * gate).astype(BF16)
    d_gate = (d_glu * lin * gate * (1.0 - gate)).astype(BF16)
    normed, inverse = normed_of(v_ref[...])
    active_t = (normed * gain_ref[...]).astype(BF16).T
    total = mm_nt(d_lin, column_join(weights, 1)) + mm_nt(d_gate, column_join(weights, 2))
    back, grad_gain = norm_back(normed, inverse, gain_ref[...], total)
    value = d_ref[...] + back
    out_ref[...] = value
    gg_ref[...] = grad_gain
    error = value.astype(BF16)
    dctx_ref[...] = mm(error, column_join(weights, 0)).astype(BF16)
    parts = [ref[...] for ref in contexts]
    context = jnp.concatenate(parts, axis=1) if halves > 1 else parts[0]
    for i, grad in enumerate((mm(error.T, context), mm(active_t, d_lin), mm(active_t, d_gate))):
        rounded = grad.astype(BF16)
        for g, grad_ref in enumerate(grads):
            grad_ref[:, i * SUB : (i + 1) * SUB] = rounded[:, g * SUB : (g + 1) * SUB]


def turn_kernel(groups, batch_rows, conv_ref, stat_ref, bn_ref, v_ref, up_ref, gains_ref, *refs):
    weights = refs[:groups]
    final_ref, out_ref, dpre_ref, gg_ref, sums_ref = refs[groups : groups + 5]
    grads, pres = refs[groups + 5 : -1], refs[-1]
    part = pres.shape[2]
    top, bottom = slice(4 * SUB, 4 * SUB + part), slice(4 * SUB + part, 4 * SUB + 2 * part)
    gain_three, gain_four = gains_ref[3:4], gains_ref[4:5]
    mean = stat_ref[0:1] / batch_rows
    white = (conv_ref[...] - mean) * lax.rsqrt(stat_ref[1:2] / batch_rows - mean * mean + EPS)
    bn_pre = bn_ref[0:1] * white + bn_ref[1:2]
    activated = (bn_pre * jax.nn.sigmoid(bn_pre)).astype(BF16)
    outward = column_join(weights, 3)
    third = v_ref[...] + mm_nt(activated, outward)
    normed, inverse = normed_of(third)
    active = (normed * gain_three).astype(BF16)
    total = jnp.zeros_like(third)
    for g, weight in enumerate(weights):
        pre = mm(active, weight[:, top])
        pres[g] = pre
        total += mm_nt((pre * jax.nn.sigmoid(pre)).astype(BF16), weight[:, bottom])
    last_normed, last_inverse = normed_of(third + 0.5 * total)
    final_ref[...] = (last_normed * gain_four).astype(BF16)
    fourth, grad_four = norm_back(last_normed, last_inverse, gain_four, up_ref[...])
    error = (0.5 * fourth).astype(BF16)
    active_t = active.T
    error_t = error.T
    total = jnp.zeros_like(third)
    for g, (weight, grad_ref) in enumerate(zip(weights, grads)):
        pre = pres[g]
        logistic = jax.nn.sigmoid(pre)
        hidden = (pre * logistic).astype(BF16)
        grad_ref[:, SUB + part :] = mm(error_t, hidden).astype(BF16)
        d_hidden = mm(error, weight[:, bottom])
        d_pre = (d_hidden * (logistic * (1.0 + pre * (1.0 - logistic)))).astype(BF16)
        grad_ref[:, SUB : SUB + part] = mm(active_t, d_pre).astype(BF16)
        total += mm_nt(d_pre, weight[:, top])
    back, grad_three = norm_back(normed, inverse, gain_three, total)
    value = fourth + back
    out_ref[...] = value
    gg_ref[0:1] = grad_three
    gg_ref[1:2] = grad_four
    error = value.astype(BF16)
    grad = mm(error.T, activated).astype(BF16)
    for g, grad_ref in enumerate(grads):
        grad_ref[:, :SUB] = grad[:, g * SUB : (g + 1) * SUB]
    d_pre = mm(error, outward) * swish_grad(bn_pre)
    dpre_ref[...] = d_pre
    sums_ref[0:1] = jnp.sum(d_pre, axis=0, keepdims=True)
    sums_ref[1:2] = jnp.sum(d_pre * white, axis=0, keepdims=True)


def build_skew(line_ref, skew, heads, chunks):
    for h in range(heads):
        for c in range(chunks):
            window = jnp.concatenate(
                [line_ref[0, h, c + 1 : c + 2, :], line_ref[0, h, c : c + 1, :]], axis=1
            )
            window = jnp.broadcast_to(window, (SUB, 2 * SUB))
            rolled = pltpu.roll(window, 1, 1, stride=1, stride_axis=0)
            skew[h, SUB * c : SUB * (c + 1), :] = rolled[:, SUB:]


def stack_heads(rows, heads, factor):
    lane = lax.broadcasted_iota(jnp.int32, rows.shape, 1)
    size = rows.shape[1] // heads
    return jnp.concatenate(
        [
            rows * jnp.where((lane >= h * size) & (lane < (h + 1) * size), factor, 0.0).astype(BF16)
            for h in range(heads)
        ],
        axis=0,
    )


def diagonal_heads(value, heads):
    size, columns = value.shape[0] // heads, value.shape[1] // heads
    parts = [
        value[h * size : (h + 1) * size, h * columns : (h + 1) * columns] for h in range(heads)
    ]
    return jnp.concatenate(parts, axis=0)


def tile_bias(skew, columns, block, offset_of):
    parts = [
        skew[h, pl.ds(pl.multiple_of(offset_of(qb), SUB), block), :] for h, qb in columns
    ]
    return jnp.concatenate(parts, axis=1)


def column_tiles(heads, steps):
    columns = [(h, qb) for h in range(heads) for qb in range(steps)]
    return [columns[i : i + 2] for i in range(0, len(columns), 2)]


def attend_forward_kernel(pieces, heads, qpos, kpos, q_ref, line_ref, *refs):
    k_refs = refs[:pieces]
    v_refs = refs[pieces : 2 * pieces]
    ctx_ref, lse_ref, ctx32_ref, skew, query, scores, probs, v_t = refs[2 * pieces :]
    rows, width = q_ref.shape
    block = rows // 2
    chunks = skew.shape[1] // SUB
    middle = skew.shape[1] // 2
    tiles = column_tiles(heads, rows // SUB)
    span = 2 * SUB
    build_skew(line_ref, skew, heads, chunks)
    for p in range(pieces):
        v_t[:width, p * rows : (p + 1) * rows] = v_refs[p][0].T
    v_t[width:, :] = jnp.ones_like(v_t[width:, :])
    query[...] = stack_heads(q_ref[...], heads, (width // heads) ** (-0.5))
    tops = [jnp.full((8, span), -jnp.inf, F32) for _ in tiles]
    for c in range(2 * pieces):
        keys = k_refs[c // 2][0, (c % 2) * block : (c % 2 + 1) * block, :]
        for t, tile in enumerate(tiles):
            raw = mm_nt(keys, query[t * span : (t + 1) * span, :])
            raw = raw + tile_bias(skew, tile, block, lambda qb: kpos[c] - qpos[qb] + middle)
            scores[c * block : (c + 1) * block, t * span : (t + 1) * span] = raw
            tops[t] = jnp.maximum(tops[t], jnp.max(raw.reshape(block // 8, 8, span), axis=0))
    tops = [jnp.max(top, axis=0, keepdims=True) for top in tops]
    for c in range(2 * pieces):
        for t in range(len(tiles)):
            part = (slice(c * block, (c + 1) * block), slice(t * span, (t + 1) * span))
            probs[part] = jnp.exp(scores[part] - tops[t]).astype(BF16)
    out_t = mm(v_t[...], probs[...])
    total = out_t[width : width + 1, :]
    out_t = out_t[:width, :] / total
    out = diagonal_heads(out_t, heads).T
    ctx_ref[...] = out.astype(BF16)
    ctx32_ref[...] = out
    lse_ref[0] = jnp.concatenate(tops, axis=1) + jnp.log(total)


def attend_backward_kernel(pieces, heads, qpos, kpos, q_ref, d_ref, ctx_ref, lse_ref, line_ref, *refs):
    k_refs = refs[:pieces]
    v_refs = refs[pieces : 2 * pieces]
    dq_ref = refs[2 * pieces]
    dkv_refs = refs[2 * pieces + 1 : 3 * pieces + 1]
    line_grad, skew, skew_grad, query, error, probs, d_scores, k_t = refs[3 * pieces + 1 :]
    rows, width = q_ref.shape
    block = rows // 2
    chunks = skew.shape[1] // SUB
    middle = skew.shape[1] // 2
    scale = (width // heads) ** (-0.5)
    size = width // heads
    tiles = column_tiles(heads, rows // SUB)
    span = 2 * SUB
    build_skew(line_ref, skew, heads, chunks)
    skew_grad[...] = jnp.zeros_like(skew_grad)
    for p in range(pieces):
        k_t[:, p * rows : (p + 1) * rows] = k_refs[p][0].T
    query[...] = stack_heads(q_ref[...], heads, scale)
    error[...] = stack_heads(d_ref[...], heads, 1.0)
    weighed = (d_ref[...].astype(F32) * ctx_ref[...]).T
    dot_sum = jnp.concatenate(
        [jnp.sum(weighed[h * size : (h + 1) * size], axis=0, keepdims=True) for h in range(heads)],
        axis=1,
    )
    lse = lse_ref[0]
    for c in range(2 * pieces):
        part = slice((c % 2) * block, (c % 2 + 1) * block)
        here = slice(c * block, (c + 1) * block)
        keys = k_refs[c // 2][0, part, :]
        values = v_refs[c // 2][0, part, :]
        for t, tile in enumerate(tiles):
            cols = slice(t * span, (t + 1) * span)
            raw = mm_nt(keys, query[cols, :])
            bias = tile_bias(skew, tile, block, lambda qb: kpos[c] - qpos[qb] + middle)
            prob = jnp.exp(raw + bias - lse[:, cols])
            d_score = prob * (mm_nt(values, error[cols, :]) - dot_sum[:, cols])
            probs[c % 2, :, cols] = prob.astype(BF16)
            d_scores[here, cols] = d_score.astype(BF16)
            for i, (h, qb) in enumerate(tile):
                offset = pl.multiple_of(kpos[c] - qpos[qb] + middle, SUB)
                skew_grad[h, pl.ds(offset, block), :] += d_score[:, i * SUB : (i + 1) * SUB]
        dkv_refs[c // 2][0, part, :] = mm(d_scores[here, :], query[...]).astype(BF16)
        dkv_refs[c // 2][1, part, :] = mm(probs[c % 2], error[...]).astype(BF16)
    dq_t = mm(k_t[...], d_scores[...])
    dq_ref[...] = (diagonal_heads(dq_t, heads).T * scale).astype(BF16)
    line_grad[...] = jnp.zeros_like(line_grad)
    for h in range(heads):
        for c in range(chunks):
            block_grad = skew_grad[h, SUB * c : SUB * (c + 1), :]
            value = jnp.concatenate([jnp.zeros_like(block_grad), block_grad], axis=1)
            half = SUB // 2
            while half >= 1:
                value = value[:half] + pltpu.roll(value[half:], 2 * SUB - half, 1)
                half //= 2
            value = pltpu.roll(value, 2 * SUB - 1, 1)
            line_grad[0, h, c + 1 : c + 2, :] += value[:, :SUB]
            line_grad[0, h, c : c + 1, :] += value[:, SUB:]


def attention_specs(rows, first, pieces, shifts, line_shape):
    whole_q = pl.BlockSpec((rows, SUB), lambda j, *_: (0, j + first))
    own = pl.BlockSpec((rows, SUB), lambda j, *_: (0, j))
    line = pl.BlockSpec((1,) + line_shape[1:], lambda j, *_: (j + first, 0, 0, 0))
    keys, values = [], []
    for p in range(pieces):
        keys.append(pl.BlockSpec((1, rows, SUB), lambda j, *_, d=shifts[p]: (0, 0, j ^ d)))
        values.append(pl.BlockSpec((1, rows, SUB), lambda j, *_, d=shifts[p]: (1, 0, j ^ d)))
    return (whole_q, own, line, keys, values)


def attend_forward(query, pairs, shifts, line, first, qpos, kpos):
    rows = query.shape[0]
    heads = line.shape[1]
    groups = pairs[0].shape[2] // SUB
    pieces = len(pairs)
    table = (line.shape[2] - 1) * SUB
    whole_q, own, line_spec, keys, values = attention_specs(rows, first, pieces, shifts, line.shape)
    return pl.pallas_call(
        functools.partial(attend_forward_kernel, pieces, heads),
        out_shape=(
            jax.ShapeDtypeStruct((rows, groups * SUB), BF16),
            jax.ShapeDtypeStruct((groups, 1, heads * rows), F32),
            jax.ShapeDtypeStruct((rows, groups * SUB), F32),
        ),
        grid_spec=pltpu.PrefetchScalarGridSpec(
            num_scalar_prefetch=2,
            grid=(groups,),
            in_specs=[whole_q, line_spec] + keys + values,
            out_specs=(
                own,
                pl.BlockSpec((1, 1, heads * rows), lambda j, *_: (j, 0, 0)),
                own,
            ),
            scratch_shapes=[
                pltpu.VMEM((heads, table, SUB), F32),
                pltpu.VMEM((heads * rows, SUB), BF16),
                pltpu.VMEM((pieces * rows, heads * rows), F32),
                pltpu.VMEM((pieces * rows, heads * rows), BF16),
                pltpu.VMEM((SUB + 16, pieces * rows), BF16),
            ],
        ),
        name="attend_forward",
    )(qpos, kpos, query, line, *pairs, *pairs)


def attend_backward(query, d_context, lse, context, pairs, shifts, line, first, qpos, kpos):
    rows = query.shape[0]
    heads = line.shape[1]
    groups = pairs[0].shape[2] // SUB
    pieces = len(pairs)
    table = (line.shape[2] - 1) * SUB
    whole_q, own, line_spec, keys, values = attention_specs(rows, first, pieces, shifts, line.shape)
    lse_spec = pl.BlockSpec((1, 1, heads * rows), lambda j, *_: (j, 0, 0))
    pair_specs = [
        pl.BlockSpec((2, rows, SUB), lambda j, *_, d=shifts[p]: (0, 0, j ^ d))
        for p in range(pieces)
    ]
    return pl.pallas_call(
        functools.partial(attend_backward_kernel, pieces, heads),
        out_shape=(
            (jax.ShapeDtypeStruct((rows, groups * SUB), BF16),)
            + tuple(jax.ShapeDtypeStruct(pairs[0].shape, BF16) for _ in range(pieces))
            + (jax.ShapeDtypeStruct((groups,) + line.shape[1:], F32),)
        ),
        grid_spec=pltpu.PrefetchScalarGridSpec(
            num_scalar_prefetch=2,
            grid=(groups,),
            in_specs=[whole_q, whole_q, own, lse_spec, line_spec] + keys + values,
            out_specs=(
                (own,)
                + tuple(pair_specs)
                + (pl.BlockSpec((1,) + line.shape[1:], lambda j, *_: (j, 0, 0, 0)),)
            ),
            scratch_shapes=[
                pltpu.VMEM((heads, table, SUB), F32),
                pltpu.VMEM((heads, table, SUB), F32),
                pltpu.VMEM((heads * rows, SUB), BF16),
                pltpu.VMEM((heads * rows, SUB), BF16),
                pltpu.VMEM((2, rows // 2, heads * rows), BF16),
                pltpu.VMEM((pieces * rows, heads * rows), BF16),
                pltpu.VMEM((SUB, pieces * rows), BF16),
            ],
        ),
        name="attend_backward",
    )(qpos, kpos, query, d_context, context, lse, line, *pairs, *pairs)


def block_step(
    block_input,
    out_cotangent,
    early_up,
    early_down,
    attention_in,
    attention_out,
    relative_bias,
    pointwise_in,
    depthwise,
    batch_norm,
    pointwise_out,
    late_up,
    late_down,
    norm_gains,
):
    dp_n, mp_n = lax.axis_size("dp"), lax.axis_size("mp")
    held_rows, features = block_input.shape[1:]
    block = held_rows // mp_n
    rows = 2 * block
    batch_rows = held_rows * dp_n
    batch = lax.axis_index("dp") % 2
    place = lax.axis_index("mp")
    shard_rows, part = early_up.shape
    heads, table_part = relative_bias.shape
    channel_part, kernel = depthwise.shape
    head_width = attention_out.shape[0]
    channels = mp_n * head_width
    margin = (kernel - 1) // 2
    order_a, order_b = full_order()
    fold = max(1, SUB // head_width)
    groups = mp_n // fold
    blocks = jnp.array(reversed_blocks(dp_n), jnp.int32)
    to_natural = blocks[jnp.arange(dp_n, dtype=jnp.int32) ^ lax.axis_index("dp")]
    to_held = blocks ^ lax.axis_index("dp")
    choice = block_choice(features, dp_n, BF16)

    def exchanged(value):
        mine = lax.dynamic_slice_in_dim(value, place * block, block, 1)
        own = lax.dynamic_index_in_dim(mine, batch, 0, keepdims=False)
        away = lax.dynamic_index_in_dim(mine, 1 - batch, 0, keepdims=False)
        other = flip_pair(away, "dp", 0)
        return mm(jnp.concatenate([own, other], axis=0), choice)

    def listed(parts, widths):
        return regroup([parts[delta] for delta in range(mp_n)], widths, fold)

    def unlisted(parts, widths):
        return dict(enumerate(ungroup(list(parts), widths, fold)))

    bias_rows = heads * table_part // SUB
    tap_n = kernel + 2
    gain_row = bias_rows + channel_part
    small_rows = gain_row + norm_gains.shape[0]
    small = jnp.concatenate(
        [
            relative_bias.reshape(bias_rows, SUB),
            jnp.pad(jnp.concatenate([depthwise, batch_norm.T], axis=1), ((0, 0), (0, SUB - tap_n))),
            jnp.pad(norm_gains, ((0, shard_rows - small_rows), (0, SUB - shard_rows))),
        ],
        axis=0,
    )
    early_u = gather_groups(early_up, order_a)
    early_d = gather_groups(early_down.T, order_b)
    start = exchanged(block_input)
    pair_widths = [head_width] * 3
    att_shard = jnp.concatenate([attention_in[0], attention_in[1], attention_in[2], small], axis=1)
    att_held = gather_groups(att_shard, order_b)
    rest_widths = [head_width] * 4 + [part] * 2
    rest_shard = jnp.concatenate(
        [
            attention_out.T,
            pointwise_in[0],
            pointwise_in[1],
            pointwise_out.T,
            late_up,
            late_down.T,
        ],
        axis=1,
    )
    rest = listed(gather_groups(rest_shard, order_b), rest_widths)
    if fold == 1:
        att = [att_held[delta] for delta in range(mp_n)]
    else:
        att = listed({d: value[:, : 3 * head_width] for d, value in att_held.items()}, pair_widths)
    gains = (
        att_held[0]
        .reshape(dp_n, shard_rows, -1)[:, gain_row:small_rows, 3 * head_width : 3 * head_width + shard_rows]
        .transpose(1, 0, 2)
        .reshape(5, features)
        .astype(F32)
    )
    gain = [gains[i : i + 1] for i in range(5)]
    tiny = jnp.stack([att_held[delta][:, 3 * head_width :] for delta in range(mp_n)])
    tiny = tiny.reshape(mp_n, dp_n, shard_rows, SUB)[:, to_natural]
    line = (
        tiny[:, :, :bias_rows]
        .reshape(mp_n, dp_n, heads, table_part // SUB, SUB)
        .transpose(0, 2, 1, 3, 4)
        .reshape(mp_n, heads, dp_n * table_part // SUB, SUB)
    )
    line = jnp.einsum("ghcl,lk->ghck", line, lane_flip(BF16), preferred_element_type=F32)
    line = jnp.pad(line, ((0, 0), (0, 0), (1, 0), (0, 0)))
    line = line.reshape(groups, heads * fold, line.shape[2], SUB)
    taps = (
        tiny[:, :, bias_rows : bias_rows + channel_part, :tap_n].reshape(channels, tap_n).T.astype(F32)
    )

    half_of_slot = jnp.stack([batch, 1 - batch]).astype(jnp.int32)
    kept = [0]
    for bit in range(bits_of("mp") - 1, -1, -1):
        kept = kept + [delta ^ 1 << bit for delta in kept]
    qpos = (
        half_of_slot[:, None] * held_rows
        + place * block
        + SUB * jnp.arange(block // SUB, dtype=jnp.int32)[None, :]
    ).reshape(-1)
    kpos = jnp.stack(
        [half_of_slot[r] * held_rows + (place ^ delta) * block for delta in kept for r in (0, 1)]
    )
    wide = (rows, channels)
    halves = 2 if fold == 1 and mp_n >= 4 else 1
    local = groups // halves
    up_list = [early_u[delta] for delta in range(mp_n)]
    down_list = [early_d[delta] for delta in range(mp_n)]
    (after_first,) = call_kernel(
        functools.partial(ffn_forward_kernel, mp_n),
        [((rows, features), F32)],
        start,
        gain[0],
        *up_list,
        *down_list,
    )
    query, *pair_halves = call_kernel(
        functools.partial(project_kernel, groups),
        [(wide, BF16)] + [((2, rows, local * SUB), BF16)] * halves,
        after_first,
        gain[1],
        *att,
    )
    top_bit = bits_of("mp") - 1
    held_pairs = []
    for h in range(halves):
        pieces = [pair_halves[h]]
        away = pair_halves[halves - 1 - h]
        if h > 0:
            away = tied(away, held_pairs[h - 1][1])
        pieces.append(flip_pair(away, "mp", top_bit))
        for bit in range(top_bit - 1, -1, -1):
            pieces = pieces + [flip_pair(piece, "mp", bit) for piece in pieces]
        if fold > 1:
            pieces = [swap_groups(piece, mp_n, delta) for piece, delta in zip(pieces, kept)]
        held_pairs.append(pieces)
    shifts = [delta & (local - 1) if fold == 1 else 0 for delta in kept]
    attended = []
    for h in range(halves):
        attended.append(attend_forward(query, held_pairs[h], shifts, line, h * local, qpos, kpos))
    contexts = [item[0] for item in attended]
    after_second, lin, gate_sig, glu = call_kernel(
        functools.partial(middle_kernel, groups, halves),
        [((rows, features), F32), (wide, F32), (wide, F32), (wide, BF16)],
        after_first,
        gain[2],
        *rest,
        *contexts,
    )
    cotangent = exchanged(out_cotangent)
    glu = tied(glu, cotangent).reshape(2, block, channels)
    edge = margin + 1
    before, after = edge_rows(glu[:, :edge], glu[:, block - edge :], half_of_slot)
    extended = jnp.concatenate([before[:, 1:], glu, after[:, :margin]], axis=1).astype(F32)
    conv = jnp.zeros((2, block, channels), F32)
    for tap in range(kernel):
        conv = conv + taps[tap] * extended[:, tap : tap + block]
    conv = conv.reshape(rows, channels)
    sums = channel_total(jnp.stack([jnp.sum(conv, axis=0), jnp.sum(conv * conv, axis=0)]))
    bmean = sums[0:1] / batch_rows
    binv = lax.rsqrt(sums[1:2] / batch_rows - bmean * bmean + EPS)
    bn_rows = taps[kernel:]

    wide_part = part * fold
    turn_widths = [head_width, part, part]
    final_rows, d_third, d_pre, gg_last, local_sums, *turn_grads = pl.pallas_call(
        functools.partial(turn_kernel, groups, batch_rows),
        out_shape=[
            jax.ShapeDtypeStruct((rows, features), BF16),
            jax.ShapeDtypeStruct((rows, features), F32),
            jax.ShapeDtypeStruct(wide, F32),
            jax.ShapeDtypeStruct((2, features), F32),
            jax.ShapeDtypeStruct((2, channels), F32),
        ]
        + [jax.ShapeDtypeStruct((features, SUB + 2 * wide_part), BF16)] * groups,
        scratch_shapes=[pltpu.VMEM((groups, rows, wide_part), F32)],
        name="turn",
    )(conv, sums, bn_rows, after_second, cotangent, gains, *rest)
    turn_marks = []
    own_turn = scatter_groups(unlisted(turn_grads, turn_widths), order_a, turn_marks)

    sums = channel_total(local_sums)
    white = (conv - bmean) * binv
    d_conv = (
        binv * bn_rows[0:1] * (d_pre - sums[0:1] / batch_rows - white * sums[1:2] / batch_rows)
    ).reshape(2, block, channels)
    before, after = edge_rows(d_conv[:, :edge], d_conv[:, block - edge :], half_of_slot)
    d_extended = jnp.concatenate([before[:, 1:], d_conv, after[:, :margin]], axis=1)
    d_glu = jnp.zeros((2, block, channels), F32)
    tap_grads = []
    for tap in range(kernel):
        d_glu = d_glu + taps[tap] * d_extended[:, kernel - 1 - tap : kernel - 1 - tap + block]
        tap_grads.append(jnp.sum(extended[:, tap : tap + block] * d_conv, axis=(0, 1)))
    tap_grads = jnp.stack(tap_grads + [local_sums[1], local_sums[0]])
    d_second, gain_two, d_context, *middle_grads = call_kernel(
        functools.partial(middle_backward_kernel, groups, halves),
        [((rows, features), F32), (gain[2].shape, F32), (wide, BF16)]
        + [((features, 3 * SUB), BF16)] * groups,
        tied(d_glu.reshape(rows, channels), turn_marks[0][1 << top_bit]),
        lin,
        gate_sig,
        after_second,
        d_third,
        gain[2],
        *rest,
        *contexts,
    )
    own_middle = scatter_groups(unlisted(middle_grads, pair_widths), order_b)
    d_queries, kept_pairs, sent_pairs, line_grads = [], [], [], []
    for h in range(halves):
        grads = attend_backward(
            query, d_context, attended[h][1], attended[h][2], held_pairs[h], shifts, line,
            h * local, qpos, kpos,
        )
        d_queries.append(grads[0])
        line_grads.append(grads[-1])
        pieces = dict(zip(kept, grads[1:-1]))
        if fold > 1:
            pieces = {delta: swap_groups(value, mp_n, delta) for delta, value in pieces.items()}
        for bit in range(top_bit):
            for delta in [d for d in pieces if d >> bit & 1]:
                other = flip_pair(pieces.pop(delta), "mp", bit)
                home = delta ^ 1 << bit
                pieces[home] = (pieces[home].astype(F32) + other.astype(F32)).astype(BF16)
        kept_pairs.append(pieces[0])
        sent_pairs.append(flip_pair(pieces[1 << top_bit], "mp", top_bit))
    d_pairs = [
        (kept_pairs[h].astype(F32) + sent_pairs[halves - 1 - h].astype(F32)).astype(BF16)
        for h in range(halves)
    ]
    line_grad = jnp.concatenate(line_grads, axis=0)[:, :, 1:].reshape(mp_n, heads, -1, SUB)
    line_grad = jnp.einsum(
        "ghcl,lk->ghck", line_grad, lane_flip(F32), precision=lax.Precision.HIGHEST
    )
    tiny = jnp.concatenate(
        [
            line_grad.reshape(mp_n, heads, dp_n, table_part // SUB, SUB)
            .transpose(0, 2, 1, 3, 4)
            .reshape(mp_n, dp_n, bias_rows, SUB)[:, to_held],
            jnp.pad(
                tap_grads.T.reshape(mp_n, dp_n, channel_part, tap_n)[:, to_held],
                (
                    (0, 0),
                    (0, 0),
                    (0, shard_rows - bias_rows - channel_part),
                    (0, SUB - tap_n),
                ),
            ),
        ],
        axis=2,
    ).astype(BF16)
    tiny = tiny.reshape(mp_n, features, SUB)
    smalls = [tiny[g] for g in range(groups)]
    d_first, gain_one, *att_grads = call_kernel(
        functools.partial(project_backward_kernel, groups, halves),
        [((rows, features), F32), (gain[1].shape, F32)] + [((features, 4 * SUB), BF16)] * groups,
        after_first,
        d_second,
        gain[1],
        *att,
        *smalls,
        *d_queries,
        *d_pairs,
    )
    if fold > 1:
        att_grads = ungroup([grad[:, : 3 * SUB] for grad in att_grads], pair_widths, fold)
        att_grads = [jnp.concatenate([g, t], axis=1) for g, t in zip(att_grads, tiny)]
    own_att = scatter_groups(dict(enumerate(att_grads)), order_a)
    d_start, *early_grads = call_kernel(
        functools.partial(ffn_backward_kernel, mp_n),
        [((rows, features), F32)]
        + [((features, part), BF16)] * mp_n
        + [((features, part + SUB), BF16)] * mp_n,
        start,
        d_first,
        gain[0],
        gain_one,
        gain_two,
        gg_last,
        *up_list,
        *down_list,
    )
    up_marks = []
    own_up = scatter_groups(dict(enumerate(early_grads[:mp_n])), order_a, up_marks)
    own_down = scatter_groups(dict(enumerate(early_grads[mp_n:])), order_b)

    def returned(own, away):
        other = flip_pair(away, "dp", 0).astype(own.dtype)
        first = batch == 0
        return jnp.stack([jnp.where(first, own, other), jnp.where(first, other, own)])

    def columns(value, index):
        return value[:, index * head_width : (index + 1) * head_width]

    tail = own_att[:, 3 * head_width :]
    per_channel = tail[bias_rows : bias_rows + channel_part]
    natural = lax.dot_general(
        tied(d_start, up_marks[0][1 << top_bit]), choice.astype(F32), NT, precision=lax.Precision.HIGHEST
    )
    final_rows = mm_nt(final_rows, choice).astype(BF16)
    return (
        returned(final_rows[:block], final_rows[block:]),
        returned(natural[:block], natural[block:].astype(BF16)),
        own_up,
        own_down[:, :part].T,
        jnp.stack([columns(own_att, i) for i in range(3)]),
        columns(own_middle, 0).T,
        tail[:bias_rows].reshape(heads, table_part),
        jnp.stack([columns(own_middle, 1), columns(own_middle, 2)]),
        per_channel[:, :kernel],
        per_channel[:, kernel:tap_n].T,
        columns(own_turn, 0).T,
        own_turn[:, head_width : head_width + part],
        own_turn[:, head_width + part :].T,
        own_down[:, part : part + 5].T,
    )


def solution(mesh):
    placed = (
        P(None, "dp", None),
        P(None, "dp", None),
        P("dp", "mp"),
        P("mp", "dp"),
        P(None, "dp", "mp"),
        P("mp", "dp"),
        P("mp", "dp"),
        P(None, "dp", "mp"),
        P(("mp", "dp"), None),
        P(None, ("mp", "dp")),
        P("mp", "dp"),
        P("dp", "mp"),
        P("mp", "dp"),
        P(None, "dp"),
    )
    returned = (P(None, ("dp", "mp"), None), P(None, ("dp", "mp"), None)) + placed[2:]
    return jax.shard_map(block_step, mesh=mesh, in_specs=placed, out_specs=returned, check_vma=False)
```

```python
import functools

import jax
import jax.numpy as jnp
from jax import lax
from jax.experimental import pallas as pl
from jax.experimental.pallas import tpu as pltpu
from jax.sharding import PartitionSpec as P


EPS = 1e-05
BF16 = jnp.bfloat16
F32 = jnp.float32
SUB = 128
NT = (((1,), (1,)), ((), ()))


def flip_pair(value, axis, bit):
    return lax.ppermute(value, axis, [(i, i ^ 1 << bit) for i in range(lax.axis_size(axis))])


def bits_of(axis):
    return (lax.axis_size(axis) - 1).bit_length()


def own_bit(axis, bit):
    return lax.shift_right_logical(lax.axis_index(axis), bit) & 1


def full_order():
    dp_bits, mp_bits = bits_of("dp"), bits_of("mp")
    dp_high = [("dp", bit) for bit in range(dp_bits - 1, 0, -1)]
    mp_high = [("mp", bit) for bit in range(mp_bits - 1, 0, -1)]
    first = dp_high + [("dp", 0)] + mp_high + [("mp", 0)]
    second = dp_high + mp_high + [("dp", 0)] + [("mp", 0)]
    return (first, second)


def tied(value, other):
    return lax.optimization_barrier((value, other))[0]


def gather_groups(shard, order):
    held = {0: shard}
    for axis, bit in order:
        for delta in list(held):
            own = held[delta]
            other = flip_pair(own, axis, bit)
            if axis == "mp":
                held[delta ^ 1 << bit] = other
            else:
                held[delta] = jnp.concatenate([own, other], axis=0)
    return held


def scatter_groups(parts, order, marks=None):
    parts = dict(parts)
    total = None
    for axis, bit in reversed(order):
        if axis == "mp":
            for delta in [d for d in parts if d >> bit & 1]:
                other = flip_pair(parts.pop(delta), axis, bit)
                home = delta ^ 1 << bit
                parts[home] = (parts[home].astype(F32) + other.astype(F32)).astype(BF16)
        else:
            for delta in parts:
                half = parts[delta].shape[0] // 2
                keep, send = parts[delta][:half], parts[delta][half:]
                other = flip_pair(send, axis, bit)
                total = keep.astype(F32) + other.astype(F32)
                parts[delta] = total.astype(BF16)
        if marks is not None:
            marks.append(dict(parts))
    return total


def reversed_blocks(count):
    bits = (count - 1).bit_length()
    return [int(format(i, "b").zfill(bits)[::-1], 2) if bits else 0 for i in range(count)]


def block_choice(features, count, dtype):
    row = lax.broadcasted_iota(jnp.int32, (features, features), 0)
    col = lax.broadcasted_iota(jnp.int32, (features, features), 1)
    size = features // count
    block, image = col // size, jnp.zeros_like(col)
    for bit in range((count - 1).bit_length()):
        image = image * 2 + (block >> bit & 1)
    image = image ^ lax.axis_index("dp")
    return (row == image * size + col % size).astype(dtype)


def lane_flip(dtype):
    row = lax.broadcasted_iota(jnp.int32, (SUB, SUB), 0)
    col = lax.broadcasted_iota(jnp.int32, (SUB, SUB), 1)
    return (row + col == SUB - 1).astype(dtype)


def regroup(parts, widths, count):
    if count == 1:
        return parts
    joined = []
    for start in range(0, len(parts), count):
        pieces, at = [], 0
        for width in widths:
            pieces += [part[:, at : at + width] for part in parts[start : start + count]]
            at += width
        joined.append(jnp.concatenate(pieces, axis=1))
    return joined


def ungroup(parts, widths, count):
    if count == 1:
        return parts
    split = []
    for part in parts:
        for i in range(count):
            pieces, at = [], 0
            for width in widths:
                pieces.append(part[:, at + i * width : at + (i + 1) * width])
                at += width * count
            split.append(jnp.concatenate(pieces, axis=1))
    return split


def swap_groups(value, groups, delta):
    width = value.shape[-1] // groups
    parts = [value[..., (g ^ delta) * width : ((g ^ delta) + 1) * width] for g in range(groups)]
    return jnp.concatenate(parts, axis=-1)


def absolute_groups(value, groups):
    for bit in range((groups - 1).bit_length()):
        value = jnp.where(own_bit("mp", bit) == 0, value, swap_groups(value, groups, 1 << bit))
    return value


def channel_total(sums):
    groups = lax.axis_size("mp")
    for bit in range(bits_of("mp")):
        sums = sums + swap_groups(flip_pair(sums, "mp", bit), groups, 1 << bit)
    for bit in range(1, bits_of("dp")):
        sums = sums + flip_pair(sums, "dp", bit)
    return sums


def edge_rows(first_rows, last_rows, half_of_slot):
    groups = lax.axis_size("mp")
    place = lax.axis_index("mp")
    up = [(i, (i + 1) % groups) for i in range(groups)]
    down = [(i, (i - 1) % groups) for i in range(groups)]
    before = lax.ppermute(absolute_groups(last_rows, groups), "mp", up)
    after = lax.ppermute(absolute_groups(first_rows, groups), "mp", down)
    before = absolute_groups(before, groups)
    after = absolute_groups(after, groups)
    second = half_of_slot[:, None, None] == 1
    nothing = jnp.zeros_like(before)
    before = jnp.where(place == 0, jnp.where(second, before[::-1], nothing), before)
    after = jnp.where(place == groups - 1, jnp.where(second, nothing, after[::-1]), after)
    return (before, after)


def swish_grad(value):
    logistic = jax.nn.sigmoid(value)
    return logistic * (1.0 + value * (1.0 - logistic))


def normed_of(value):
    centred = value - jnp.mean(value, axis=-1, keepdims=True)
    inverse = lax.rsqrt(jnp.mean(centred * centred, axis=-1, keepdims=True) + EPS)
    return (centred * inverse, inverse)


def norm_back(normed, inverse, gain, upstream):
    scaled = upstream * gain
    inner = (
        scaled
        - jnp.mean(scaled, axis=-1, keepdims=True)
        - normed * jnp.mean(scaled * normed, axis=-1, keepdims=True)
    )
    return (inverse * inner, jnp.sum(upstream * normed, axis=0, keepdims=True))


def mm(left, right):
    return jnp.dot(left, right, preferred_element_type=F32)


def mm_nt(left, right):
    return lax.dot_general(left, right, NT, preferred_element_type=F32)


def call_kernel(kernel, outs, *inputs):
    return pl.pallas_call(
        kernel, out_shape=[jax.ShapeDtypeStruct(shape, dtype) for shape, dtype in outs]
    )(*inputs)


def column_join(refs, index):
    return jnp.concatenate([ref[:, index * SUB : (index + 1) * SUB] for ref in refs], axis=1)


def ffn_forward_kernel(groups, v_ref, gain_ref, *refs):
    ups, downs, out_ref = refs[:groups], refs[groups : 2 * groups], refs[-1]
    value = v_ref[...]
    normed, _ = normed_of(value)
    active = (normed * gain_ref[...]).astype(BF16)
    total = jnp.zeros_like(value)
    for up_ref, down_ref in zip(ups, downs):
        pre = mm(active, up_ref[...])
        hidden = (pre * jax.nn.sigmoid(pre)).astype(BF16)
        total += mm_nt(hidden, down_ref[...])
    out_ref[...] = value + 0.5 * total


def ffn_backward_kernel(groups, v_ref, d_ref, gain_ref, one_ref, two_ref, last_ref, *refs):
    ups, downs = refs[:groups], refs[groups : 2 * groups]
    out_ref = refs[2 * groups]
    gus, gds = refs[2 * groups + 1 : 3 * groups + 1], refs[3 * groups + 1 :]
    part = ups[0].shape[1]
    normed, inverse = normed_of(v_ref[...])
    upstream = d_ref[...]
    active = (normed * gain_ref[...]).astype(BF16)
    error = (0.5 * upstream).astype(BF16)
    active_t = active.T
    error_t = error.T
    total = jnp.zeros_like(upstream)
    for up_ref, down_ref, gu_ref, gd_ref in zip(ups, downs, gus, gds):
        pre = mm(active, up_ref[...])
        logistic = jax.nn.sigmoid(pre)
        hidden = (pre * logistic).astype(BF16)
        gd_ref[:, :part] = mm(error_t, hidden).astype(BF16)
        d_hidden = mm(error, down_ref[...])
        d_pre = (d_hidden * (logistic * (1.0 + pre * (1.0 - logistic)))).astype(BF16)
        gu_ref[...] = mm(active_t, d_pre).astype(BF16)
        total += mm_nt(d_pre, up_ref[...])
    back, grad_gain = norm_back(normed, inverse, gain_ref[...], total)
    out_ref[...] = upstream + back
    known = [grad_gain, one_ref[...], two_ref[...], last_ref[...]]
    count = sum(value.shape[0] for value in known)
    known.append(jnp.zeros((SUB - count, upstream.shape[1]), F32))
    columns = jnp.concatenate(known, axis=0).T.astype(BF16)
    for gd_ref in gds:
        gd_ref[:, part:] = columns


def project_kernel(groups, v_ref, gain_ref, *refs):
    weights, q_ref = refs[:groups], refs[groups]
    pair_refs = refs[groups + 1 :]
    normed, _ = normed_of(v_ref[...])
    active = (normed * gain_ref[...]).astype(BF16)
    q_ref[...] = mm(active, column_join(weights, 0)).astype(BF16)
    width = q_ref.shape[1] // len(pair_refs)
    for i in (0, 1):
        projected = mm(active, column_join(weights, i + 1)).astype(BF16)
        for h, pair_ref in enumerate(pair_refs):
            pair_ref[i] = projected[:, h * width : (h + 1) * width]


def project_backward_kernel(groups, halves, v_ref, d_ref, gain_ref, *refs):
    weights, smalls = refs[:groups], refs[groups : 2 * groups]
    dqs = refs[2 * groups : 2 * groups + halves]
    pairs = refs[2 * groups + halves : 2 * groups + 2 * halves]
    others = refs[2 * groups + 2 * halves : 2 * groups + 3 * halves]
    out_ref, gg_ref = refs[2 * groups + 3 * halves : 2 * groups + 3 * halves + 2]
    grads = refs[2 * groups + 3 * halves + 2 :]
    normed, inverse = normed_of(v_ref[...])
    active_t = (normed * gain_ref[...]).astype(BF16).T
    total = jnp.zeros_like(d_ref[...])
    for i in range(3):
        if i == 0:
            parts = [ref[...] for ref in dqs]
        else:
            parts = [
                (ref[i - 1].astype(F32) + other[i - 1].astype(F32)).astype(BF16)
                for ref, other in zip(pairs, others)
            ]
        error = jnp.concatenate(parts, axis=1) if halves > 1 else parts[0]
        total += mm_nt(error, column_join(weights, i))
        grad = mm(active_t, error).astype(BF16)
        for g, grad_ref in enumerate(grads):
            grad_ref[:, i * SUB : (i + 1) * SUB] = grad[:, g * SUB : (g + 1) * SUB]
    for small_ref, grad_ref in zip(smalls, grads):
        grad_ref[:, 3 * SUB :] = small_ref[...]
    back, grad_gain = norm_back(normed, inverse, gain_ref[...], total)
    out_ref[...] = d_ref[...] + back
    gg_ref[...] = grad_gain


def middle_kernel(groups, halves, v_ref, gain_ref, *refs):
    weights, contexts = refs[:groups], refs[groups : groups + halves]
    out_ref, lin_ref, sig_ref, glu_ref = refs[groups + halves :]
    parts = [ref[...] for ref in contexts]
    context = jnp.concatenate(parts, axis=1) if halves > 1 else parts[0]
    value = v_ref[...] + mm_nt(context, column_join(weights, 0))
    out_ref[...] = value
    normed, _ = normed_of(value)
    active = (normed * gain_ref[...]).astype(BF16)
    lin = mm(active, column_join(weights, 1))
    gate = jax.nn.sigmoid(mm(active, column_join(weights, 2)))
    lin_ref[...] = lin
    sig_ref[...] = gate
    glu_ref[...] = (lin * gate).astype(BF16)


def middle_backward_kernel(groups, halves, dglu_ref, lin_ref, sig_ref, v_ref, d_ref, gain_ref, *refs):
    weights, contexts = refs[:groups], refs[groups : groups + halves]
    out_ref, gg_ref, dctx_ref = refs[groups + halves : groups + halves + 3]
    grads = refs[groups + halves + 3 :]
    d_glu, lin, gate = dglu_ref[...], lin_ref[...], sig_ref[...]
    d_lin = (d_glu * gate).astype(BF16)
    d_gate = (d_glu * lin * gate * (1.0 - gate)).astype(BF16)
    normed, inverse = normed_of(v_ref[...])
    active_t = (normed * gain_ref[...]).astype(BF16).T
    total = mm_nt(d_lin, column_join(weights, 1)) + mm_nt(d_gate, column_join(weights, 2))
    back, grad_gain = norm_back(normed, inverse, gain_ref[...], total)
    value = d_ref[...] + back
    out_ref[...] = value
    gg_ref[...] = grad_gain
    error = value.astype(BF16)
    dctx_ref[...] = mm(error, column_join(weights, 0)).astype(BF16)
    parts = [ref[...] for ref in contexts]
    context = jnp.concatenate(parts, axis=1) if halves > 1 else parts[0]
    for i, grad in enumerate((mm(error.T, context), mm(active_t, d_lin), mm(active_t, d_gate))):
        rounded = grad.astype(BF16)
        for g, grad_ref in enumerate(grads):
            grad_ref[:, i * SUB : (i + 1) * SUB] = rounded[:, g * SUB : (g + 1) * SUB]


def turn_kernel(groups, batch_rows, conv_ref, stat_ref, bn_ref, v_ref, up_ref, gains_ref, *refs):
    weights = refs[:groups]
    final_ref, out_ref, dpre_ref, gg_ref, sums_ref = refs[groups : groups + 5]
    grads, pres = refs[groups + 5 : -1], refs[-1]
    part = pres.shape[2]
    top, bottom = slice(4 * SUB, 4 * SUB + part), slice(4 * SUB + part, 4 * SUB + 2 * part)
    gain_three, gain_four = gains_ref[3:4], gains_ref[4:5]
    mean = stat_ref[0:1] / batch_rows
    white = (conv_ref[...] - mean) * lax.rsqrt(stat_ref[1:2] / batch_rows - mean * mean + EPS)
    bn_pre = bn_ref[0:1] * white + bn_ref[1:2]
    activated = (bn_pre * jax.nn.sigmoid(bn_pre)).astype(BF16)
    outward = column_join(weights, 3)
    third = v_ref[...] + mm_nt(activated, outward)
    normed, inverse = normed_of(third)
    active = (normed * gain_three).astype(BF16)
    total = jnp.zeros_like(third)
    for g, weight in enumerate(weights):
        pre = mm(active, weight[:, top])
        pres[g] = pre
        total += mm_nt((pre * jax.nn.sigmoid(pre)).astype(BF16), weight[:, bottom])
    last_normed, last_inverse = normed_of(third + 0.5 * total)
    final_ref[...] = (last_normed * gain_four).astype(BF16)
    fourth, grad_four = norm_back(last_normed, last_inverse, gain_four, up_ref[...])
    error = (0.5 * fourth).astype(BF16)
    active_t = active.T
    error_t = error.T
    total = jnp.zeros_like(third)
    for g, (weight, grad_ref) in enumerate(zip(weights, grads)):
        pre = pres[g]
        logistic = jax.nn.sigmoid(pre)
        hidden = (pre * logistic).astype(BF16)
        grad_ref[:, SUB + part :] = mm(error_t, hidden).astype(BF16)
        d_hidden = mm(error, weight[:, bottom])
        d_pre = (d_hidden * (logistic * (1.0 + pre * (1.0 - logistic)))).astype(BF16)
        grad_ref[:, SUB : SUB + part] = mm(active_t, d_pre).astype(BF16)
        total += mm_nt(d_pre, weight[:, top])
    back, grad_three = norm_back(normed, inverse, gain_three, total)
    value = fourth + back
    out_ref[...] = value
    gg_ref[0:1] = grad_three
    gg_ref[1:2] = grad_four
    error = value.astype(BF16)
    grad = mm(error.T, activated).astype(BF16)
    for g, grad_ref in enumerate(grads):
        grad_ref[:, :SUB] = grad[:, g * SUB : (g + 1) * SUB]
    d_pre = mm(error, outward) * swish_grad(bn_pre)
    dpre_ref[...] = d_pre
    sums_ref[0:1] = jnp.sum(d_pre, axis=0, keepdims=True)
    sums_ref[1:2] = jnp.sum(d_pre * white, axis=0, keepdims=True)


def build_skew(line_ref, skew, heads, chunks):
    for h in range(heads):
        for c in range(chunks):
            window = jnp.concatenate(
                [line_ref[0, h, c + 1 : c + 2, :], line_ref[0, h, c : c + 1, :]], axis=1
            )
            window = jnp.broadcast_to(window, (SUB, 2 * SUB))
            rolled = pltpu.roll(window, 1, 1, stride=1, stride_axis=0)
            skew[h, SUB * c : SUB * (c + 1), :] = rolled[:, SUB:]


def stack_heads(rows, heads, factor):
    lane = lax.broadcasted_iota(jnp.int32, rows.shape, 1)
    size = rows.shape[1] // heads
    return jnp.concatenate(
        [
            rows * jnp.where((lane >= h * size) & (lane < (h + 1) * size), factor, 0.0).astype(BF16)
            for h in range(heads)
        ],
        axis=0,
    )


def diagonal_heads(value, heads):
    size, columns = value.shape[0] // heads, value.shape[1] // heads
    parts = [
        value[h * size : (h + 1) * size, h * columns : (h + 1) * columns] for h in range(heads)
    ]
    return jnp.concatenate(parts, axis=0)


def tile_bias(skew, columns, block, offset_of):
    parts = [
        skew[h, pl.ds(pl.multiple_of(offset_of(qb), SUB), block), :] for h, qb in columns
    ]
    return jnp.concatenate(parts, axis=1)


def column_tiles(heads, steps):
    columns = [(h, qb) for h in range(heads) for qb in range(steps)]
    return [columns[i : i + 2] for i in range(0, len(columns), 2)]


def attend_forward_kernel(pieces, heads, qpos, kpos, q_ref, line_ref, *refs):
    k_refs = refs[:pieces]
    v_refs = refs[pieces : 2 * pieces]
    ctx_ref, lse_ref, ctx32_ref, skew, query, scores, probs, v_t = refs[2 * pieces :]
    rows, width = q_ref.shape
    block = rows // 2
    chunks = skew.shape[1] // SUB
    middle = skew.shape[1] // 2
    tiles = column_tiles(heads, rows // SUB)
    span = 2 * SUB
    build_skew(line_ref, skew, heads, chunks)
    for p in range(pieces):
        v_t[:width, p * rows : (p + 1) * rows] = v_refs[p][0].T
    v_t[width:, :] = jnp.ones_like(v_t[width:, :])
    query[...] = stack_heads(q_ref[...], heads, (width // heads) ** (-0.5))
    tops = [jnp.full((8, span), -jnp.inf, F32) for _ in tiles]
    for c in range(2 * pieces):
        keys = k_refs[c // 2][0, (c % 2) * block : (c % 2 + 1) * block, :]
        for t, tile in enumerate(tiles):
            raw = mm_nt(keys, query[t * span : (t + 1) * span, :])
            raw = raw + tile_bias(skew, tile, block, lambda qb: kpos[c] - qpos[qb] + middle)
            scores[c * block : (c + 1) * block, t * span : (t + 1) * span] = raw
            tops[t] = jnp.maximum(tops[t], jnp.max(raw.reshape(block // 8, 8, span), axis=0))
    tops = [jnp.max(top, axis=0, keepdims=True) for top in tops]
    for c in range(2 * pieces):
        for t in range(len(tiles)):
            part = (slice(c * block, (c + 1) * block), slice(t * span, (t + 1) * span))
            probs[part] = jnp.exp(scores[part] - tops[t]).astype(BF16)
    out_t = mm(v_t[...], probs[...])
    total = out_t[width : width + 1, :]
    out_t = out_t[:width, :] / total
    out = diagonal_heads(out_t, heads).T
    ctx_ref[...] = out.astype(BF16)
    ctx32_ref[...] = out
    lse_ref[0] = jnp.concatenate(tops, axis=1) + jnp.log(total)


def attend_backward_kernel(pieces, heads, qpos, kpos, q_ref, d_ref, ctx_ref, lse_ref, line_ref, *refs):
    k_refs = refs[:pieces]
    v_refs = refs[pieces : 2 * pieces]
    dq_ref = refs[2 * pieces]
    dkv_refs = refs[2 * pieces + 1 : 3 * pieces + 1]
    line_grad, skew, skew_grad, query, error, probs, d_scores, k_t = refs[3 * pieces + 1 :]
    rows, width = q_ref.shape
    block = rows // 2
    chunks = skew.shape[1] // SUB
    middle = skew.shape[1] // 2
    scale = (width // heads) ** (-0.5)
    size = width // heads
    tiles = column_tiles(heads, rows // SUB)
    span = 2 * SUB
    build_skew(line_ref, skew, heads, chunks)
    skew_grad[...] = jnp.zeros_like(skew_grad)
    for p in range(pieces):
        k_t[:, p * rows : (p + 1) * rows] = k_refs[p][0].T
    query[...] = stack_heads(q_ref[...], heads, scale)
    error[...] = stack_heads(d_ref[...], heads, 1.0)
    weighed = (d_ref[...].astype(F32) * ctx_ref[...]).T
    dot_sum = jnp.concatenate(
        [jnp.sum(weighed[h * size : (h + 1) * size], axis=0, keepdims=True) for h in range(heads)],
        axis=1,
    )
    lse = lse_ref[0]
    for c in range(2 * pieces):
        part = slice((c % 2) * block, (c % 2 + 1) * block)
        here = slice(c * block, (c + 1) * block)
        keys = k_refs[c // 2][0, part, :]
        values = v_refs[c // 2][0, part, :]
        for t, tile in enumerate(tiles):
            cols = slice(t * span, (t + 1) * span)
            raw = mm_nt(keys, query[cols, :])
            bias = tile_bias(skew, tile, block, lambda qb: kpos[c] - qpos[qb] + middle)
            prob = jnp.exp(raw + bias - lse[:, cols])
            d_score = prob * (mm_nt(values, error[cols, :]) - dot_sum[:, cols])
            probs[c % 2, :, cols] = prob.astype(BF16)
            d_scores[here, cols] = d_score.astype(BF16)
            for i, (h, qb) in enumerate(tile):
                offset = pl.multiple_of(kpos[c] - qpos[qb] + middle, SUB)
                skew_grad[h, pl.ds(offset, block), :] += d_score[:, i * SUB : (i + 1) * SUB]
        dkv_refs[c // 2][0, part, :] = mm(d_scores[here, :], query[...]).astype(BF16)
        dkv_refs[c // 2][1, part, :] = mm(probs[c % 2], error[...]).astype(BF16)
    dq_t = mm(k_t[...], d_scores[...])
    dq_ref[...] = (diagonal_heads(dq_t, heads).T * scale).astype(BF16)
    line_grad[...] = jnp.zeros_like(line_grad)
    for h in range(heads):
        for c in range(chunks):
            block_grad = skew_grad[h, SUB * c : SUB * (c + 1), :]
            value = jnp.concatenate([jnp.zeros_like(block_grad), block_grad], axis=1)
            half = SUB // 2
            while half >= 1:
                value = value[:half] + pltpu.roll(value[half:], 2 * SUB - half, 1)
                half //= 2
            value = pltpu.roll(value, 2 * SUB - 1, 1)
            line_grad[0, h, c + 1 : c + 2, :] += value[:, :SUB]
            line_grad[0, h, c : c + 1, :] += value[:, SUB:]


def attention_specs(rows, first, pieces, shifts, line_shape):
    whole_q = pl.BlockSpec((rows, SUB), lambda j, *_: (0, j + first))
    own = pl.BlockSpec((rows, SUB), lambda j, *_: (0, j))
    line = pl.BlockSpec((1,) + line_shape[1:], lambda j, *_: (j + first, 0, 0, 0))
    keys, values = [], []
    for p in range(pieces):
        keys.append(pl.BlockSpec((1, rows, SUB), lambda j, *_, d=shifts[p]: (0, 0, j ^ d)))
        values.append(pl.BlockSpec((1, rows, SUB), lambda j, *_, d=shifts[p]: (1, 0, j ^ d)))
    return (whole_q, own, line, keys, values)


def attend_forward(query, pairs, shifts, line, first, qpos, kpos):
    rows = query.shape[0]
    heads = line.shape[1]
    groups = pairs[0].shape[2] // SUB
    pieces = len(pairs)
    table = (line.shape[2] - 1) * SUB
    whole_q, own, line_spec, keys, values = attention_specs(rows, first, pieces, shifts, line.shape)
    return pl.pallas_call(
        functools.partial(attend_forward_kernel, pieces, heads),
        out_shape=(
            jax.ShapeDtypeStruct((rows, groups * SUB), BF16),
            jax.ShapeDtypeStruct((groups, 1, heads * rows), F32),
            jax.ShapeDtypeStruct((rows, groups * SUB), F32),
        ),
        grid_spec=pltpu.PrefetchScalarGridSpec(
            num_scalar_prefetch=2,
            grid=(groups,),
            in_specs=[whole_q, line_spec] + keys + values,
            out_specs=(
                own,
                pl.BlockSpec((1, 1, heads * rows), lambda j, *_: (j, 0, 0)),
                own,
            ),
            scratch_shapes=[
                pltpu.VMEM((heads, table, SUB), F32),
                pltpu.VMEM((heads * rows, SUB), BF16),
                pltpu.VMEM((pieces * rows, heads * rows), F32),
                pltpu.VMEM((pieces * rows, heads * rows), BF16),
                pltpu.VMEM((SUB + 16, pieces * rows), BF16),
            ],
        ),
        name="attend_forward",
    )(qpos, kpos, query, line, *pairs, *pairs)


def attend_backward(query, d_context, lse, context, pairs, shifts, line, first, qpos, kpos):
    rows = query.shape[0]
    heads = line.shape[1]
    groups = pairs[0].shape[2] // SUB
    pieces = len(pairs)
    table = (line.shape[2] - 1) * SUB
    whole_q, own, line_spec, keys, values = attention_specs(rows, first, pieces, shifts, line.shape)
    lse_spec = pl.BlockSpec((1, 1, heads * rows), lambda j, *_: (j, 0, 0))
    pair_specs = [
        pl.BlockSpec((2, rows, SUB), lambda j, *_, d=shifts[p]: (0, 0, j ^ d))
        for p in range(pieces)
    ]
    return pl.pallas_call(
        functools.partial(attend_backward_kernel, pieces, heads),
        out_shape=(
            (jax.ShapeDtypeStruct((rows, groups * SUB), BF16),)
            + tuple(jax.ShapeDtypeStruct(pairs[0].shape, BF16) for _ in range(pieces))
            + (jax.ShapeDtypeStruct((groups,) + line.shape[1:], F32),)
        ),
        grid_spec=pltpu.PrefetchScalarGridSpec(
            num_scalar_prefetch=2,
            grid=(groups,),
            in_specs=[whole_q, whole_q, own, lse_spec, line_spec] + keys + values,
            out_specs=(
                (own,)
                + tuple(pair_specs)
                + (pl.BlockSpec((1,) + line.shape[1:], lambda j, *_: (j, 0, 0, 0)),)
            ),
            scratch_shapes=[
                pltpu.VMEM((heads, table, SUB), F32),
                pltpu.VMEM((heads, table, SUB), F32),
                pltpu.VMEM((heads * rows, SUB), BF16),
                pltpu.VMEM((heads * rows, SUB), BF16),
                pltpu.VMEM((2, rows // 2, heads * rows), BF16),
                pltpu.VMEM((pieces * rows, heads * rows), BF16),
                pltpu.VMEM((SUB, pieces * rows), BF16),
            ],
        ),
        name="attend_backward",
    )(qpos, kpos, query, d_context, context, lse, line, *pairs, *pairs)


def block_step(
    block_input,
    out_cotangent,
    early_up,
    early_down,
    attention_in,
    attention_out,
    relative_bias,
    pointwise_in,
    depthwise,
    batch_norm,
    pointwise_out,
    late_up,
    late_down,
    norm_gains,
):
    dp_n, mp_n = lax.axis_size("dp"), lax.axis_size("mp")
    held_rows, features = block_input.shape[1:]
    block = held_rows // mp_n
    rows = 2 * block
    batch_rows = held_rows * dp_n
    batch = lax.axis_index("dp") % 2
    place = lax.axis_index("mp")
    shard_rows, part = early_up.shape
    heads, table_part = relative_bias.shape
    channel_part, kernel = depthwise.shape
    head_width = attention_out.shape[0]
    channels = mp_n * head_width
    margin = (kernel - 1) // 2
    order_a, order_b = full_order()
    fold = max(1, SUB // head_width)
    groups = mp_n // fold
    blocks = jnp.array(reversed_blocks(dp_n), jnp.int32)
    to_natural = blocks[jnp.arange(dp_n, dtype=jnp.int32) ^ lax.axis_index("dp")]
    to_held = blocks ^ lax.axis_index("dp")
    choice = block_choice(features, dp_n, BF16)

    def exchanged(value):
        mine = lax.dynamic_slice_in_dim(value, place * block, block, 1)
        own = lax.dynamic_index_in_dim(mine, batch, 0, keepdims=False)
        away = lax.dynamic_index_in_dim(mine, 1 - batch, 0, keepdims=False)
        other = flip_pair(away, "dp", 0)
        return mm(jnp.concatenate([own, other], axis=0), choice)

    def listed(parts, widths):
        return regroup([parts[delta] for delta in range(mp_n)], widths, fold)

    def unlisted(parts, widths):
        return dict(enumerate(ungroup(list(parts), widths, fold)))

    bias_rows = heads * table_part // SUB
    tap_n = kernel + 2
    gain_row = bias_rows + channel_part
    small_rows = gain_row + norm_gains.shape[0]
    small = jnp.concatenate(
        [
            relative_bias.reshape(bias_rows, SUB),
            jnp.pad(jnp.concatenate([depthwise, batch_norm.T], axis=1), ((0, 0), (0, SUB - tap_n))),
            jnp.pad(norm_gains, ((0, shard_rows - small_rows), (0, SUB - shard_rows))),
        ],
        axis=0,
    )
    early_u = gather_groups(early_up, order_a)
    early_d = gather_groups(early_down.T, order_b)
    start = exchanged(block_input)
    pair_widths = [head_width] * 3
    att_shard = jnp.concatenate([attention_in[0], attention_in[1], attention_in[2], small], axis=1)
    att_held = gather_groups(att_shard, order_b)
    rest_widths = [head_width] * 4 + [part] * 2
    rest_shard = jnp.concatenate(
        [
            attention_out.T,
            pointwise_in[0],
            pointwise_in[1],
            pointwise_out.T,
            late_up,
            late_down.T,
        ],
        axis=1,
    )
    rest = listed(gather_groups(rest_shard, order_b), rest_widths)
    if fold == 1:
        att = [att_held[delta] for delta in range(mp_n)]
    else:
        att = listed({d: value[:, : 3 * head_width] for d, value in att_held.items()}, pair_widths)
    gains = (
        att_held[0]
        .reshape(dp_n, shard_rows, -1)[:, gain_row:small_rows, 3 * head_width : 3 * head_width + shard_rows]
        .transpose(1, 0, 2)
        .reshape(5, features)
        .astype(F32)
    )
    gain = [gains[i : i + 1] for i in range(5)]
    tiny = jnp.stack([att_held[delta][:, 3 * head_width :] for delta in range(mp_n)])
    tiny = tiny.reshape(mp_n, dp_n, shard_rows, SUB)[:, to_natural]
    line = (
        tiny[:, :, :bias_rows]
        .reshape(mp_n, dp_n, heads, table_part // SUB, SUB)
        .transpose(0, 2, 1, 3, 4)
        .reshape(mp_n, heads, dp_n * table_part // SUB, SUB)
    )
    line = jnp.einsum("ghcl,lk->ghck", line, lane_flip(BF16), preferred_element_type=F32)
    line = jnp.pad(line, ((0, 0), (0, 0), (1, 0), (0, 0)))
    line = line.reshape(groups, heads * fold, line.shape[2], SUB)
    taps = (
        tiny[:, :, bias_rows : bias_rows + channel_part, :tap_n].reshape(channels, tap_n).T.astype(F32)
    )

    half_of_slot = jnp.stack([batch, 1 - batch]).astype(jnp.int32)
    kept = [0]
    for bit in range(bits_of("mp") - 1, -1, -1):
        kept = kept + [delta ^ 1 << bit for delta in kept]
    qpos = (
        half_of_slot[:, None] * held_rows
        + place * block
        + SUB * jnp.arange(block // SUB, dtype=jnp.int32)[None, :]
    ).reshape(-1)
    kpos = jnp.stack(
        [half_of_slot[r] * held_rows + (place ^ delta) * block for delta in kept for r in (0, 1)]
    )
    wide = (rows, channels)
    halves = 2 if fold == 1 and mp_n >= 4 else 1
    local = groups // halves
    up_list = [early_u[delta] for delta in range(mp_n)]
    down_list = [early_d[delta] for delta in range(mp_n)]
    (after_first,) = call_kernel(
        functools.partial(ffn_forward_kernel, mp_n),
        [((rows, features), F32)],
        start,
        gain[0],
        *up_list,
        *down_list,
    )
    query, *pair_halves = call_kernel(
        functools.partial(project_kernel, groups),
        [(wide, BF16)] + [((2, rows, local * SUB), BF16)] * halves,
        after_first,
        gain[1],
        *att,
    )
    top_bit = bits_of("mp") - 1
    held_pairs = []
    for h in range(halves):
        pieces = [pair_halves[h]]
        away = pair_halves[halves - 1 - h]
        if h > 0:
            away = tied(away, held_pairs[h - 1][1])
        pieces.append(flip_pair(away, "mp", top_bit))
        for bit in range(top_bit - 1, -1, -1):
            pieces = pieces + [flip_pair(piece, "mp", bit) for piece in pieces]
        if fold > 1:
            pieces = [swap_groups(piece, mp_n, delta) for piece, delta in zip(pieces, kept)]
        held_pairs.append(pieces)
    shifts = [delta & (local - 1) if fold == 1 else 0 for delta in kept]
    attended = []
    for h in range(halves):
        attended.append(attend_forward(query, held_pairs[h], shifts, line, h * local, qpos, kpos))
    contexts = [item[0] for item in attended]
    after_second, lin, gate_sig, glu = call_kernel(
        functools.partial(middle_kernel, groups, halves),
        [((rows, features), F32), (wide, F32), (wide, F32), (wide, BF16)],
        after_first,
        gain[2],
        *rest,
        *contexts,
    )
    cotangent = exchanged(out_cotangent)
    glu = tied(glu, cotangent).reshape(2, block, channels)
    edge = margin + 1
    before, after = edge_rows(glu[:, :edge], glu[:, block - edge :], half_of_slot)
    extended = jnp.concatenate([before[:, 1:], glu, after[:, :margin]], axis=1).astype(F32)
    conv = jnp.zeros((2, block, channels), F32)
    for tap in range(kernel):
        conv = conv + taps[tap] * extended[:, tap : tap + block]
    conv = conv.reshape(rows, channels)
    sums = channel_total(jnp.stack([jnp.sum(conv, axis=0), jnp.sum(conv * conv, axis=0)]))
    bmean = sums[0:1] / batch_rows
    binv = lax.rsqrt(sums[1:2] / batch_rows - bmean * bmean + EPS)
    bn_rows = taps[kernel:]

    wide_part = part * fold
    turn_widths = [head_width, part, part]
    final_rows, d_third, d_pre, gg_last, local_sums, *turn_grads = pl.pallas_call(
        functools.partial(turn_kernel, groups, batch_rows),
        out_shape=[
            jax.ShapeDtypeStruct((rows, features), BF16),
            jax.ShapeDtypeStruct((rows, features), F32),
            jax.ShapeDtypeStruct(wide, F32),
            jax.ShapeDtypeStruct((2, features), F32),
            jax.ShapeDtypeStruct((2, channels), F32),
        ]
        + [jax.ShapeDtypeStruct((features, SUB + 2 * wide_part), BF16)] * groups,
        scratch_shapes=[pltpu.VMEM((groups, rows, wide_part), F32)],
        name="turn",
    )(conv, sums, bn_rows, after_second, cotangent, gains, *rest)
    turn_marks = []
    own_turn = scatter_groups(unlisted(turn_grads, turn_widths), order_a, turn_marks)

    sums = channel_total(local_sums)
    white = (conv - bmean) * binv
    d_conv = (
        binv * bn_rows[0:1] * (d_pre - sums[0:1] / batch_rows - white * sums[1:2] / batch_rows)
    ).reshape(2, block, channels)
    before, after = edge_rows(d_conv[:, :edge], d_conv[:, block - edge :], half_of_slot)
    d_extended = jnp.concatenate([before[:, 1:], d_conv, after[:, :margin]], axis=1)
    d_glu = jnp.zeros((2, block, channels), F32)
    tap_grads = []
    for tap in range(kernel):
        d_glu = d_glu + taps[tap] * d_extended[:, kernel - 1 - tap : kernel - 1 - tap + block]
        tap_grads.append(jnp.sum(extended[:, tap : tap + block] * d_conv, axis=(0, 1)))
    tap_grads = jnp.stack(tap_grads + [local_sums[1], local_sums[0]])
    d_second, gain_two, d_context, *middle_grads = call_kernel(
        functools.partial(middle_backward_kernel, groups, halves),
        [((rows, features), F32), (gain[2].shape, F32), (wide, BF16)]
        + [((features, 3 * SUB), BF16)] * groups,
        tied(d_glu.reshape(rows, channels), turn_marks[0][1 << top_bit]),
        lin,
        gate_sig,
        after_second,
        d_third,
        gain[2],
        *rest,
        *contexts,
    )
    own_middle = scatter_groups(unlisted(middle_grads, pair_widths), order_b)
    d_queries, kept_pairs, sent_pairs, line_grads = [], [], [], []
    for h in range(halves):
        grads = attend_backward(
            query, d_context, attended[h][1], attended[h][2], held_pairs[h], shifts, line,
            h * local, qpos, kpos,
        )
        d_queries.append(grads[0])
        line_grads.append(grads[-1])
        pieces = dict(zip(kept, grads[1:-1]))
        if fold > 1:
            pieces = {delta: swap_groups(value, mp_n, delta) for delta, value in pieces.items()}
        for bit in range(top_bit):
            for delta in [d for d in pieces if d >> bit & 1]:
                other = flip_pair(pieces.pop(delta), "mp", bit)
                home = delta ^ 1 << bit
                pieces[home] = (pieces[home].astype(F32) + other.astype(F32)).astype(BF16)
        kept_pairs.append(pieces[0])
        sent_pairs.append(flip_pair(pieces[1 << top_bit], "mp", top_bit))
    line_grad = jnp.concatenate(line_grads, axis=0)[:, :, 1:].reshape(mp_n, heads, -1, SUB)
    line_grad = jnp.einsum(
        "ghcl,lk->ghck", line_grad, lane_flip(F32), precision=lax.Precision.HIGHEST
    )
    tiny = jnp.concatenate(
        [
            line_grad.reshape(mp_n, heads, dp_n, table_part // SUB, SUB)
            .transpose(0, 2, 1, 3, 4)
            .reshape(mp_n, dp_n, bias_rows, SUB)[:, to_held],
            jnp.pad(
                tap_grads.T.reshape(mp_n, dp_n, channel_part, tap_n)[:, to_held],
                (
                    (0, 0),
                    (0, 0),
                    (0, shard_rows - bias_rows - channel_part),
                    (0, SUB - tap_n),
                ),
            ),
        ],
        axis=2,
    ).astype(BF16)
    tiny = tiny.reshape(mp_n, features, SUB)
    smalls = [tiny[g] for g in range(groups)]
    d_first, gain_one, *att_grads = call_kernel(
        functools.partial(project_backward_kernel, groups, halves),
        [((rows, features), F32), (gain[1].shape, F32)] + [((features, 4 * SUB), BF16)] * groups,
        after_first,
        d_second,
        gain[1],
        *att,
        *smalls,
        *d_queries,
        *kept_pairs,
        *sent_pairs[::-1],
    )
    if fold > 1:
        att_grads = ungroup([grad[:, : 3 * SUB] for grad in att_grads], pair_widths, fold)
        att_grads = [jnp.concatenate([g, t], axis=1) for g, t in zip(att_grads, tiny)]
    own_att = scatter_groups(dict(enumerate(att_grads)), order_a)
    d_start, *early_grads = call_kernel(
        functools.partial(ffn_backward_kernel, mp_n),
        [((rows, features), F32)]
        + [((features, part), BF16)] * mp_n
        + [((features, part + SUB), BF16)] * mp_n,
        start,
        d_first,
        gain[0],
        gain_one,
        gain_two,
        gg_last,
        *up_list,
        *down_list,
    )
    up_marks = []
    own_up = scatter_groups(dict(enumerate(early_grads[:mp_n])), order_a, up_marks)
    own_down = scatter_groups(dict(enumerate(early_grads[mp_n:])), order_b)

    def returned(own, away):
        other = flip_pair(away, "dp", 0).astype(own.dtype)
        first = batch == 0
        return jnp.stack([jnp.where(first, own, other), jnp.where(first, other, own)])

    def columns(value, index):
        return value[:, index * head_width : (index + 1) * head_width]

    tail = own_att[:, 3 * head_width :]
    per_channel = tail[bias_rows : bias_rows + channel_part]
    natural = lax.dot_general(
        tied(d_start, up_marks[0][1 << top_bit]), choice.astype(F32), NT, precision=lax.Precision.HIGHEST
    )
    final_rows = mm_nt(final_rows, choice).astype(BF16)
    return (
        returned(final_rows[:block], final_rows[block:]),
        returned(natural[:block], natural[block:].astype(BF16)),
        own_up,
        own_down[:, :part].T,
        jnp.stack([columns(own_att, i) for i in range(3)]),
        columns(own_middle, 0).T,
        tail[:bias_rows].reshape(heads, table_part),
        jnp.stack([columns(own_middle, 1), columns(own_middle, 2)]),
        per_channel[:, :kernel],
        per_channel[:, kernel:tap_n].T,
        columns(own_turn, 0).T,
        own_turn[:, head_width : head_width + part],
        own_turn[:, head_width + part :].T,
        own_down[:, part : part + 5].T,
    )


def solution(mesh):
    placed = (
        P(None, "dp", None),
        P(None, "dp", None),
        P("dp", "mp"),
        P("mp", "dp"),
        P(None, "dp", "mp"),
        P("mp", "dp"),
        P("mp", "dp"),
        P(None, "dp", "mp"),
        P(("mp", "dp"), None),
        P(None, ("mp", "dp")),
        P("mp", "dp"),
        P("dp", "mp"),
        P("mp", "dp"),
        P(None, "dp"),
    )
    returned = (P(None, ("dp", "mp"), None), P(None, ("dp", "mp"), None)) + placed[2:]
    return jax.shard_map(block_step, mesh=mesh, in_specs=placed, out_specs=returned, check_vma=False)
```

```python
import functools

import jax
import jax.numpy as jnp
from jax import lax
from jax.experimental import pallas as pl
from jax.experimental.pallas import tpu as pltpu
from jax.sharding import PartitionSpec as P


EPS = 1e-05
BF16 = jnp.bfloat16
F32 = jnp.float32
SUB = 128
NT = (((1,), (1,)), ((), ()))


def flip_pair(value, axis, bit):
    return lax.ppermute(value, axis, [(i, i ^ 1 << bit) for i in range(lax.axis_size(axis))])


def bits_of(axis):
    return (lax.axis_size(axis) - 1).bit_length()


def own_bit(axis, bit):
    return lax.shift_right_logical(lax.axis_index(axis), bit) & 1


def full_order():
    dp_bits, mp_bits = bits_of("dp"), bits_of("mp")
    dp_high = [("dp", bit) for bit in range(dp_bits - 1, 0, -1)]
    mp_high = [("mp", bit) for bit in range(mp_bits - 1, 0, -1)]
    first = dp_high + [("dp", 0)] + mp_high + [("mp", 0)]
    second = dp_high + mp_high + [("dp", 0)] + [("mp", 0)]
    return (first, second)


def tied(value, other):
    return lax.optimization_barrier((value, other))[0]


def gather_groups(shard, order):
    held = {0: shard}
    for axis, bit in order:
        for delta in list(held):
            own = held[delta]
            other = flip_pair(own, axis, bit)
            if axis == "mp":
                held[delta ^ 1 << bit] = other
            else:
                held[delta] = jnp.concatenate([own, other], axis=0)
    return held


def scatter_groups(parts, order, marks=None):
    parts = dict(parts)
    total = None
    for axis, bit in reversed(order):
        if axis == "mp":
            for delta in [d for d in parts if d >> bit & 1]:
                other = flip_pair(parts.pop(delta), axis, bit)
                home = delta ^ 1 << bit
                parts[home] = (parts[home].astype(F32) + other.astype(F32)).astype(BF16)
        else:
            for delta in parts:
                half = parts[delta].shape[0] // 2
                keep, send = parts[delta][:half], parts[delta][half:]
                other = flip_pair(send, axis, bit)
                total = keep.astype(F32) + other.astype(F32)
                parts[delta] = total.astype(BF16)
        if marks is not None:
            marks.append(dict(parts))
    return total


def reversed_blocks(count):
    bits = (count - 1).bit_length()
    return [int(format(i, "b").zfill(bits)[::-1], 2) if bits else 0 for i in range(count)]


def block_choice(features, count, dtype):
    row = lax.broadcasted_iota(jnp.int32, (features, features), 0)
    col = lax.broadcasted_iota(jnp.int32, (features, features), 1)
    size = features // count
    block, image = col // size, jnp.zeros_like(col)
    for bit in range((count - 1).bit_length()):
        image = image * 2 + (block >> bit & 1)
    image = image ^ lax.axis_index("dp")
    return (row == image * size + col % size).astype(dtype)


def lane_flip(dtype):
    row = lax.broadcasted_iota(jnp.int32, (SUB, SUB), 0)
    col = lax.broadcasted_iota(jnp.int32, (SUB, SUB), 1)
    return (row + col == SUB - 1).astype(dtype)


def regroup(parts, widths, count):
    if count == 1:
        return parts
    joined = []
    for start in range(0, len(parts), count):
        pieces, at = [], 0
        for width in widths:
            pieces += [part[:, at : at + width] for part in parts[start : start + count]]
            at += width
        joined.append(jnp.concatenate(pieces, axis=1))
    return joined


def ungroup(parts, widths, count):
    if count == 1:
        return parts
    split = []
    for part in parts:
        for i in range(count):
            pieces, at = [], 0
            for width in widths:
                pieces.append(part[:, at + i * width : at + (i + 1) * width])
                at += width * count
            split.append(jnp.concatenate(pieces, axis=1))
    return split


def swap_groups(value, groups, delta):
    width = value.shape[-1] // groups
    parts = [value[..., (g ^ delta) * width : ((g ^ delta) + 1) * width] for g in range(groups)]
    return jnp.concatenate(parts, axis=-1)


def absolute_groups(value, groups):
    for bit in range((groups - 1).bit_length()):
        value = jnp.where(own_bit("mp", bit) == 0, value, swap_groups(value, groups, 1 << bit))
    return value


def channel_total(sums):
    groups = lax.axis_size("mp")
    for bit in range(bits_of("mp")):
        sums = sums + swap_groups(flip_pair(sums, "mp", bit), groups, 1 << bit)
    for bit in range(1, bits_of("dp")):
        sums = sums + flip_pair(sums, "dp", bit)
    return sums


def edge_rows(first_rows, last_rows, half_of_slot):
    groups = lax.axis_size("mp")
    place = lax.axis_index("mp")
    up = [(i, (i + 1) % groups) for i in range(groups)]
    down = [(i, (i - 1) % groups) for i in range(groups)]
    before = lax.ppermute(absolute_groups(last_rows, groups), "mp", up)
    after = lax.ppermute(absolute_groups(first_rows, groups), "mp", down)
    before = absolute_groups(before, groups)
    after = absolute_groups(after, groups)
    second = half_of_slot[:, None, None] == 1
    nothing = jnp.zeros_like(before)
    before = jnp.where(place == 0, jnp.where(second, before[::-1], nothing), before)
    after = jnp.where(place == groups - 1, jnp.where(second, nothing, after[::-1]), after)
    return (before, after)


def swish_grad(value):
    logistic = jax.nn.sigmoid(value)
    return logistic * (1.0 + value * (1.0 - logistic))


def normed_of(value):
    centred = value - jnp.mean(value, axis=-1, keepdims=True)
    inverse = lax.rsqrt(jnp.mean(centred * centred, axis=-1, keepdims=True) + EPS)
    return (centred * inverse, inverse)


def norm_back(normed, inverse, gain, upstream):
    scaled = upstream * gain
    inner = (
        scaled
        - jnp.mean(scaled, axis=-1, keepdims=True)
        - normed * jnp.mean(scaled * normed, axis=-1, keepdims=True)
    )
    return (inverse * inner, jnp.sum(upstream * normed, axis=0, keepdims=True))


def mm(left, right):
    return jnp.dot(left, right, preferred_element_type=F32)


def mm_nt(left, right):
    return lax.dot_general(left, right, NT, preferred_element_type=F32)


def call_kernel(kernel, outs, *inputs):
    return pl.pallas_call(
        kernel, out_shape=[jax.ShapeDtypeStruct(shape, dtype) for shape, dtype in outs]
    )(*inputs)


def column_join(refs, index):
    return jnp.concatenate([ref[:, index * SUB : (index + 1) * SUB] for ref in refs], axis=1)


def ffn_forward_kernel(groups, v_ref, gain_ref, *refs):
    ups, downs, out_ref = refs[:groups], refs[groups : 2 * groups], refs[-1]
    value = v_ref[...]
    normed, _ = normed_of(value)
    active = (normed * gain_ref[...]).astype(BF16)
    total = jnp.zeros_like(value)
    for up_ref, down_ref in zip(ups, downs):
        pre = mm(active, up_ref[...])
        hidden = (pre * jax.nn.sigmoid(pre)).astype(BF16)
        total += mm_nt(hidden, down_ref[...])
    out_ref[...] = value + 0.5 * total


def ffn_backward_kernel(groups, v_ref, d_ref, gain_ref, one_ref, two_ref, last_ref, *refs):
    ups, downs = refs[:groups], refs[groups : 2 * groups]
    out_ref = refs[2 * groups]
    gus, gds = refs[2 * groups + 1 : 3 * groups + 1], refs[3 * groups + 1 :]
    part = ups[0].shape[1]
    normed, inverse = normed_of(v_ref[...])
    upstream = d_ref[...]
    active = (normed * gain_ref[...]).astype(BF16)
    error = (0.5 * upstream).astype(BF16)
    active_t = active.T
    error_t = error.T
    total = jnp.zeros_like(upstream)
    for up_ref, down_ref, gu_ref, gd_ref in zip(ups, downs, gus, gds):
        pre = mm(active, up_ref[...])
        logistic = jax.nn.sigmoid(pre)
        hidden = (pre * logistic).astype(BF16)
        gd_ref[:, :part] = mm(error_t, hidden).astype(BF16)
        d_hidden = mm(error, down_ref[...])
        d_pre = (d_hidden * (logistic * (1.0 + pre * (1.0 - logistic)))).astype(BF16)
        gu_ref[...] = mm(active_t, d_pre).astype(BF16)
        total += mm_nt(d_pre, up_ref[...])
    back, grad_gain = norm_back(normed, inverse, gain_ref[...], total)
    out_ref[...] = upstream + back
    known = [grad_gain, one_ref[...], two_ref[...], last_ref[...]]
    count = sum(value.shape[0] for value in known)
    known.append(jnp.zeros((SUB - count, upstream.shape[1]), F32))
    columns = jnp.concatenate(known, axis=0).T.astype(BF16)
    for gd_ref in gds:
        gd_ref[:, part:] = columns


def project_kernel(groups, v_ref, gain_ref, *refs):
    weights, q_ref = refs[:groups], refs[groups]
    pair_refs = refs[groups + 1 :]
    normed, _ = normed_of(v_ref[...])
    active = (normed * gain_ref[...]).astype(BF16)
    q_ref[...] = mm(active, column_join(weights, 0)).astype(BF16)
    width = q_ref.shape[1] // len(pair_refs)
    for i in (0, 1):
        projected = mm(active, column_join(weights, i + 1)).astype(BF16)
        for h, pair_ref in enumerate(pair_refs):
            pair_ref[i] = projected[:, h * width : (h + 1) * width]


def project_backward_kernel(groups, halves, v_ref, d_ref, gain_ref, *refs):
    weights, smalls = refs[:groups], refs[groups : 2 * groups]
    dqs = refs[2 * groups : 2 * groups + halves]
    pairs, tail = refs[2 * groups + halves : -2 - groups], refs[-2 - groups :]
    each = len(pairs) // halves
    out_ref, gg_ref, grads = tail[0], tail[1], tail[2:]
    normed, inverse = normed_of(v_ref[...])
    active_t = (normed * gain_ref[...]).astype(BF16).T
    total = jnp.zeros_like(d_ref[...])
    for i in range(3):
        if i == 0:
            parts = [ref[...] for ref in dqs]
        else:
            parts = [
                sum(ref[i - 1].astype(F32) for ref in pairs[h * each : (h + 1) * each]).astype(BF16)
                for h in range(halves)
            ]
        error = jnp.concatenate(parts, axis=1) if halves > 1 else parts[0]
        total += mm_nt(error, column_join(weights, i))
        grad = mm(active_t, error).astype(BF16)
        for g, grad_ref in enumerate(grads):
            grad_ref[:, i * SUB : (i + 1) * SUB] = grad[:, g * SUB : (g + 1) * SUB]
    for small_ref, grad_ref in zip(smalls, grads):
        grad_ref[:, 3 * SUB :] = small_ref[...]
    back, grad_gain = norm_back(normed, inverse, gain_ref[...], total)
    out_ref[...] = d_ref[...] + back
    gg_ref[...] = grad_gain


def middle_kernel(groups, halves, v_ref, gain_ref, *refs):
    weights, contexts = refs[:groups], refs[groups : groups + halves]
    out_ref, lin_ref, sig_ref, glu_ref = refs[groups + halves :]
    parts = [ref[...] for ref in contexts]
    context = jnp.concatenate(parts, axis=1) if halves > 1 else parts[0]
    value = v_ref[...] + mm_nt(context, column_join(weights, 0))
    out_ref[...] = value
    normed, _ = normed_of(value)
    active = (normed * gain_ref[...]).astype(BF16)
    lin = mm(active, column_join(weights, 1))
    gate = jax.nn.sigmoid(mm(active, column_join(weights, 2)))
    lin_ref[...] = lin
    sig_ref[...] = gate
    glu_ref[...] = (lin * gate).astype(BF16)


def middle_backward_kernel(groups, halves, dglu_ref, lin_ref, sig_ref, v_ref, d_ref, gain_ref, *refs):
    weights, contexts = refs[:groups], refs[groups : groups + halves]
    out_ref, gg_ref, dctx_ref = refs[groups + halves : groups + halves + 3]
    grads = refs[groups + halves + 3 :]
    d_glu, lin, gate = dglu_ref[...], lin_ref[...], sig_ref[...]
    d_lin = (d_glu * gate).astype(BF16)
    d_gate = (d_glu * lin * gate * (1.0 - gate)).astype(BF16)
    normed, inverse = normed_of(v_ref[...])
    active_t = (normed * gain_ref[...]).astype(BF16).T
    total = mm_nt(d_lin, column_join(weights, 1)) + mm_nt(d_gate, column_join(weights, 2))
    back, grad_gain = norm_back(normed, inverse, gain_ref[...], total)
    value = d_ref[...] + back
    out_ref[...] = value
    gg_ref[...] = grad_gain
    error = value.astype(BF16)
    dctx_ref[...] = mm(error, column_join(weights, 0)).astype(BF16)
    parts = [ref[...] for ref in contexts]
    context = jnp.concatenate(parts, axis=1) if halves > 1 else parts[0]
    for i, grad in enumerate((mm(error.T, context), mm(active_t, d_lin), mm(active_t, d_gate))):
        rounded = grad.astype(BF16)
        for g, grad_ref in enumerate(grads):
            grad_ref[:, i * SUB : (i + 1) * SUB] = rounded[:, g * SUB : (g + 1) * SUB]


def turn_kernel(groups, batch_rows, conv_ref, stat_ref, bn_ref, v_ref, up_ref, gains_ref, *refs):
    mids, weights = refs[:groups], refs[groups : 2 * groups]
    final_ref, out_ref, dpre_ref, gg_ref, sums_ref = refs[2 * groups : 2 * groups + 5]
    grads, pres = refs[2 * groups + 5 : -1], refs[-1]
    part = pres.shape[2]
    top, bottom = slice(0, part), slice(part, 2 * part)
    gain_three, gain_four = gains_ref[3:4], gains_ref[4:5]
    mean = stat_ref[0:1] / batch_rows
    white = (conv_ref[...] - mean) * lax.rsqrt(stat_ref[1:2] / batch_rows - mean * mean + EPS)
    bn_pre = bn_ref[0:1] * white + bn_ref[1:2]
    activated = (bn_pre * jax.nn.sigmoid(bn_pre)).astype(BF16)
    outward = column_join(mids, 3)
    third = v_ref[...] + mm_nt(activated, outward)
    normed, inverse = normed_of(third)
    active = (normed * gain_three).astype(BF16)
    total = jnp.zeros_like(third)
    for g, weight in enumerate(weights):
        pre = mm(active, weight[:, top])
        pres[g] = pre
        total += mm_nt((pre * jax.nn.sigmoid(pre)).astype(BF16), weight[:, bottom])
    last_normed, last_inverse = normed_of(third + 0.5 * total)
    final_ref[...] = (last_normed * gain_four).astype(BF16)
    fourth, grad_four = norm_back(last_normed, last_inverse, gain_four, up_ref[...])
    error = (0.5 * fourth).astype(BF16)
    active_t = active.T
    error_t = error.T
    total = jnp.zeros_like(third)
    for g, (weight, grad_ref) in enumerate(zip(weights, grads)):
        pre = pres[g]
        logistic = jax.nn.sigmoid(pre)
        hidden = (pre * logistic).astype(BF16)
        grad_ref[:, SUB + part :] = mm(error_t, hidden).astype(BF16)
        d_hidden = mm(error, weight[:, bottom])
        d_pre = (d_hidden * (logistic * (1.0 + pre * (1.0 - logistic)))).astype(BF16)
        grad_ref[:, SUB : SUB + part] = mm(active_t, d_pre).astype(BF16)
        total += mm_nt(d_pre, weight[:, top])
    back, grad_three = norm_back(normed, inverse, gain_three, total)
    value = fourth + back
    out_ref[...] = value
    gg_ref[0:1] = grad_three
    gg_ref[1:2] = grad_four
    error = value.astype(BF16)
    grad = mm(error.T, activated).astype(BF16)
    for g, grad_ref in enumerate(grads):
        grad_ref[:, :SUB] = grad[:, g * SUB : (g + 1) * SUB]
    d_pre = mm(error, outward) * swish_grad(bn_pre)
    dpre_ref[...] = d_pre
    sums_ref[0:1] = jnp.sum(d_pre, axis=0, keepdims=True)
    sums_ref[1:2] = jnp.sum(d_pre * white, axis=0, keepdims=True)


def build_skew(line_ref, skew, heads, chunks):
    for h in range(heads):
        for c in range(chunks):
            window = jnp.concatenate(
                [line_ref[0, h, c + 1 : c + 2, :], line_ref[0, h, c : c + 1, :]], axis=1
            )
            window = jnp.broadcast_to(window, (SUB, 2 * SUB))
            rolled = pltpu.roll(window, 1, 1, stride=1, stride_axis=0)
            skew[h, SUB * c : SUB * (c + 1), :] = rolled[:, SUB:]


def stack_heads(rows, heads, factor):
    lane = lax.broadcasted_iota(jnp.int32, rows.shape, 1)
    size = rows.shape[1] // heads
    return jnp.concatenate(
        [
            rows * jnp.where((lane >= h * size) & (lane < (h + 1) * size), factor, 0.0).astype(BF16)
            for h in range(heads)
        ],
        axis=0,
    )


def diagonal_heads(value, heads):
    size, columns = value.shape[0] // heads, value.shape[1] // heads
    parts = [
        value[h * size : (h + 1) * size, h * columns : (h + 1) * columns] for h in range(heads)
    ]
    return jnp.concatenate(parts, axis=0)


def tile_bias(skew, columns, block, offset_of):
    parts = [
        skew[h, pl.ds(pl.multiple_of(offset_of(qb), SUB), block), :] for h, qb in columns
    ]
    return jnp.concatenate(parts, axis=1)


def column_tiles(heads, steps):
    columns = [(h, qb) for h in range(heads) for qb in range(steps)]
    return [columns[i : i + 2] for i in range(0, len(columns), 2)]


def attend_forward_kernel(pieces, heads, qpos, kpos, q_ref, line_ref, *refs):
    k_refs = refs[:pieces]
    v_refs = refs[pieces : 2 * pieces]
    ctx_ref, lse_ref, ctx32_ref, skew, query, scores, probs, v_t = refs[2 * pieces :]
    rows, width = q_ref.shape
    block = rows // 2
    chunks = skew.shape[1] // SUB
    middle = skew.shape[1] // 2
    tiles = column_tiles(heads, rows // SUB)
    span = 2 * SUB
    build_skew(line_ref, skew, heads, chunks)
    for p in range(pieces):
        v_t[:width, p * rows : (p + 1) * rows] = v_refs[p][0].T
    v_t[width:, :] = jnp.ones_like(v_t[width:, :])
    query[...] = stack_heads(q_ref[...], heads, (width // heads) ** (-0.5))
    tops = [jnp.full((8, span), -jnp.inf, F32) for _ in tiles]
    for c in range(2 * pieces):
        keys = k_refs[c // 2][0, (c % 2) * block : (c % 2 + 1) * block, :]
        for t, tile in enumerate(tiles):
            raw = mm_nt(keys, query[t * span : (t + 1) * span, :])
            raw = raw + tile_bias(skew, tile, block, lambda qb: kpos[c] - qpos[qb] + middle)
            scores[c * block : (c + 1) * block, t * span : (t + 1) * span] = raw
            tops[t] = jnp.maximum(tops[t], jnp.max(raw.reshape(block // 8, 8, span), axis=0))
    tops = [jnp.max(top, axis=0, keepdims=True) for top in tops]
    for c in range(2 * pieces):
        for t in range(len(tiles)):
            part = (slice(c * block, (c + 1) * block), slice(t * span, (t + 1) * span))
            probs[part] = jnp.exp(scores[part] - tops[t]).astype(BF16)
    out_t = mm(v_t[...], probs[...])
    total = out_t[width : width + 1, :]
    out_t = out_t[:width, :] / total
    out = diagonal_heads(out_t, heads).T
    ctx_ref[...] = out.astype(BF16)
    ctx32_ref[...] = out
    lse_ref[0] = jnp.concatenate(tops, axis=1) + jnp.log(total)


def attend_backward_kernel(pieces, heads, qpos, kpos, q_ref, d_ref, ctx_ref, lse_ref, line_ref, *refs):
    k_refs = refs[:pieces]
    v_refs = refs[pieces : 2 * pieces]
    dq_ref = refs[2 * pieces]
    dkv_refs = refs[2 * pieces + 1 : 3 * pieces + 1]
    line_grad, skew, skew_grad, query, error, probs, d_scores, k_t = refs[3 * pieces + 1 :]
    rows, width = q_ref.shape
    block = rows // 2
    chunks = skew.shape[1] // SUB
    middle = skew.shape[1] // 2
    scale = (width // heads) ** (-0.5)
    size = width // heads
    tiles = column_tiles(heads, rows // SUB)
    span = 2 * SUB
    build_skew(line_ref, skew, heads, chunks)
    skew_grad[...] = jnp.zeros_like(skew_grad)
    for p in range(pieces):
        k_t[:, p * rows : (p + 1) * rows] = k_refs[p][0].T
    query[...] = stack_heads(q_ref[...], heads, scale)
    error[...] = stack_heads(d_ref[...], heads, 1.0)
    weighed = (d_ref[...].astype(F32) * ctx_ref[...]).T
    dot_sum = jnp.concatenate(
        [jnp.sum(weighed[h * size : (h + 1) * size], axis=0, keepdims=True) for h in range(heads)],
        axis=1,
    )
    lse = lse_ref[0]
    for c in range(2 * pieces):
        part = slice((c % 2) * block, (c % 2 + 1) * block)
        here = slice(c * block, (c + 1) * block)
        keys = k_refs[c // 2][0, part, :]
        values = v_refs[c // 2][0, part, :]
        for t, tile in enumerate(tiles):
            cols = slice(t * span, (t + 1) * span)
            raw = mm_nt(keys, query[cols, :])
            bias = tile_bias(skew, tile, block, lambda qb: kpos[c] - qpos[qb] + middle)
            prob = jnp.exp(raw + bias - lse[:, cols])
            d_score = prob * (mm_nt(values, error[cols, :]) - dot_sum[:, cols])
            probs[c % 2, :, cols] = prob.astype(BF16)
            d_scores[here, cols] = d_score.astype(BF16)
            for i, (h, qb) in enumerate(tile):
                offset = pl.multiple_of(kpos[c] - qpos[qb] + middle, SUB)
                skew_grad[h, pl.ds(offset, block), :] += d_score[:, i * SUB : (i + 1) * SUB]
        dkv_refs[c // 2][0, part, :] = mm(d_scores[here, :], query[...]).astype(BF16)
        dkv_refs[c // 2][1, part, :] = mm(probs[c % 2], error[...]).astype(BF16)
    dq_t = mm(k_t[...], d_scores[...])
    dq_ref[...] = (diagonal_heads(dq_t, heads).T * scale).astype(BF16)
    line_grad[...] = jnp.zeros_like(line_grad)
    for h in range(heads):
        for c in range(chunks):
            block_grad = skew_grad[h, SUB * c : SUB * (c + 1), :]
            value = jnp.concatenate([jnp.zeros_like(block_grad), block_grad], axis=1)
            half = SUB // 2
            while half >= 1:
                value = value[:half] + pltpu.roll(value[half:], 2 * SUB - half, 1)
                half //= 2
            value = pltpu.roll(value, 2 * SUB - 1, 1)
            line_grad[0, h, c + 1 : c + 2, :] += value[:, :SUB]
            line_grad[0, h, c : c + 1, :] += value[:, SUB:]


def attention_specs(rows, first, pieces, shifts, line_shape):
    whole_q = pl.BlockSpec((rows, SUB), lambda j, *_: (0, j + first))
    own = pl.BlockSpec((rows, SUB), lambda j, *_: (0, j))
    line = pl.BlockSpec((1,) + line_shape[1:], lambda j, *_: (j + first, 0, 0, 0))
    keys, values = [], []
    for p in range(pieces):
        keys.append(pl.BlockSpec((1, rows, SUB), lambda j, *_, d=shifts[p]: (0, 0, j ^ d)))
        values.append(pl.BlockSpec((1, rows, SUB), lambda j, *_, d=shifts[p]: (1, 0, j ^ d)))
    return (whole_q, own, line, keys, values)


def attend_forward(query, pairs, shifts, line, first, qpos, kpos):
    rows = query.shape[0]
    heads = line.shape[1]
    groups = pairs[0].shape[2] // SUB
    pieces = len(pairs)
    table = (line.shape[2] - 1) * SUB
    whole_q, own, line_spec, keys, values = attention_specs(rows, first, pieces, shifts, line.shape)
    return pl.pallas_call(
        functools.partial(attend_forward_kernel, pieces, heads),
        out_shape=(
            jax.ShapeDtypeStruct((rows, groups * SUB), BF16),
            jax.ShapeDtypeStruct((groups, 1, heads * rows), F32),
            jax.ShapeDtypeStruct((rows, groups * SUB), F32),
        ),
        grid_spec=pltpu.PrefetchScalarGridSpec(
            num_scalar_prefetch=2,
            grid=(groups,),
            in_specs=[whole_q, line_spec] + keys + values,
            out_specs=(
                own,
                pl.BlockSpec((1, 1, heads * rows), lambda j, *_: (j, 0, 0)),
                own,
            ),
            scratch_shapes=[
                pltpu.VMEM((heads, table, SUB), F32),
                pltpu.VMEM((heads * rows, SUB), BF16),
                pltpu.VMEM((pieces * rows, heads * rows), F32),
                pltpu.VMEM((pieces * rows, heads * rows), BF16),
                pltpu.VMEM((SUB + 16, pieces * rows), BF16),
            ],
        ),
        name="attend_forward",
    )(qpos, kpos, query, line, *pairs, *pairs)


def attend_backward(query, d_context, lse, context, pairs, shifts, line, first, qpos, kpos):
    rows = query.shape[0]
    heads = line.shape[1]
    groups = pairs[0].shape[2] // SUB
    pieces = len(pairs)
    table = (line.shape[2] - 1) * SUB
    whole_q, own, line_spec, keys, values = attention_specs(rows, first, pieces, shifts, line.shape)
    lse_spec = pl.BlockSpec((1, 1, heads * rows), lambda j, *_: (j, 0, 0))
    pair_specs = [
        pl.BlockSpec((2, rows, SUB), lambda j, *_, d=shifts[p]: (0, 0, j ^ d))
        for p in range(pieces)
    ]
    return pl.pallas_call(
        functools.partial(attend_backward_kernel, pieces, heads),
        out_shape=(
            (jax.ShapeDtypeStruct((rows, groups * SUB), BF16),)
            + tuple(jax.ShapeDtypeStruct(pairs[0].shape, BF16) for _ in range(pieces))
            + (jax.ShapeDtypeStruct((groups,) + line.shape[1:], F32),)
        ),
        grid_spec=pltpu.PrefetchScalarGridSpec(
            num_scalar_prefetch=2,
            grid=(groups,),
            in_specs=[whole_q, whole_q, own, lse_spec, line_spec] + keys + values,
            out_specs=(
                (own,)
                + tuple(pair_specs)
                + (pl.BlockSpec((1,) + line.shape[1:], lambda j, *_: (j, 0, 0, 0)),)
            ),
            scratch_shapes=[
                pltpu.VMEM((heads, table, SUB), F32),
                pltpu.VMEM((heads, table, SUB), F32),
                pltpu.VMEM((heads * rows, SUB), BF16),
                pltpu.VMEM((heads * rows, SUB), BF16),
                pltpu.VMEM((2, rows // 2, heads * rows), BF16),
                pltpu.VMEM((pieces * rows, heads * rows), BF16),
                pltpu.VMEM((SUB, pieces * rows), BF16),
            ],
        ),
        name="attend_backward",
    )(qpos, kpos, query, d_context, context, lse, line, *pairs, *pairs)


def block_step(
    block_input,
    out_cotangent,
    early_up,
    early_down,
    attention_in,
    attention_out,
    relative_bias,
    pointwise_in,
    depthwise,
    batch_norm,
    pointwise_out,
    late_up,
    late_down,
    norm_gains,
):
    dp_n, mp_n = lax.axis_size("dp"), lax.axis_size("mp")
    held_rows, features = block_input.shape[1:]
    block = held_rows // mp_n
    rows = 2 * block
    batch_rows = held_rows * dp_n
    batch = lax.axis_index("dp") % 2
    place = lax.axis_index("mp")
    shard_rows, part = early_up.shape
    heads, table_part = relative_bias.shape
    channel_part, kernel = depthwise.shape
    head_width = attention_out.shape[0]
    channels = mp_n * head_width
    margin = (kernel - 1) // 2
    order_a, order_b = full_order()
    fold = max(1, SUB // head_width)
    groups = mp_n // fold
    blocks = jnp.array(reversed_blocks(dp_n), jnp.int32)
    to_natural = blocks[jnp.arange(dp_n, dtype=jnp.int32) ^ lax.axis_index("dp")]
    to_held = blocks ^ lax.axis_index("dp")
    choice = block_choice(features, dp_n, BF16)

    def exchanged(value):
        mine = lax.dynamic_slice_in_dim(value, place * block, block, 1)
        own = lax.dynamic_index_in_dim(mine, batch, 0, keepdims=False)
        away = lax.dynamic_index_in_dim(mine, 1 - batch, 0, keepdims=False)
        other = flip_pair(away, "dp", 0)
        return mm(jnp.concatenate([own, other], axis=0), choice)

    def listed(parts, widths):
        return regroup([parts[delta] for delta in range(mp_n)], widths, fold)

    def unlisted(parts, widths):
        return dict(enumerate(ungroup(list(parts), widths, fold)))

    bias_rows = heads * table_part // SUB
    tap_n = kernel + 2
    gain_row = bias_rows + channel_part
    small_rows = gain_row + norm_gains.shape[0]
    small = jnp.concatenate(
        [
            relative_bias.reshape(bias_rows, SUB),
            jnp.pad(jnp.concatenate([depthwise, batch_norm.T], axis=1), ((0, 0), (0, SUB - tap_n))),
            jnp.pad(norm_gains, ((0, shard_rows - small_rows), (0, SUB - shard_rows))),
        ],
        axis=0,
    )
    early_u = gather_groups(early_up, order_a)
    early_d = gather_groups(early_down.T, order_b)
    start = exchanged(block_input)
    pair_widths = [head_width] * 3
    att_shard = jnp.concatenate([attention_in[0], attention_in[1], attention_in[2], small], axis=1)
    att_held = gather_groups(att_shard, order_a)
    mid_shard = jnp.concatenate(
        [attention_out.T, pointwise_in[0], pointwise_in[1], pointwise_out.T], axis=1
    )
    late_shard = jnp.concatenate([late_up, late_down.T], axis=1)
    mid = listed(gather_groups(mid_shard, order_b), [head_width] * 4)
    late = listed(gather_groups(late_shard, order_a), [part] * 2)
    if fold == 1:
        att = [att_held[delta] for delta in range(mp_n)]
    else:
        att = listed({d: value[:, : 3 * head_width] for d, value in att_held.items()}, pair_widths)
    gains = (
        att_held[0]
        .reshape(dp_n, shard_rows, -1)[:, gain_row:small_rows, 3 * head_width : 3 * head_width + shard_rows]
        .transpose(1, 0, 2)
        .reshape(5, features)
        .astype(F32)
    )
    gain = [gains[i : i + 1] for i in range(5)]
    tiny = jnp.stack([att_held[delta][:, 3 * head_width :] for delta in range(mp_n)])
    tiny = tiny.reshape(mp_n, dp_n, shard_rows, SUB)[:, to_natural]
    line = (
        tiny[:, :, :bias_rows]
        .reshape(mp_n, dp_n, heads, table_part // SUB, SUB)
        .transpose(0, 2, 1, 3, 4)
        .reshape(mp_n, heads, dp_n * table_part // SUB, SUB)
    )
    line = jnp.einsum("ghcl,lk->ghck", line, lane_flip(BF16), preferred_element_type=F32)
    line = jnp.pad(line, ((0, 0), (0, 0), (1, 0), (0, 0)))
    line = line.reshape(groups, heads * fold, line.shape[2], SUB)
    taps = (
        tiny[:, :, bias_rows : bias_rows + channel_part, :tap_n].reshape(channels, tap_n).T.astype(F32)
    )

    half_of_slot = jnp.stack([batch, 1 - batch]).astype(jnp.int32)
    kept = [0]
    for bit in range(bits_of("mp") - 1, -1, -1):
        kept = kept + [delta ^ 1 << bit for delta in kept]
    qpos = (
        half_of_slot[:, None] * held_rows
        + place * block
        + SUB * jnp.arange(block // SUB, dtype=jnp.int32)[None, :]
    ).reshape(-1)
    kpos = jnp.stack(
        [half_of_slot[r] * held_rows + (place ^ delta) * block for delta in kept for r in (0, 1)]
    )
    wide = (rows, channels)
    halves = 2 if fold == 1 and mp_n >= 4 else 1
    local = groups // halves
    up_list = [early_u[delta] for delta in range(mp_n)]
    down_list = [early_d[delta] for delta in range(mp_n)]
    (after_first,) = call_kernel(
        functools.partial(ffn_forward_kernel, mp_n),
        [((rows, features), F32)],
        start,
        gain[0],
        *up_list,
        *down_list,
    )
    query, *pair_halves = call_kernel(
        functools.partial(project_kernel, groups),
        [(wide, BF16)] + [((2, rows, local * SUB), BF16)] * halves,
        after_first,
        gain[1],
        *att,
    )
    top_bit = bits_of("mp") - 1
    held_pairs = []
    for h in range(halves):
        pieces = [pair_halves[h]]
        away = pair_halves[halves - 1 - h]
        if h > 0:
            away = tied(away, held_pairs[h - 1][1])
        pieces.append(flip_pair(away, "mp", top_bit))
        for bit in range(top_bit - 1, -1, -1):
            pieces = pieces + [flip_pair(piece, "mp", bit) for piece in pieces]
        if fold > 1:
            pieces = [swap_groups(piece, mp_n, delta) for piece, delta in zip(pieces, kept)]
        held_pairs.append(pieces)
    shifts = [delta & (local - 1) if fold == 1 else 0 for delta in kept]
    attended = []
    for h in range(halves):
        attended.append(attend_forward(query, held_pairs[h], shifts, line, h * local, qpos, kpos))
    contexts = [item[0] for item in attended]
    after_second, lin, gate_sig, glu = call_kernel(
        functools.partial(middle_kernel, groups, halves),
        [((rows, features), F32), (wide, F32), (wide, F32), (wide, BF16)],
        after_first,
        gain[2],
        *mid,
        *contexts,
    )
    cotangent = exchanged(out_cotangent)
    glu = tied(glu, cotangent).reshape(2, block, channels)
    edge = margin + 1
    before, after = edge_rows(glu[:, :edge], glu[:, block - edge :], half_of_slot)
    extended = jnp.concatenate([before[:, 1:], glu, after[:, :margin]], axis=1).astype(F32)
    conv = jnp.zeros((2, block, channels), F32)
    for tap in range(kernel):
        conv = conv + taps[tap] * extended[:, tap : tap + block]
    conv = conv.reshape(rows, channels)
    sums = channel_total(jnp.stack([jnp.sum(conv, axis=0), jnp.sum(conv * conv, axis=0)]))
    bmean = sums[0:1] / batch_rows
    binv = lax.rsqrt(sums[1:2] / batch_rows - bmean * bmean + EPS)
    bn_rows = taps[kernel:]

    wide_part = part * fold
    turn_widths = [head_width, part, part]
    final_rows, d_third, d_pre, gg_last, local_sums, *turn_grads = pl.pallas_call(
        functools.partial(turn_kernel, groups, batch_rows),
        out_shape=[
            jax.ShapeDtypeStruct((rows, features), BF16),
            jax.ShapeDtypeStruct((rows, features), F32),
            jax.ShapeDtypeStruct(wide, F32),
            jax.ShapeDtypeStruct((2, features), F32),
            jax.ShapeDtypeStruct((2, channels), F32),
        ]
        + [jax.ShapeDtypeStruct((features, SUB + 2 * wide_part), BF16)] * groups,
        scratch_shapes=[pltpu.VMEM((groups, rows, wide_part), F32)],
        name="turn",
    )(conv, sums, bn_rows, after_second, cotangent, gains, *mid, *late)
    turn_marks = []
    own_turn = scatter_groups(unlisted(turn_grads, turn_widths), order_a, turn_marks)

    sums = channel_total(local_sums)
    white = (conv - bmean) * binv
    d_conv = (
        binv * bn_rows[0:1] * (d_pre - sums[0:1] / batch_rows - white * sums[1:2] / batch_rows)
    ).reshape(2, block, channels)
    before, after = edge_rows(d_conv[:, :edge], d_conv[:, block - edge :], half_of_slot)
    d_extended = jnp.concatenate([before[:, 1:], d_conv, after[:, :margin]], axis=1)
    d_glu = jnp.zeros((2, block, channels), F32)
    tap_grads = []
    for tap in range(kernel):
        d_glu = d_glu + taps[tap] * d_extended[:, kernel - 1 - tap : kernel - 1 - tap + block]
        tap_grads.append(jnp.sum(extended[:, tap : tap + block] * d_conv, axis=(0, 1)))
    tap_grads = jnp.stack(tap_grads + [local_sums[1], local_sums[0]])
    d_second, gain_two, d_context, *middle_grads = call_kernel(
        functools.partial(middle_backward_kernel, groups, halves),
        [((rows, features), F32), (gain[2].shape, F32), (wide, BF16)]
        + [((features, 3 * SUB), BF16)] * groups,
        tied(d_glu.reshape(rows, channels), turn_marks[0][1 << top_bit]),
        lin,
        gate_sig,
        after_second,
        d_third,
        gain[2],
        *mid,
        *contexts,
    )
    own_middle = scatter_groups(unlisted(middle_grads, pair_widths), order_b)
    d_queries, kept_pairs, sent_pairs, line_grads = [], [], [], []
    for h in range(halves):
        grads = attend_backward(
            query, d_context, attended[h][1], attended[h][2], held_pairs[h], shifts, line,
            h * local, qpos, kpos,
        )
        d_queries.append(grads[0])
        line_grads.append(grads[-1])
        pieces = dict(zip(kept, grads[1:-1]))
        if fold > 1:
            pieces = {delta: swap_groups(value, mp_n, delta) for delta, value in pieces.items()}
        kept_pairs.append([pieces[0]])
        for bit in range(top_bit):
            for delta in [d for d in pieces if d >> bit & 1]:
                other = flip_pair(pieces.pop(delta), "mp", bit)
                home = delta ^ 1 << bit
                if home == 0:
                    kept_pairs[h].append(other)
                else:
                    pieces[home] = (pieces[home].astype(F32) + other.astype(F32)).astype(BF16)
        sent_pairs.append(flip_pair(pieces[1 << top_bit], "mp", top_bit))
    line_grad = jnp.concatenate(line_grads, axis=0)[:, :, 1:].reshape(mp_n, heads, -1, SUB)
    line_grad = jnp.einsum(
        "ghcl,lk->ghck", line_grad, lane_flip(F32), precision=lax.Precision.HIGHEST
    )
    tiny = jnp.concatenate(
        [
            line_grad.reshape(mp_n, heads, dp_n, table_part // SUB, SUB)
            .transpose(0, 2, 1, 3, 4)
            .reshape(mp_n, dp_n, bias_rows, SUB)[:, to_held],
            jnp.pad(
                tap_grads.T.reshape(mp_n, dp_n, channel_part, tap_n)[:, to_held],
                (
                    (0, 0),
                    (0, 0),
                    (0, shard_rows - bias_rows - channel_part),
                    (0, SUB - tap_n),
                ),
            ),
        ],
        axis=2,
    ).astype(BF16)
    tiny = tiny.reshape(mp_n, features, SUB)
    smalls = [tiny[g] for g in range(groups)]
    d_first, gain_one, *att_grads = call_kernel(
        functools.partial(project_backward_kernel, groups, halves),
        [((rows, features), F32), (gain[1].shape, F32)] + [((features, 4 * SUB), BF16)] * groups,
        after_first,
        d_second,
        gain[1],
        *att,
        *smalls,
        *d_queries,
        *[
            part
            for h in range(halves)
            for part in kept_pairs[h] + [sent_pairs[halves - 1 - h]]
        ],
    )
    if fold > 1:
        att_grads = ungroup([grad[:, : 3 * SUB] for grad in att_grads], pair_widths, fold)
        att_grads = [jnp.concatenate([g, t], axis=1) for g, t in zip(att_grads, tiny)]
    own_att = scatter_groups(dict(enumerate(att_grads)), order_a)
    d_start, *early_grads = call_kernel(
        functools.partial(ffn_backward_kernel, mp_n),
        [((rows, features), F32)]
        + [((features, part), BF16)] * mp_n
        + [((features, part + SUB), BF16)] * mp_n,
        start,
        d_first,
        gain[0],
        gain_one,
        gain_two,
        gg_last,
        *up_list,
        *down_list,
    )
    up_marks = []
    own_up = scatter_groups(dict(enumerate(early_grads[:mp_n])), order_a, up_marks)
    own_down = scatter_groups(dict(enumerate(early_grads[mp_n:])), order_b)

    def returned(own, away):
        other = flip_pair(away, "dp", 0).astype(own.dtype)
        first = batch == 0
        return jnp.stack([jnp.where(first, own, other), jnp.where(first, other, own)])

    def columns(value, index):
        return value[:, index * head_width : (index + 1) * head_width]

    tail = own_att[:, 3 * head_width :]
    per_channel = tail[bias_rows : bias_rows + channel_part]
    natural = lax.dot_general(
        tied(d_start, up_marks[0][1 << top_bit]), choice.astype(F32), NT, precision=lax.Precision.HIGHEST
    )
    final_rows = mm_nt(final_rows, choice).astype(BF16)
    return (
        returned(final_rows[:block], final_rows[block:]),
        returned(natural[:block], natural[block:].astype(BF16)),
        own_up,
        own_down[:, :part].T,
        jnp.stack([columns(own_att, i) for i in range(3)]),
        columns(own_middle, 0).T,
        tail[:bias_rows].reshape(heads, table_part),
        jnp.stack([columns(own_middle, 1), columns(own_middle, 2)]),
        per_channel[:, :kernel],
        per_channel[:, kernel:tap_n].T,
        columns(own_turn, 0).T,
        own_turn[:, head_width : head_width + part],
        own_turn[:, head_width + part :].T,
        own_down[:, part : part + 5].T,
    )


def solution(mesh):
    placed = (
        P(None, "dp", None),
        P(None, "dp", None),
        P("dp", "mp"),
        P("mp", "dp"),
        P(None, "dp", "mp"),
        P("mp", "dp"),
        P("mp", "dp"),
        P(None, "dp", "mp"),
        P(("mp", "dp"), None),
        P(None, ("mp", "dp")),
        P("mp", "dp"),
        P("dp", "mp"),
        P("mp", "dp"),
        P(None, "dp"),
    )
    returned = (P(None, ("dp", "mp"), None), P(None, ("dp", "mp"), None)) + placed[2:]
    return jax.shard_map(block_step, mesh=mesh, in_specs=placed, out_specs=returned, check_vma=False)
```

```python
import functools

import jax
import jax.numpy as jnp
from jax import lax
from jax.experimental import pallas as pl
from jax.experimental.pallas import tpu as pltpu
from jax.sharding import PartitionSpec as P


EPS = 1e-05
BF16 = jnp.bfloat16
F32 = jnp.float32
SUB = 128
NT = (((1,), (1,)), ((), ()))


def flip_pair(value, axis, bit):
    return lax.ppermute(value, axis, [(i, i ^ 1 << bit) for i in range(lax.axis_size(axis))])


def bits_of(axis):
    return (lax.axis_size(axis) - 1).bit_length()


def own_bit(axis, bit):
    return lax.shift_right_logical(lax.axis_index(axis), bit) & 1


def full_order():
    dp_bits, mp_bits = bits_of("dp"), bits_of("mp")
    dp_high = [("dp", bit) for bit in range(dp_bits - 1, 0, -1)]
    mp_high = [("mp", bit) for bit in range(mp_bits - 1, 0, -1)]
    first = dp_high + [("dp", 0)] + mp_high + [("mp", 0)]
    second = dp_high + mp_high + [("dp", 0)] + [("mp", 0)]
    return (first, second)


def tied(value, other):
    return lax.optimization_barrier((value, other))[0]


def gather_groups(shard, order):
    held = {0: shard}
    for axis, bit in order:
        for delta in list(held):
            own = held[delta]
            other = flip_pair(own, axis, bit)
            if axis == "mp":
                held[delta ^ 1 << bit] = other
            else:
                held[delta] = jnp.concatenate([own, other], axis=0)
    return held


def scatter_groups(parts, order, marks=None):
    parts = dict(parts)
    total = None
    for axis, bit in reversed(order):
        if axis == "mp":
            for delta in [d for d in parts if d >> bit & 1]:
                other = flip_pair(parts.pop(delta), axis, bit)
                home = delta ^ 1 << bit
                parts[home] = (parts[home].astype(F32) + other.astype(F32)).astype(BF16)
        else:
            for delta in parts:
                half = parts[delta].shape[0] // 2
                keep, send = parts[delta][:half], parts[delta][half:]
                other = flip_pair(send, axis, bit)
                total = keep.astype(F32) + other.astype(F32)
                parts[delta] = total.astype(BF16)
        if marks is not None:
            marks.append(dict(parts))
    return total


def reversed_blocks(count):
    bits = (count - 1).bit_length()
    return [int(format(i, "b").zfill(bits)[::-1], 2) if bits else 0 for i in range(count)]


def block_choice(features, count, dtype):
    row = lax.broadcasted_iota(jnp.int32, (features, features), 0)
    col = lax.broadcasted_iota(jnp.int32, (features, features), 1)
    size = features // count
    block, image = col // size, jnp.zeros_like(col)
    for bit in range((count - 1).bit_length()):
        image = image * 2 + (block >> bit & 1)
    image = image ^ lax.axis_index("dp")
    return (row == image * size + col % size).astype(dtype)


def lane_flip(dtype):
    row = lax.broadcasted_iota(jnp.int32, (SUB, SUB), 0)
    col = lax.broadcasted_iota(jnp.int32, (SUB, SUB), 1)
    return (row + col == SUB - 1).astype(dtype)


def regroup(parts, widths, count):
    if count == 1:
        return parts
    joined = []
    for start in range(0, len(parts), count):
        pieces, at = [], 0
        for width in widths:
            pieces += [part[:, at : at + width] for part in parts[start : start + count]]
            at += width
        joined.append(jnp.concatenate(pieces, axis=1))
    return joined


def ungroup(parts, widths, count):
    if count == 1:
        return parts
    split = []
    for part in parts:
        for i in range(count):
            pieces, at = [], 0
            for width in widths:
                pieces.append(part[:, at + i * width : at + (i + 1) * width])
                at += width * count
            split.append(jnp.concatenate(pieces, axis=1))
    return split


def swap_groups(value, groups, delta):
    width = value.shape[-1] // groups
    parts = [value[..., (g ^ delta) * width : ((g ^ delta) + 1) * width] for g in range(groups)]
    return jnp.concatenate(parts, axis=-1)


def absolute_groups(value, groups):
    for bit in range((groups - 1).bit_length()):
        value = jnp.where(own_bit("mp", bit) == 0, value, swap_groups(value, groups, 1 << bit))
    return value


def channel_total(sums):
    groups = lax.axis_size("mp")
    for bit in range(bits_of("mp")):
        sums = sums + swap_groups(flip_pair(sums, "mp", bit), groups, 1 << bit)
    for bit in range(1, bits_of("dp")):
        sums = sums + flip_pair(sums, "dp", bit)
    return sums


def edge_rows(first_rows, last_rows, half_of_slot):
    groups = lax.axis_size("mp")
    place = lax.axis_index("mp")
    up = [(i, (i + 1) % groups) for i in range(groups)]
    down = [(i, (i - 1) % groups) for i in range(groups)]
    before = lax.ppermute(absolute_groups(last_rows, groups), "mp", up)
    after = lax.ppermute(absolute_groups(first_rows, groups), "mp", down)
    before = absolute_groups(before, groups)
    after = absolute_groups(after, groups)
    second = half_of_slot[:, None, None] == 1
    nothing = jnp.zeros_like(before)
    before = jnp.where(place == 0, jnp.where(second, before[::-1], nothing), before)
    after = jnp.where(place == groups - 1, jnp.where(second, nothing, after[::-1]), after)
    return (before, after)


def swish_grad(value):
    logistic = jax.nn.sigmoid(value)
    return logistic * (1.0 + value * (1.0 - logistic))


def normed_of(value):
    centred = value - jnp.mean(value, axis=-1, keepdims=True)
    inverse = lax.rsqrt(jnp.mean(centred * centred, axis=-1, keepdims=True) + EPS)
    return (centred * inverse, inverse)


def norm_back(normed, inverse, gain, upstream):
    scaled = upstream * gain
    inner = (
        scaled
        - jnp.mean(scaled, axis=-1, keepdims=True)
        - normed * jnp.mean(scaled * normed, axis=-1, keepdims=True)
    )
    return (inverse * inner, jnp.sum(upstream * normed, axis=0, keepdims=True))


def mm(left, right):
    return jnp.dot(left, right, preferred_element_type=F32)


def mm_nt(left, right):
    return lax.dot_general(left, right, NT, preferred_element_type=F32)


def call_kernel(kernel, outs, *inputs):
    return pl.pallas_call(
        kernel, out_shape=[jax.ShapeDtypeStruct(shape, dtype) for shape, dtype in outs]
    )(*inputs)


def column_join(refs, index):
    return jnp.concatenate([ref[:, index * SUB : (index + 1) * SUB] for ref in refs], axis=1)


def ffn_forward_kernel(groups, v_ref, gain_ref, *refs):
    ups, downs, out_ref = refs[:groups], refs[groups : 2 * groups], refs[-1]
    value = v_ref[...]
    normed, _ = normed_of(value)
    active = (normed * gain_ref[...]).astype(BF16)
    total = jnp.zeros_like(value)
    for up_ref, down_ref in zip(ups, downs):
        pre = mm(active, up_ref[...])
        hidden = (pre * jax.nn.sigmoid(pre)).astype(BF16)
        total += mm_nt(hidden, down_ref[...])
    out_ref[...] = value + 0.5 * total


def ffn_backward_kernel(groups, v_ref, d_ref, gain_ref, one_ref, two_ref, last_ref, *refs):
    ups, downs = refs[:groups], refs[groups : 2 * groups]
    out_ref = refs[2 * groups]
    gus, gds = refs[2 * groups + 1 : 3 * groups + 1], refs[3 * groups + 1 :]
    part = ups[0].shape[1]
    normed, inverse = normed_of(v_ref[...])
    upstream = d_ref[...]
    active = (normed * gain_ref[...]).astype(BF16)
    error = (0.5 * upstream).astype(BF16)
    active_t = active.T
    error_t = error.T
    total = jnp.zeros_like(upstream)
    for up_ref, down_ref, gu_ref, gd_ref in zip(ups, downs, gus, gds):
        pre = mm(active, up_ref[...])
        logistic = jax.nn.sigmoid(pre)
        hidden = (pre * logistic).astype(BF16)
        gd_ref[:, :part] = mm(error_t, hidden).astype(BF16)
        d_hidden = mm(error, down_ref[...])
        d_pre = (d_hidden * (logistic * (1.0 + pre * (1.0 - logistic)))).astype(BF16)
        gu_ref[...] = mm(active_t, d_pre).astype(BF16)
        total += mm_nt(d_pre, up_ref[...])
    back, grad_gain = norm_back(normed, inverse, gain_ref[...], total)
    out_ref[...] = upstream + back
    known = [grad_gain, one_ref[...], two_ref[...], last_ref[...]]
    count = sum(value.shape[0] for value in known)
    known.append(jnp.zeros((SUB - count, upstream.shape[1]), F32))
    columns = jnp.concatenate(known, axis=0).T.astype(BF16)
    for gd_ref in gds:
        gd_ref[:, part:] = columns


def project_kernel(groups, v_ref, gain_ref, *refs):
    weights, q_ref = refs[:groups], refs[groups]
    pair_refs = refs[groups + 1 :]
    normed, _ = normed_of(v_ref[...])
    active = (normed * gain_ref[...]).astype(BF16)
    q_ref[...] = mm(active, column_join(weights, 0)).astype(BF16)
    width = q_ref.shape[1] // len(pair_refs)
    for i in (0, 1):
        projected = mm(active, column_join(weights, i + 1)).astype(BF16)
        for h, pair_ref in enumerate(pair_refs):
            pair_ref[i] = projected[:, h * width : (h + 1) * width]


def project_backward_kernel(groups, halves, v_ref, d_ref, gain_ref, *refs):
    weights, smalls = refs[:groups], refs[groups : 2 * groups]
    dqs = refs[2 * groups : 2 * groups + halves]
    pairs, tail = refs[2 * groups + halves : -2 - groups], refs[-2 - groups :]
    each = len(pairs) // halves
    out_ref, gg_ref, grads = tail[0], tail[1], tail[2:]
    normed, inverse = normed_of(v_ref[...])
    active_t = (normed * gain_ref[...]).astype(BF16).T
    total = jnp.zeros_like(d_ref[...])
    for i in range(3):
        if i == 0:
            parts = [ref[...] for ref in dqs]
        else:
            parts = [
                sum(ref[i - 1].astype(F32) for ref in pairs[h * each : (h + 1) * each]).astype(BF16)
                for h in range(halves)
            ]
        error = jnp.concatenate(parts, axis=1) if halves > 1 else parts[0]
        total += mm_nt(error, column_join(weights, i))
        grad = mm(active_t, error).astype(BF16)
        for g, grad_ref in enumerate(grads):
            grad_ref[:, i * SUB : (i + 1) * SUB] = grad[:, g * SUB : (g + 1) * SUB]
    for small_ref, grad_ref in zip(smalls, grads):
        grad_ref[:, 3 * SUB :] = small_ref[...]
    back, grad_gain = norm_back(normed, inverse, gain_ref[...], total)
    out_ref[...] = d_ref[...] + back
    gg_ref[...] = grad_gain


def middle_kernel(groups, halves, v_ref, gain_ref, *refs):
    weights, contexts = refs[:groups], refs[groups : groups + halves]
    out_ref, lin_ref, sig_ref, glu_ref = refs[groups + halves :]
    parts = [ref[...] for ref in contexts]
    context = jnp.concatenate(parts, axis=1) if halves > 1 else parts[0]
    value = v_ref[...] + mm_nt(context, column_join(weights, 0))
    out_ref[...] = value
    normed, _ = normed_of(value)
    active = (normed * gain_ref[...]).astype(BF16)
    lin = mm(active, column_join(weights, 1))
    gate = jax.nn.sigmoid(mm(active, column_join(weights, 2)))
    lin_ref[...] = lin
    sig_ref[...] = gate
    glu_ref[...] = (lin * gate).astype(BF16)


def middle_backward_kernel(groups, halves, dglu_ref, lin_ref, sig_ref, v_ref, d_ref, gain_ref, *refs):
    weights, contexts = refs[:groups], refs[groups : groups + halves]
    out_ref, gg_ref, dctx_ref = refs[groups + halves : groups + halves + 3]
    grads = refs[groups + halves + 3 :]
    d_glu, lin, gate = dglu_ref[...], lin_ref[...], sig_ref[...]
    d_lin = (d_glu * gate).astype(BF16)
    d_gate = (d_glu * lin * gate * (1.0 - gate)).astype(BF16)
    normed, inverse = normed_of(v_ref[...])
    active_t = (normed * gain_ref[...]).astype(BF16).T
    total = mm_nt(d_lin, column_join(weights, 1)) + mm_nt(d_gate, column_join(weights, 2))
    back, grad_gain = norm_back(normed, inverse, gain_ref[...], total)
    value = d_ref[...] + back
    out_ref[...] = value
    gg_ref[...] = grad_gain
    error = value.astype(BF16)
    dctx_ref[...] = mm(error, column_join(weights, 0)).astype(BF16)
    parts = [ref[...] for ref in contexts]
    context = jnp.concatenate(parts, axis=1) if halves > 1 else parts[0]
    for i, grad in enumerate((mm(error.T, context), mm(active_t, d_lin), mm(active_t, d_gate))):
        rounded = grad.astype(BF16)
        for g, grad_ref in enumerate(grads):
            grad_ref[:, i * SUB : (i + 1) * SUB] = rounded[:, g * SUB : (g + 1) * SUB]


def turn_kernel(groups, batch_rows, conv_ref, stat_ref, bn_ref, v_ref, up_ref, gains_ref, *refs):
    mids, weights = refs[:groups], refs[groups : 2 * groups]
    final_ref, out_ref, dpre_ref, gg_ref, sums_ref = refs[2 * groups : 2 * groups + 5]
    grads, pres = refs[2 * groups + 5 : -1], refs[-1]
    part = pres.shape[2]
    top, bottom = slice(0, part), slice(part, 2 * part)
    gain_three, gain_four = gains_ref[3:4], gains_ref[4:5]
    mean = stat_ref[0:1] / batch_rows
    white = (conv_ref[...] - mean) * lax.rsqrt(stat_ref[1:2] / batch_rows - mean * mean + EPS)
    bn_pre = bn_ref[0:1] * white + bn_ref[1:2]
    activated = (bn_pre * jax.nn.sigmoid(bn_pre)).astype(BF16)
    outward = column_join(mids, 3)
    third = v_ref[...] + mm_nt(activated, outward)
    normed, inverse = normed_of(third)
    active = (normed * gain_three).astype(BF16)
    total = jnp.zeros_like(third)
    for g, weight in enumerate(weights):
        pre = mm(active, weight[:, top])
        pres[g] = pre
        total += mm_nt((pre * jax.nn.sigmoid(pre)).astype(BF16), weight[:, bottom])
    last_normed, last_inverse = normed_of(third + 0.5 * total)
    final_ref[...] = (last_normed * gain_four).astype(BF16)
    fourth, grad_four = norm_back(last_normed, last_inverse, gain_four, up_ref[...])
    error = (0.5 * fourth).astype(BF16)
    active_t = active.T
    error_t = error.T
    total = jnp.zeros_like(third)
    for g, (weight, grad_ref) in enumerate(zip(weights, grads)):
        pre = pres[g]
        logistic = jax.nn.sigmoid(pre)
        hidden = (pre * logistic).astype(BF16)
        grad_ref[:, SUB + part :] = mm(error_t, hidden).astype(BF16)
        d_hidden = mm(error, weight[:, bottom])
        d_pre = (d_hidden * (logistic * (1.0 + pre * (1.0 - logistic)))).astype(BF16)
        grad_ref[:, SUB : SUB + part] = mm(active_t, d_pre).astype(BF16)
        total += mm_nt(d_pre, weight[:, top])
    back, grad_three = norm_back(normed, inverse, gain_three, total)
    value = fourth + back
    out_ref[...] = value
    gg_ref[0:1] = grad_three
    gg_ref[1:2] = grad_four
    error = value.astype(BF16)
    grad = mm(error.T, activated).astype(BF16)
    for g, grad_ref in enumerate(grads):
        grad_ref[:, :SUB] = grad[:, g * SUB : (g + 1) * SUB]
    d_pre = mm(error, outward) * swish_grad(bn_pre)
    dpre_ref[...] = d_pre
    sums_ref[0:1] = jnp.sum(d_pre, axis=0, keepdims=True)
    sums_ref[1:2] = jnp.sum(d_pre * white, axis=0, keepdims=True)


def build_skew(line_ref, skew, heads, chunks):
    for h in range(heads):
        for c in range(chunks):
            window = jnp.concatenate(
                [line_ref[0, h, c + 1 : c + 2, :], line_ref[0, h, c : c + 1, :]], axis=1
            )
            window = jnp.broadcast_to(window, (SUB, 2 * SUB))
            rolled = pltpu.roll(window, 1, 1, stride=1, stride_axis=0)
            skew[h, SUB * c : SUB * (c + 1), :] = rolled[:, SUB:]


def stack_heads(rows, heads, factor):
    lane = lax.broadcasted_iota(jnp.int32, rows.shape, 1)
    size = rows.shape[1] // heads
    return jnp.concatenate(
        [
            rows * jnp.where((lane >= h * size) & (lane < (h + 1) * size), factor, 0.0).astype(BF16)
            for h in range(heads)
        ],
        axis=0,
    )


def diagonal_heads(value, heads):
    size, columns = value.shape[0] // heads, value.shape[1] // heads
    parts = [
        value[h * size : (h + 1) * size, h * columns : (h + 1) * columns] for h in range(heads)
    ]
    return jnp.concatenate(parts, axis=0)


def tile_bias(skew, columns, block, offset_of):
    parts = [
        skew[h, pl.ds(pl.multiple_of(offset_of(qb), SUB), block), :] for h, qb in columns
    ]
    return jnp.concatenate(parts, axis=1)


def column_tiles(heads, steps):
    columns = [(h, qb) for h in range(heads) for qb in range(steps)]
    return [columns[i : i + 2] for i in range(0, len(columns), 2)]


def attend_forward_kernel(pieces, heads, qpos, kpos, q_ref, line_ref, *refs):
    k_refs = refs[:pieces]
    v_refs = refs[pieces : 2 * pieces]
    ctx_ref, lse_ref, ctx32_ref, skew, query, scores, probs, v_t = refs[2 * pieces :]
    rows, width = q_ref.shape
    block = rows // 2
    chunks = skew.shape[1] // SUB
    middle = skew.shape[1] // 2
    tiles = column_tiles(heads, rows // SUB)
    span = 2 * SUB
    build_skew(line_ref, skew, heads, chunks)
    for p in range(pieces):
        v_t[:width, p * rows : (p + 1) * rows] = v_refs[p][0].T
    v_t[width:, :] = jnp.ones_like(v_t[width:, :])
    query[...] = stack_heads(q_ref[...], heads, (width // heads) ** (-0.5))
    tops = [jnp.full((8, span), -jnp.inf, F32) for _ in tiles]
    for c in range(2 * pieces):
        keys = k_refs[c // 2][0, (c % 2) * block : (c % 2 + 1) * block, :]
        for t, tile in enumerate(tiles):
            raw = mm_nt(keys, query[t * span : (t + 1) * span, :])
            raw = raw + tile_bias(skew, tile, block, lambda qb: kpos[c] - qpos[qb] + middle)
            scores[c * block : (c + 1) * block, t * span : (t + 1) * span] = raw
            tops[t] = jnp.maximum(tops[t], jnp.max(raw.reshape(block // 8, 8, span), axis=0))
    tops = [jnp.max(top, axis=0, keepdims=True) for top in tops]
    for c in range(2 * pieces):
        for t in range(len(tiles)):
            part = (slice(c * block, (c + 1) * block), slice(t * span, (t + 1) * span))
            probs[part] = jnp.exp(scores[part] - tops[t]).astype(BF16)
    out_t = mm(v_t[...], probs[...])
    total = out_t[width : width + 1, :]
    out_t = out_t[:width, :] / total
    out = diagonal_heads(out_t, heads).T
    ctx_ref[...] = out.astype(BF16)
    ctx32_ref[...] = out
    lse_ref[0] = jnp.concatenate(tops, axis=1) + jnp.log(total)


def attend_backward_kernel(pieces, heads, qpos, kpos, q_ref, d_ref, ctx_ref, lse_ref, line_ref, *refs):
    k_refs = refs[:pieces]
    v_refs = refs[pieces : 2 * pieces]
    dq_ref = refs[2 * pieces]
    dkv_refs = refs[2 * pieces + 1 : 3 * pieces + 1]
    line_grad, skew, skew_grad, query, error, probs, d_scores, k_t = refs[3 * pieces + 1 :]
    rows, width = q_ref.shape
    block = rows // 2
    chunks = skew.shape[1] // SUB
    middle = skew.shape[1] // 2
    scale = (width // heads) ** (-0.5)
    size = width // heads
    tiles = column_tiles(heads, rows // SUB)
    span = 2 * SUB
    build_skew(line_ref, skew, heads, chunks)
    skew_grad[...] = jnp.zeros_like(skew_grad)
    for p in range(pieces):
        k_t[:, p * rows : (p + 1) * rows] = k_refs[p][0].T
    query[...] = stack_heads(q_ref[...], heads, scale)
    error[...] = stack_heads(d_ref[...], heads, 1.0)
    weighed = (d_ref[...].astype(F32) * ctx_ref[...]).T
    dot_sum = jnp.concatenate(
        [jnp.sum(weighed[h * size : (h + 1) * size], axis=0, keepdims=True) for h in range(heads)],
        axis=1,
    )
    lse = lse_ref[0]
    for c in range(2 * pieces):
        part = slice((c % 2) * block, (c % 2 + 1) * block)
        here = slice(c * block, (c + 1) * block)
        keys = k_refs[c // 2][0, part, :]
        values = v_refs[c // 2][0, part, :]
        for t, tile in enumerate(tiles):
            cols = slice(t * span, (t + 1) * span)
            raw = mm_nt(keys, query[cols, :])
            bias = tile_bias(skew, tile, block, lambda qb: kpos[c] - qpos[qb] + middle)
            prob = jnp.exp(raw + bias - lse[:, cols])
            d_score = prob * (mm_nt(values, error[cols, :]) - dot_sum[:, cols])
            probs[c % 2, :, cols] = prob.astype(BF16)
            d_scores[here, cols] = d_score.astype(BF16)
            for i, (h, qb) in enumerate(tile):
                offset = pl.multiple_of(kpos[c] - qpos[qb] + middle, SUB)
                skew_grad[h, pl.ds(offset, block), :] += d_score[:, i * SUB : (i + 1) * SUB]
        dkv_refs[c // 2][0, part, :] = mm(d_scores[here, :], query[...]).astype(BF16)
        dkv_refs[c // 2][1, part, :] = mm(probs[c % 2], error[...]).astype(BF16)
    dq_t = mm(k_t[...], d_scores[...])
    dq_ref[...] = (diagonal_heads(dq_t, heads).T * scale).astype(BF16)
    line_grad[...] = jnp.zeros_like(line_grad)
    for h in range(heads):
        for c in range(chunks):
            block_grad = skew_grad[h, SUB * c : SUB * (c + 1), :]
            value = jnp.concatenate([jnp.zeros_like(block_grad), block_grad], axis=1)
            half = SUB // 2
            while half >= 1:
                value = value[:half] + pltpu.roll(value[half:], 2 * SUB - half, 1)
                half //= 2
            value = pltpu.roll(value, 2 * SUB - 1, 1)
            line_grad[0, h, c + 1 : c + 2, :] += value[:, :SUB]
            line_grad[0, h, c : c + 1, :] += value[:, SUB:]


def attention_specs(rows, first, pieces, shifts, line_shape):
    whole_q = pl.BlockSpec((rows, SUB), lambda j, *_: (0, j + first))
    own = pl.BlockSpec((rows, SUB), lambda j, *_: (0, j))
    line = pl.BlockSpec((1,) + line_shape[1:], lambda j, *_: (j + first, 0, 0, 0))
    keys, values = [], []
    for p in range(pieces):
        keys.append(pl.BlockSpec((1, rows, SUB), lambda j, *_, d=shifts[p]: (0, 0, j ^ d)))
        values.append(pl.BlockSpec((1, rows, SUB), lambda j, *_, d=shifts[p]: (1, 0, j ^ d)))
    return (whole_q, own, line, keys, values)


def attend_forward(query, pairs, shifts, line, first, qpos, kpos):
    rows = query.shape[0]
    heads = line.shape[1]
    groups = pairs[0].shape[2] // SUB
    pieces = len(pairs)
    table = (line.shape[2] - 1) * SUB
    whole_q, own, line_spec, keys, values = attention_specs(rows, first, pieces, shifts, line.shape)
    return pl.pallas_call(
        functools.partial(attend_forward_kernel, pieces, heads),
        out_shape=(
            jax.ShapeDtypeStruct((rows, groups * SUB), BF16),
            jax.ShapeDtypeStruct((groups, 1, heads * rows), F32),
            jax.ShapeDtypeStruct((rows, groups * SUB), F32),
        ),
        grid_spec=pltpu.PrefetchScalarGridSpec(
            num_scalar_prefetch=2,
            grid=(groups,),
            in_specs=[whole_q, line_spec] + keys + values,
            out_specs=(
                own,
                pl.BlockSpec((1, 1, heads * rows), lambda j, *_: (j, 0, 0)),
                own,
            ),
            scratch_shapes=[
                pltpu.VMEM((heads, table, SUB), F32),
                pltpu.VMEM((heads * rows, SUB), BF16),
                pltpu.VMEM((pieces * rows, heads * rows), F32),
                pltpu.VMEM((pieces * rows, heads * rows), BF16),
                pltpu.VMEM((SUB + 16, pieces * rows), BF16),
            ],
        ),
        name="attend_forward",
    )(qpos, kpos, query, line, *pairs, *pairs)


def attend_backward(query, d_context, lse, context, pairs, shifts, line, first, qpos, kpos):
    rows = query.shape[0]
    heads = line.shape[1]
    groups = pairs[0].shape[2] // SUB
    pieces = len(pairs)
    table = (line.shape[2] - 1) * SUB
    whole_q, own, line_spec, keys, values = attention_specs(rows, first, pieces, shifts, line.shape)
    lse_spec = pl.BlockSpec((1, 1, heads * rows), lambda j, *_: (j, 0, 0))
    pair_specs = [
        pl.BlockSpec((2, rows, SUB), lambda j, *_, d=shifts[p]: (0, 0, j ^ d))
        for p in range(pieces)
    ]
    return pl.pallas_call(
        functools.partial(attend_backward_kernel, pieces, heads),
        out_shape=(
            (jax.ShapeDtypeStruct((rows, groups * SUB), BF16),)
            + tuple(jax.ShapeDtypeStruct(pairs[0].shape, BF16) for _ in range(pieces))
            + (jax.ShapeDtypeStruct((groups,) + line.shape[1:], F32),)
        ),
        grid_spec=pltpu.PrefetchScalarGridSpec(
            num_scalar_prefetch=2,
            grid=(groups,),
            in_specs=[whole_q, whole_q, own, lse_spec, line_spec] + keys + values,
            out_specs=(
                (own,)
                + tuple(pair_specs)
                + (pl.BlockSpec((1,) + line.shape[1:], lambda j, *_: (j, 0, 0, 0)),)
            ),
            scratch_shapes=[
                pltpu.VMEM((heads, table, SUB), F32),
                pltpu.VMEM((heads, table, SUB), F32),
                pltpu.VMEM((heads * rows, SUB), BF16),
                pltpu.VMEM((heads * rows, SUB), BF16),
                pltpu.VMEM((2, rows // 2, heads * rows), BF16),
                pltpu.VMEM((pieces * rows, heads * rows), BF16),
                pltpu.VMEM((SUB, pieces * rows), BF16),
            ],
        ),
        name="attend_backward",
    )(qpos, kpos, query, d_context, context, lse, line, *pairs, *pairs)


def block_step(
    block_input,
    out_cotangent,
    early_up,
    early_down,
    attention_in,
    attention_out,
    relative_bias,
    pointwise_in,
    depthwise,
    batch_norm,
    pointwise_out,
    late_up,
    late_down,
    norm_gains,
):
    dp_n, mp_n = lax.axis_size("dp"), lax.axis_size("mp")
    held_rows, features = block_input.shape[1:]
    block = held_rows // mp_n
    rows = 2 * block
    batch_rows = held_rows * dp_n
    batch = lax.axis_index("dp") % 2
    place = lax.axis_index("mp")
    shard_rows, part = early_up.shape
    heads, table_part = relative_bias.shape
    channel_part, kernel = depthwise.shape
    head_width = attention_out.shape[0]
    channels = mp_n * head_width
    margin = (kernel - 1) // 2
    order_a, order_b = full_order()
    fold = max(1, SUB // head_width)
    groups = mp_n // fold
    blocks = jnp.array(reversed_blocks(dp_n), jnp.int32)
    to_natural = blocks[jnp.arange(dp_n, dtype=jnp.int32) ^ lax.axis_index("dp")]
    to_held = blocks ^ lax.axis_index("dp")
    choice = block_choice(features, dp_n, BF16)

    def exchanged(value):
        mine = lax.dynamic_slice_in_dim(value, place * block, block, 1)
        own = lax.dynamic_index_in_dim(mine, batch, 0, keepdims=False)
        away = lax.dynamic_index_in_dim(mine, 1 - batch, 0, keepdims=False)
        other = flip_pair(away, "dp", 0)
        return mm(jnp.concatenate([own, other], axis=0), choice)

    def listed(parts, widths):
        return regroup([parts[delta] for delta in range(mp_n)], widths, fold)

    def unlisted(parts, widths):
        return dict(enumerate(ungroup(list(parts), widths, fold)))

    bias_rows = heads * table_part // SUB
    tap_n = kernel + 2
    gain_row = bias_rows + channel_part
    small_rows = gain_row + norm_gains.shape[0]
    small = jnp.concatenate(
        [
            relative_bias.reshape(bias_rows, SUB),
            jnp.pad(jnp.concatenate([depthwise, batch_norm.T], axis=1), ((0, 0), (0, SUB - tap_n))),
            jnp.pad(norm_gains, ((0, shard_rows - small_rows), (0, SUB - shard_rows))),
        ],
        axis=0,
    )
    early_u = gather_groups(early_up, order_a)
    early_d = gather_groups(early_down.T, order_b)
    start = exchanged(block_input)
    pair_widths = [head_width] * 3
    att_shard = jnp.concatenate([attention_in[0], attention_in[1], attention_in[2], small], axis=1)
    att_held = gather_groups(att_shard, order_a)
    mid_shard = jnp.concatenate(
        [attention_out.T, pointwise_in[0], pointwise_in[1], pointwise_out.T], axis=1
    )
    late_shard = jnp.concatenate([late_up, late_down.T], axis=1)
    mid = listed(gather_groups(mid_shard, order_b), [head_width] * 4)
    late = listed(gather_groups(late_shard, order_a), [part] * 2)
    if fold == 1:
        att = [att_held[delta] for delta in range(mp_n)]
    else:
        att = listed({d: value[:, : 3 * head_width] for d, value in att_held.items()}, pair_widths)
    gains = (
        att_held[0]
        .reshape(dp_n, shard_rows, -1)[:, gain_row:small_rows, 3 * head_width : 3 * head_width + shard_rows]
        .transpose(1, 0, 2)
        .reshape(5, features)
        .astype(F32)
    )
    gain = [gains[i : i + 1] for i in range(5)]
    tiny = jnp.stack([att_held[delta][:, 3 * head_width :] for delta in range(mp_n)])
    tiny = tiny.reshape(mp_n, dp_n, shard_rows, SUB)[:, to_natural]
    line = (
        tiny[:, :, :bias_rows]
        .reshape(mp_n, dp_n, heads, table_part // SUB, SUB)
        .transpose(0, 2, 1, 3, 4)
        .reshape(mp_n, heads, dp_n * table_part // SUB, SUB)
    )
    line = jnp.einsum("ghcl,lk->ghck", line, lane_flip(BF16), preferred_element_type=F32)
    line = jnp.pad(line, ((0, 0), (0, 0), (1, 0), (0, 0)))
    line = line.reshape(groups, heads * fold, line.shape[2], SUB)
    taps = (
        tiny[:, :, bias_rows : bias_rows + channel_part, :tap_n].reshape(channels, tap_n).T.astype(F32)
    )
    tap_rows = [taps[tap] for tap in range(kernel)]
    bn_rows = taps[kernel:]

    half_of_slot = jnp.stack([batch, 1 - batch]).astype(jnp.int32)
    kept = [0]
    for bit in range(bits_of("mp") - 1, -1, -1):
        kept = kept + [delta ^ 1 << bit for delta in kept]
    qpos = (
        half_of_slot[:, None] * held_rows
        + place * block
        + SUB * jnp.arange(block // SUB, dtype=jnp.int32)[None, :]
    ).reshape(-1)
    kpos = jnp.stack(
        [half_of_slot[r] * held_rows + (place ^ delta) * block for delta in kept for r in (0, 1)]
    )
    wide = (rows, channels)
    halves = 2 if fold == 1 and mp_n >= 4 else 1
    local = groups // halves
    up_list = [early_u[delta] for delta in range(mp_n)]
    down_list = [early_d[delta] for delta in range(mp_n)]
    (after_first,) = call_kernel(
        functools.partial(ffn_forward_kernel, mp_n),
        [((rows, features), F32)],
        start,
        gain[0],
        *up_list,
        *down_list,
    )
    query, *pair_halves = call_kernel(
        functools.partial(project_kernel, groups),
        [(wide, BF16)] + [((2, rows, local * SUB), BF16)] * halves,
        after_first,
        gain[1],
        *att,
    )
    top_bit = bits_of("mp") - 1
    held_pairs = []
    for h in range(halves):
        pieces = [pair_halves[h]]
        away = pair_halves[halves - 1 - h]
        if h > 0:
            away = tied(away, held_pairs[h - 1][1])
        pieces.append(flip_pair(away, "mp", top_bit))
        for bit in range(top_bit - 1, -1, -1):
            pieces = pieces + [flip_pair(piece, "mp", bit) for piece in pieces]
        if fold > 1:
            pieces = [swap_groups(piece, mp_n, delta) for piece, delta in zip(pieces, kept)]
        held_pairs.append(pieces)
    shifts = [delta & (local - 1) if fold == 1 else 0 for delta in kept]
    attended = []
    for h in range(halves):
        attended.append(attend_forward(query, held_pairs[h], shifts, line, h * local, qpos, kpos))
    contexts = [item[0] for item in attended]
    after_second, lin, gate_sig, glu = call_kernel(
        functools.partial(middle_kernel, groups, halves),
        [((rows, features), F32), (wide, F32), (wide, F32), (wide, BF16)],
        after_first,
        gain[2],
        *mid,
        *contexts,
    )
    cotangent = exchanged(out_cotangent)
    glu = tied(glu, cotangent).reshape(2, block, channels)
    edge = margin + 1
    before, after = edge_rows(glu[:, :edge], glu[:, block - edge :], half_of_slot)
    extended = jnp.concatenate([before[:, 1:], glu, after[:, :margin]], axis=1).astype(F32)
    conv = jnp.zeros((2, block, channels), F32)
    for tap in range(kernel):
        conv = conv + tap_rows[tap] * extended[:, tap : tap + block]
    conv = conv.reshape(rows, channels)
    sums = channel_total(jnp.stack([jnp.sum(conv, axis=0), jnp.sum(conv * conv, axis=0)]))
    bmean = sums[0:1] / batch_rows
    binv = lax.rsqrt(sums[1:2] / batch_rows - bmean * bmean + EPS)

    wide_part = part * fold
    turn_widths = [head_width, part, part]
    final_rows, d_third, d_pre, gg_last, local_sums, *turn_grads = pl.pallas_call(
        functools.partial(turn_kernel, groups, batch_rows),
        out_shape=[
            jax.ShapeDtypeStruct((rows, features), BF16),
            jax.ShapeDtypeStruct((rows, features), F32),
            jax.ShapeDtypeStruct(wide, F32),
            jax.ShapeDtypeStruct((2, features), F32),
            jax.ShapeDtypeStruct((2, channels), F32),
        ]
        + [jax.ShapeDtypeStruct((features, SUB + 2 * wide_part), BF16)] * groups,
        scratch_shapes=[pltpu.VMEM((groups, rows, wide_part), F32)],
        name="turn",
    )(conv, sums, bn_rows, after_second, cotangent, gains, *mid, *late)
    turn_marks = []
    own_turn = scatter_groups(unlisted(turn_grads, turn_widths), order_a, turn_marks)

    sums = channel_total(local_sums)
    white = (conv - bmean) * binv
    d_conv = (
        binv * bn_rows[0:1] * (d_pre - sums[0:1] / batch_rows - white * sums[1:2] / batch_rows)
    ).reshape(2, block, channels)
    before, after = edge_rows(d_conv[:, :edge], d_conv[:, block - edge :], half_of_slot)
    d_extended = jnp.concatenate([before[:, 1:], d_conv, after[:, :margin]], axis=1)
    d_glu = jnp.zeros((2, block, channels), F32)
    tap_grads = []
    for tap in range(kernel):
        d_glu = d_glu + tap_rows[tap] * d_extended[:, kernel - 1 - tap : kernel - 1 - tap + block]
        tap_grads.append(jnp.sum(extended[:, tap : tap + block] * d_conv, axis=(0, 1)))
    tap_grads = jnp.stack(tap_grads + [local_sums[1], local_sums[0]])
    d_second, gain_two, d_context, *middle_grads = call_kernel(
        functools.partial(middle_backward_kernel, groups, halves),
        [((rows, features), F32), (gain[2].shape, F32), (wide, BF16)]
        + [((features, 3 * SUB), BF16)] * groups,
        tied(d_glu.reshape(rows, channels), turn_marks[0][1 << top_bit]),
        lin,
        gate_sig,
        after_second,
        d_third,
        gain[2],
        *mid,
        *contexts,
    )
    own_middle = scatter_groups(unlisted(middle_grads, pair_widths), order_b)
    d_queries, kept_pairs, sent_pairs, line_grads = [], [], [], []
    for h in range(halves):
        grads = attend_backward(
            query, d_context, attended[h][1], attended[h][2], held_pairs[h], shifts, line,
            h * local, qpos, kpos,
        )
        d_queries.append(grads[0])
        line_grads.append(grads[-1])
        pieces = dict(zip(kept, grads[1:-1]))
        if fold > 1:
            pieces = {delta: swap_groups(value, mp_n, delta) for delta, value in pieces.items()}
        kept_pairs.append([pieces[0]])
        for bit in range(top_bit):
            for delta in [d for d in pieces if d >> bit & 1]:
                other = flip_pair(pieces.pop(delta), "mp", bit)
                home = delta ^ 1 << bit
                if home == 0:
                    kept_pairs[h].append(other)
                else:
                    pieces[home] = (pieces[home].astype(F32) + other.astype(F32)).astype(BF16)
        sent_pairs.append(flip_pair(pieces[1 << top_bit], "mp", top_bit))
    line_grad = jnp.concatenate(line_grads, axis=0)[:, :, 1:].reshape(mp_n, heads, -1, SUB)
    line_grad = jnp.einsum(
        "ghcl,lk->ghck", line_grad, lane_flip(F32), precision=lax.Precision.HIGHEST
    )
    tiny = jnp.concatenate(
        [
            line_grad.reshape(mp_n, heads, dp_n, table_part // SUB, SUB)
            .transpose(0, 2, 1, 3, 4)
            .reshape(mp_n, dp_n, bias_rows, SUB)[:, to_held],
            jnp.pad(
                tap_grads.T.reshape(mp_n, dp_n, channel_part, tap_n)[:, to_held],
                (
                    (0, 0),
                    (0, 0),
                    (0, shard_rows - bias_rows - channel_part),
                    (0, SUB - tap_n),
                ),
            ),
        ],
        axis=2,
    ).astype(BF16)
    tiny = tiny.reshape(mp_n, features, SUB)
    smalls = [tiny[g] for g in range(groups)]
    d_first, gain_one, *att_grads = call_kernel(
        functools.partial(project_backward_kernel, groups, halves),
        [((rows, features), F32), (gain[1].shape, F32)] + [((features, 4 * SUB), BF16)] * groups,
        after_first,
        d_second,
        gain[1],
        *att,
        *smalls,
        *d_queries,
        *[
            part
            for h in range(halves)
            for part in kept_pairs[h] + [sent_pairs[halves - 1 - h]]
        ],
    )
    if fold > 1:
        att_grads = ungroup([grad[:, : 3 * SUB] for grad in att_grads], pair_widths, fold)
        att_grads = [jnp.concatenate([g, t], axis=1) for g, t in zip(att_grads, tiny)]
    own_att = scatter_groups(dict(enumerate(att_grads)), order_a)
    d_start, *early_grads = call_kernel(
        functools.partial(ffn_backward_kernel, mp_n),
        [((rows, features), F32)]
        + [((features, part), BF16)] * mp_n
        + [((features, part + SUB), BF16)] * mp_n,
        start,
        d_first,
        gain[0],
        gain_one,
        gain_two,
        gg_last,
        *up_list,
        *down_list,
    )
    up_marks = []
    own_up = scatter_groups(dict(enumerate(early_grads[:mp_n])), order_a, up_marks)
    own_down = scatter_groups(dict(enumerate(early_grads[mp_n:])), order_b)

    def returned(own, away):
        other = flip_pair(away, "dp", 0).astype(own.dtype)
        first = batch == 0
        return jnp.stack([jnp.where(first, own, other), jnp.where(first, other, own)])

    def columns(value, index):
        return value[:, index * head_width : (index + 1) * head_width]

    tail = own_att[:, 3 * head_width :]
    per_channel = tail[bias_rows : bias_rows + channel_part]
    natural = lax.dot_general(
        tied(d_start, up_marks[0][1 << top_bit]), choice.astype(F32), NT, precision=lax.Precision.HIGHEST
    )
    final_rows = mm_nt(final_rows, choice).astype(BF16)
    return (
        returned(final_rows[:block], final_rows[block:]),
        returned(natural[:block], natural[block:].astype(BF16)),
        own_up,
        own_down[:, :part].T,
        jnp.stack([columns(own_att, i) for i in range(3)]),
        columns(own_middle, 0).T,
        tail[:bias_rows].reshape(heads, table_part),
        jnp.stack([columns(own_middle, 1), columns(own_middle, 2)]),
        per_channel[:, :kernel],
        per_channel[:, kernel:tap_n].T,
        columns(own_turn, 0).T,
        own_turn[:, head_width : head_width + part],
        own_turn[:, head_width + part :].T,
        own_down[:, part : part + 5].T,
    )


def solution(mesh):
    placed = (
        P(None, "dp", None),
        P(None, "dp", None),
        P("dp", "mp"),
        P("mp", "dp"),
        P(None, "dp", "mp"),
        P("mp", "dp"),
        P("mp", "dp"),
        P(None, "dp", "mp"),
        P(("mp", "dp"), None),
        P(None, ("mp", "dp")),
        P("mp", "dp"),
        P("dp", "mp"),
        P("mp", "dp"),
        P(None, "dp"),
    )
    returned = (P(None, ("dp", "mp"), None), P(None, ("dp", "mp"), None)) + placed[2:]
    return jax.shard_map(block_step, mesh=mesh, in_specs=placed, out_specs=returned, check_vma=False)
```

```python
import functools

import jax
import jax.numpy as jnp
from jax import lax
from jax.experimental import pallas as pl
from jax.experimental.pallas import tpu as pltpu
from jax.sharding import PartitionSpec as P


EPS = 1e-05
BF16 = jnp.bfloat16
F32 = jnp.float32
SUB = 128
NT = (((1,), (1,)), ((), ()))


def flip_pair(value, axis, bit):
    return lax.ppermute(value, axis, [(i, i ^ 1 << bit) for i in range(lax.axis_size(axis))])


def bits_of(axis):
    return (lax.axis_size(axis) - 1).bit_length()


def own_bit(axis, bit):
    return lax.shift_right_logical(lax.axis_index(axis), bit) & 1


def full_order():
    dp_bits, mp_bits = bits_of("dp"), bits_of("mp")
    dp_high = [("dp", bit) for bit in range(dp_bits - 1, 0, -1)]
    mp_high = [("mp", bit) for bit in range(mp_bits - 1, 0, -1)]
    first = dp_high + [("dp", 0)] + mp_high + [("mp", 0)]
    second = dp_high + mp_high + [("dp", 0)] + [("mp", 0)]
    return (first, second)


def tied(value, other):
    return lax.optimization_barrier((value, other))[0]


def gather_groups(shard, order):
    held = {0: shard}
    for axis, bit in order:
        for delta in list(held):
            own = held[delta]
            other = flip_pair(own, axis, bit)
            if axis == "mp":
                held[delta ^ 1 << bit] = other
            else:
                held[delta] = jnp.concatenate([own, other], axis=0)
    return held


def scatter_groups(parts, order, marks=None):
    parts = dict(parts)
    total = None
    for axis, bit in reversed(order):
        if axis == "mp":
            for delta in [d for d in parts if d >> bit & 1]:
                other = flip_pair(parts.pop(delta), axis, bit)
                home = delta ^ 1 << bit
                parts[home] = (parts[home].astype(F32) + other.astype(F32)).astype(BF16)
        else:
            for delta in parts:
                half = parts[delta].shape[0] // 2
                keep, send = parts[delta][:half], parts[delta][half:]
                other = flip_pair(send, axis, bit)
                total = keep.astype(F32) + other.astype(F32)
                parts[delta] = total.astype(BF16)
        if marks is not None:
            marks.append(dict(parts))
    return total


def reversed_blocks(count):
    bits = (count - 1).bit_length()
    return [int(format(i, "b").zfill(bits)[::-1], 2) if bits else 0 for i in range(count)]


def block_choice(features, count, dtype):
    row = lax.broadcasted_iota(jnp.int32, (features, features), 0)
    col = lax.broadcasted_iota(jnp.int32, (features, features), 1)
    size = features // count
    block, image = col // size, jnp.zeros_like(col)
    for bit in range((count - 1).bit_length()):
        image = image * 2 + (block >> bit & 1)
    image = image ^ lax.axis_index("dp")
    return (row == image * size + col % size).astype(dtype)


def lane_flip(dtype):
    row = lax.broadcasted_iota(jnp.int32, (SUB, SUB), 0)
    col = lax.broadcasted_iota(jnp.int32, (SUB, SUB), 1)
    return (row + col == SUB - 1).astype(dtype)


def regroup(parts, widths, count):
    if count == 1:
        return parts
    joined = []
    for start in range(0, len(parts), count):
        pieces, at = [], 0
        for width in widths:
            pieces += [part[:, at : at + width] for part in parts[start : start + count]]
            at += width
        joined.append(jnp.concatenate(pieces, axis=1))
    return joined


def ungroup(parts, widths, count):
    if count == 1:
        return parts
    split = []
    for part in parts:
        for i in range(count):
            pieces, at = [], 0
            for width in widths:
                pieces.append(part[:, at + i * width : at + (i + 1) * width])
                at += width * count
            split.append(jnp.concatenate(pieces, axis=1))
    return split


def swap_groups(value, groups, delta):
    width = value.shape[-1] // groups
    parts = [value[..., (g ^ delta) * width : ((g ^ delta) + 1) * width] for g in range(groups)]
    return jnp.concatenate(parts, axis=-1)


def absolute_groups(value, groups):
    for bit in range((groups - 1).bit_length()):
        value = jnp.where(own_bit("mp", bit) == 0, value, swap_groups(value, groups, 1 << bit))
    return value


def channel_total(sums):
    groups = lax.axis_size("mp")
    for bit in range(bits_of("mp")):
        sums = sums + swap_groups(flip_pair(sums, "mp", bit), groups, 1 << bit)
    for bit in range(1, bits_of("dp")):
        sums = sums + flip_pair(sums, "dp", bit)
    return sums


def edge_rows(first_rows, last_rows, half_of_slot):
    groups = lax.axis_size("mp")
    place = lax.axis_index("mp")
    up = [(i, (i + 1) % groups) for i in range(groups)]
    down = [(i, (i - 1) % groups) for i in range(groups)]
    before = lax.ppermute(absolute_groups(last_rows, groups), "mp", up)
    after = lax.ppermute(absolute_groups(first_rows, groups), "mp", down)
    before = absolute_groups(before, groups)
    after = absolute_groups(after, groups)
    second = half_of_slot[:, None, None] == 1
    nothing = jnp.zeros_like(before)
    before = jnp.where(place == 0, jnp.where(second, before[::-1], nothing), before)
    after = jnp.where(place == groups - 1, jnp.where(second, nothing, after[::-1]), after)
    return (before, after)


def swish_grad(value):
    logistic = jax.nn.sigmoid(value)
    return logistic * (1.0 + value * (1.0 - logistic))


def normed_of(value):
    centred = value - jnp.mean(value, axis=-1, keepdims=True)
    inverse = lax.rsqrt(jnp.mean(centred * centred, axis=-1, keepdims=True) + EPS)
    return (centred * inverse, inverse)


def norm_back(normed, inverse, gain, upstream):
    scaled = upstream * gain
    inner = (
        scaled
        - jnp.mean(scaled, axis=-1, keepdims=True)
        - normed * jnp.mean(scaled * normed, axis=-1, keepdims=True)
    )
    return (inverse * inner, jnp.sum(upstream * normed, axis=0, keepdims=True))


def mm(left, right):
    return jnp.dot(left, right, preferred_element_type=F32)


def mm_nt(left, right):
    return lax.dot_general(left, right, NT, preferred_element_type=F32)


def call_kernel(kernel, outs, *inputs):
    return pl.pallas_call(
        kernel, out_shape=[jax.ShapeDtypeStruct(shape, dtype) for shape, dtype in outs]
    )(*inputs)


def column_join(refs, index):
    return jnp.concatenate([ref[:, index * SUB : (index + 1) * SUB] for ref in refs], axis=1)


def ffn_forward_kernel(groups, v_ref, gain_ref, *refs):
    ups, downs, out_ref = refs[:groups], refs[groups : 2 * groups], refs[-1]
    value = v_ref[...]
    normed, _ = normed_of(value)
    active = (normed * gain_ref[...]).astype(BF16)
    total = jnp.zeros_like(value)
    for up_ref, down_ref in zip(ups, downs):
        pre = mm(active, up_ref[...])
        hidden = (pre * jax.nn.sigmoid(pre)).astype(BF16)
        total += mm_nt(hidden, down_ref[...])
    out_ref[...] = value + 0.5 * total


def ffn_backward_kernel(groups, v_ref, d_ref, gain_ref, one_ref, two_ref, last_ref, *refs):
    ups, downs = refs[:groups], refs[groups : 2 * groups]
    out_ref = refs[2 * groups]
    gus, gds = refs[2 * groups + 1 : 3 * groups + 1], refs[3 * groups + 1 :]
    part = ups[0].shape[1]
    normed, inverse = normed_of(v_ref[...])
    upstream = d_ref[...]
    active = (normed * gain_ref[...]).astype(BF16)
    error = (0.5 * upstream).astype(BF16)
    active_t = active.T
    error_t = error.T
    total = jnp.zeros_like(upstream)
    for up_ref, down_ref, gu_ref, gd_ref in zip(ups, downs, gus, gds):
        pre = mm(active, up_ref[...])
        logistic = jax.nn.sigmoid(pre)
        hidden = (pre * logistic).astype(BF16)
        gd_ref[:, :part] = mm(error_t, hidden).astype(BF16)
        d_hidden = mm(error, down_ref[...])
        d_pre = (d_hidden * (logistic * (1.0 + pre * (1.0 - logistic)))).astype(BF16)
        gu_ref[...] = mm(active_t, d_pre).astype(BF16)
        total += mm_nt(d_pre, up_ref[...])
    back, grad_gain = norm_back(normed, inverse, gain_ref[...], total)
    out_ref[...] = upstream + back
    known = [grad_gain, one_ref[...], two_ref[...], last_ref[...]]
    count = sum(value.shape[0] for value in known)
    known.append(jnp.zeros((SUB - count, upstream.shape[1]), F32))
    columns = jnp.concatenate(known, axis=0).T.astype(BF16)
    for gd_ref in gds:
        gd_ref[:, part:] = columns


def project_kernel(groups, v_ref, gain_ref, *refs):
    weights, q_ref = refs[:groups], refs[groups]
    pair_refs = refs[groups + 1 :]
    normed, _ = normed_of(v_ref[...])
    active = (normed * gain_ref[...]).astype(BF16)
    q_ref[...] = mm(active, column_join(weights, 0)).astype(BF16)
    width = q_ref.shape[1] // len(pair_refs)
    for i in (0, 1):
        projected = mm(active, column_join(weights, i + 1)).astype(BF16)
        for h, pair_ref in enumerate(pair_refs):
            pair_ref[i] = projected[:, h * width : (h + 1) * width]


def project_backward_kernel(groups, halves, v_ref, d_ref, gain_ref, *refs):
    weights, smalls = refs[:groups], refs[groups : 2 * groups]
    dqs = refs[2 * groups : 2 * groups + halves]
    pairs, tail = refs[2 * groups + halves : -2 - groups], refs[-2 - groups :]
    each = len(pairs) // halves
    out_ref, gg_ref, grads = tail[0], tail[1], tail[2:]
    normed, inverse = normed_of(v_ref[...])
    active_t = (normed * gain_ref[...]).astype(BF16).T
    total = jnp.zeros_like(d_ref[...])
    for i in range(3):
        if i == 0:
            parts = [ref[...] for ref in dqs]
        else:
            parts = [
                sum(ref[i - 1].astype(F32) for ref in pairs[h * each : (h + 1) * each]).astype(BF16)
                for h in range(halves)
            ]
        error = jnp.concatenate(parts, axis=1) if halves > 1 else parts[0]
        total += mm_nt(error, column_join(weights, i))
        grad = mm(active_t, error).astype(BF16)
        for g, grad_ref in enumerate(grads):
            grad_ref[:, i * SUB : (i + 1) * SUB] = grad[:, g * SUB : (g + 1) * SUB]
    for small_ref, grad_ref in zip(smalls, grads):
        grad_ref[:, 3 * SUB :] = small_ref[...]
    back, grad_gain = norm_back(normed, inverse, gain_ref[...], total)
    out_ref[...] = d_ref[...] + back
    gg_ref[...] = grad_gain


def middle_kernel(groups, halves, v_ref, gain_ref, *refs):
    weights, contexts = refs[:groups], refs[groups : groups + halves]
    out_ref, lin_ref, sig_ref, glu_ref = refs[groups + halves :]
    parts = [ref[...] for ref in contexts]
    context = jnp.concatenate(parts, axis=1) if halves > 1 else parts[0]
    value = v_ref[...] + mm_nt(context, column_join(weights, 0))
    out_ref[...] = value
    normed, _ = normed_of(value)
    active = (normed * gain_ref[...]).astype(BF16)
    lin = mm(active, column_join(weights, 1))
    gate = jax.nn.sigmoid(mm(active, column_join(weights, 2)))
    lin_ref[...] = lin
    sig_ref[...] = gate
    glu_ref[...] = (lin * gate).astype(BF16)


def middle_backward_kernel(groups, halves, dglu_ref, lin_ref, sig_ref, v_ref, d_ref, gain_ref, *refs):
    weights, contexts = refs[:groups], refs[groups : groups + halves]
    out_ref, gg_ref, dctx_ref = refs[groups + halves : groups + halves + 3]
    grads = refs[groups + halves + 3 :]
    d_glu, lin, gate = dglu_ref[...], lin_ref[...], sig_ref[...]
    d_lin = (d_glu * gate).astype(BF16)
    d_gate = (d_glu * lin * gate * (1.0 - gate)).astype(BF16)
    normed, inverse = normed_of(v_ref[...])
    active_t = (normed * gain_ref[...]).astype(BF16).T
    total = mm_nt(d_lin, column_join(weights, 1)) + mm_nt(d_gate, column_join(weights, 2))
    back, grad_gain = norm_back(normed, inverse, gain_ref[...], total)
    value = d_ref[...] + back
    out_ref[...] = value
    gg_ref[...] = grad_gain
    error = value.astype(BF16)
    dctx_ref[...] = mm(error, column_join(weights, 0)).astype(BF16)
    parts = [ref[...] for ref in contexts]
    context = jnp.concatenate(parts, axis=1) if halves > 1 else parts[0]
    for i, grad in enumerate((mm(error.T, context), mm(active_t, d_lin), mm(active_t, d_gate))):
        rounded = grad.astype(BF16)
        for g, grad_ref in enumerate(grads):
            grad_ref[:, i * SUB : (i + 1) * SUB] = rounded[:, g * SUB : (g + 1) * SUB]


def turn_kernel(groups, batch_rows, conv_ref, stat_ref, bn_ref, v_ref, up_ref, gains_ref, *refs):
    mids, weights = refs[:groups], refs[groups : 2 * groups]
    final_ref, out_ref, dpre_ref, gg_ref, sums_ref = refs[2 * groups : 2 * groups + 5]
    grads, pres = refs[2 * groups + 5 : -1], refs[-1]
    part = pres.shape[2]
    top, bottom = slice(0, part), slice(part, 2 * part)
    gain_three, gain_four = gains_ref[3:4], gains_ref[4:5]
    mean = stat_ref[0:1] / batch_rows
    white = (conv_ref[...] - mean) * lax.rsqrt(stat_ref[1:2] / batch_rows - mean * mean + EPS)
    bn_pre = bn_ref[0:1] * white + bn_ref[1:2]
    activated = (bn_pre * jax.nn.sigmoid(bn_pre)).astype(BF16)
    outward = column_join(mids, 3)
    third = v_ref[...] + mm_nt(activated, outward)
    normed, inverse = normed_of(third)
    active = (normed * gain_three).astype(BF16)
    total = jnp.zeros_like(third)
    for g, weight in enumerate(weights):
        pre = mm(active, weight[:, top])
        pres[g] = pre
        total += mm_nt((pre * jax.nn.sigmoid(pre)).astype(BF16), weight[:, bottom])
    last_normed, last_inverse = normed_of(third + 0.5 * total)
    final_ref[...] = (last_normed * gain_four).astype(BF16)
    fourth, grad_four = norm_back(last_normed, last_inverse, gain_four, up_ref[...])
    error = (0.5 * fourth).astype(BF16)
    active_t = active.T
    error_t = error.T
    total = jnp.zeros_like(third)
    for g, (weight, grad_ref) in enumerate(zip(weights, grads)):
        pre = pres[g]
        logistic = jax.nn.sigmoid(pre)
        hidden = (pre * logistic).astype(BF16)
        grad_ref[:, SUB + part :] = mm(error_t, hidden).astype(BF16)
        d_hidden = mm(error, weight[:, bottom])
        d_pre = (d_hidden * (logistic * (1.0 + pre * (1.0 - logistic)))).astype(BF16)
        grad_ref[:, SUB : SUB + part] = mm(active_t, d_pre).astype(BF16)
        total += mm_nt(d_pre, weight[:, top])
    back, grad_three = norm_back(normed, inverse, gain_three, total)
    value = fourth + back
    out_ref[...] = value
    gg_ref[0:1] = grad_three
    gg_ref[1:2] = grad_four
    error = value.astype(BF16)
    grad = mm(error.T, activated).astype(BF16)
    for g, grad_ref in enumerate(grads):
        grad_ref[:, :SUB] = grad[:, g * SUB : (g + 1) * SUB]
    d_pre = mm(error, outward) * swish_grad(bn_pre)
    dpre_ref[...] = d_pre
    sums_ref[0:1] = jnp.sum(d_pre, axis=0, keepdims=True)
    sums_ref[1:2] = jnp.sum(d_pre * white, axis=0, keepdims=True)


def build_skew(line_ref, skew, heads, chunks):
    for h in range(heads):
        for c in range(chunks):
            window = jnp.concatenate(
                [line_ref[0, h, c + 1 : c + 2, :], line_ref[0, h, c : c + 1, :]], axis=1
            )
            window = jnp.broadcast_to(window, (SUB, 2 * SUB))
            rolled = pltpu.roll(window, 1, 1, stride=1, stride_axis=0)
            skew[h, SUB * c : SUB * (c + 1), :] = rolled[:, SUB:]


def stack_heads(rows, heads, factor):
    lane = lax.broadcasted_iota(jnp.int32, rows.shape, 1)
    size = rows.shape[1] // heads
    return jnp.concatenate(
        [
            rows * jnp.where((lane >= h * size) & (lane < (h + 1) * size), factor, 0.0).astype(BF16)
            for h in range(heads)
        ],
        axis=0,
    )


def diagonal_heads(value, heads):
    size, columns = value.shape[0] // heads, value.shape[1] // heads
    parts = [
        value[h * size : (h + 1) * size, h * columns : (h + 1) * columns] for h in range(heads)
    ]
    return jnp.concatenate(parts, axis=0)


def tile_bias(skew, columns, block, offset_of):
    parts = [
        skew[h, pl.ds(pl.multiple_of(offset_of(qb), SUB), block), :] for h, qb in columns
    ]
    return jnp.concatenate(parts, axis=1)


def column_tiles(heads, steps):
    columns = [(h, qb) for h in range(heads) for qb in range(steps)]
    return [columns[i : i + 2] for i in range(0, len(columns), 2)]


def attend_forward_kernel(pieces, heads, qpos, kpos, q_ref, line_ref, *refs):
    k_refs = refs[:pieces]
    v_refs = refs[pieces : 2 * pieces]
    ctx_ref, lse_ref, ctx32_ref, skew, query, scores, probs, v_t = refs[2 * pieces :]
    rows, width = q_ref.shape
    block = rows // 2
    chunks = skew.shape[1] // SUB
    middle = skew.shape[1] // 2
    tiles = column_tiles(heads, rows // SUB)
    span = 2 * SUB
    build_skew(line_ref, skew, heads, chunks)
    for p in range(pieces):
        v_t[:width, p * rows : (p + 1) * rows] = v_refs[p][0].T
    v_t[width:, :] = jnp.ones_like(v_t[width:, :])
    query[...] = stack_heads(q_ref[...], heads, (width // heads) ** (-0.5))
    tops = [jnp.full((8, span), -jnp.inf, F32) for _ in tiles]
    for c in range(2 * pieces):
        keys = k_refs[c // 2][0, (c % 2) * block : (c % 2 + 1) * block, :]
        for t, tile in enumerate(tiles):
            raw = mm_nt(keys, query[t * span : (t + 1) * span, :])
            raw = raw + tile_bias(skew, tile, block, lambda qb: kpos[c] - qpos[qb] + middle)
            scores[c * block : (c + 1) * block, t * span : (t + 1) * span] = raw
            tops[t] = jnp.maximum(tops[t], jnp.max(raw.reshape(block // 8, 8, span), axis=0))
    tops = [jnp.max(top, axis=0, keepdims=True) for top in tops]
    for c in range(2 * pieces):
        for t in range(len(tiles)):
            part = (slice(c * block, (c + 1) * block), slice(t * span, (t + 1) * span))
            probs[part] = jnp.exp(scores[part] - tops[t]).astype(BF16)
    out_t = mm(v_t[...], probs[...])
    total = out_t[width : width + 1, :]
    out_t = out_t[:width, :] / total
    out = diagonal_heads(out_t, heads).T
    ctx_ref[...] = out.astype(BF16)
    ctx32_ref[...] = out
    lse_ref[0] = jnp.concatenate(tops, axis=1) + jnp.log(total)


def attend_backward_kernel(pieces, heads, qpos, kpos, q_ref, d_ref, ctx_ref, lse_ref, line_ref, *refs):
    k_refs = refs[:pieces]
    v_refs = refs[pieces : 2 * pieces]
    dq_ref = refs[2 * pieces]
    dkv_refs = refs[2 * pieces + 1 : 3 * pieces + 1]
    line_grad, skew, skew_grad, query, error, probs, d_scores, k_t = refs[3 * pieces + 1 :]
    rows, width = q_ref.shape
    block = rows // 2
    chunks = skew.shape[1] // SUB
    middle = skew.shape[1] // 2
    scale = (width // heads) ** (-0.5)
    size = width // heads
    tiles = column_tiles(heads, rows // SUB)
    span = 2 * SUB
    build_skew(line_ref, skew, heads, chunks)
    skew_grad[...] = jnp.zeros_like(skew_grad)
    for p in range(pieces):
        k_t[:, p * rows : (p + 1) * rows] = k_refs[p][0].T
    query[...] = stack_heads(q_ref[...], heads, scale)
    error[...] = stack_heads(d_ref[...], heads, 1.0)
    weighed = (d_ref[...].astype(F32) * ctx_ref[...]).T
    dot_sum = jnp.concatenate(
        [jnp.sum(weighed[h * size : (h + 1) * size], axis=0, keepdims=True) for h in range(heads)],
        axis=1,
    )
    lse = lse_ref[0]
    for c in range(2 * pieces):
        part = slice((c % 2) * block, (c % 2 + 1) * block)
        here = slice(c * block, (c + 1) * block)
        keys = k_refs[c // 2][0, part, :]
        values = v_refs[c // 2][0, part, :]
        for t, tile in enumerate(tiles):
            cols = slice(t * span, (t + 1) * span)
            raw = mm_nt(keys, query[cols, :])
            bias = tile_bias(skew, tile, block, lambda qb: kpos[c] - qpos[qb] + middle)
            prob = jnp.exp(raw + bias - lse[:, cols])
            d_score = prob * (mm_nt(values, error[cols, :]) - dot_sum[:, cols])
            probs[c % 2, :, cols] = prob.astype(BF16)
            d_scores[here, cols] = d_score.astype(BF16)
            for i, (h, qb) in enumerate(tile):
                offset = pl.multiple_of(kpos[c] - qpos[qb] + middle, SUB)
                skew_grad[h, pl.ds(offset, block), :] += d_score[:, i * SUB : (i + 1) * SUB]
        dkv_refs[c // 2][0, part, :] = mm(d_scores[here, :], query[...]).astype(BF16)
        dkv_refs[c // 2][1, part, :] = mm(probs[c % 2], error[...]).astype(BF16)
    dq_t = mm(k_t[...], d_scores[...])
    dq_ref[...] = (diagonal_heads(dq_t, heads).T * scale).astype(BF16)
    line_grad[...] = jnp.zeros_like(line_grad)
    for h in range(heads):
        for c in range(chunks):
            block_grad = skew_grad[h, SUB * c : SUB * (c + 1), :]
            value = jnp.concatenate([jnp.zeros_like(block_grad), block_grad], axis=1)
            half = SUB // 2
            while half >= 1:
                value = value[:half] + pltpu.roll(value[half:], 2 * SUB - half, 1)
                half //= 2
            value = pltpu.roll(value, 2 * SUB - 1, 1)
            line_grad[0, h, c + 1 : c + 2, :] += value[:, :SUB]
            line_grad[0, h, c : c + 1, :] += value[:, SUB:]


def attention_specs(rows, first, pieces, shifts, line_shape):
    whole_q = pl.BlockSpec((rows, SUB), lambda j, *_: (0, j + first))
    own = pl.BlockSpec((rows, SUB), lambda j, *_: (0, j))
    line = pl.BlockSpec((1,) + line_shape[1:], lambda j, *_: (j + first, 0, 0, 0))
    keys, values = [], []
    for p in range(pieces):
        keys.append(pl.BlockSpec((1, rows, SUB), lambda j, *_, d=shifts[p]: (0, 0, j ^ d)))
        values.append(pl.BlockSpec((1, rows, SUB), lambda j, *_, d=shifts[p]: (1, 0, j ^ d)))
    return (whole_q, own, line, keys, values)


def attend_forward(query, pairs, shifts, line, first, qpos, kpos):
    rows = query.shape[0]
    heads = line.shape[1]
    groups = pairs[0].shape[2] // SUB
    pieces = len(pairs)
    table = (line.shape[2] - 1) * SUB
    whole_q, own, line_spec, keys, values = attention_specs(rows, first, pieces, shifts, line.shape)
    return pl.pallas_call(
        functools.partial(attend_forward_kernel, pieces, heads),
        out_shape=(
            jax.ShapeDtypeStruct((rows, groups * SUB), BF16),
            jax.ShapeDtypeStruct((groups, 1, heads * rows), F32),
            jax.ShapeDtypeStruct((rows, groups * SUB), F32),
        ),
        grid_spec=pltpu.PrefetchScalarGridSpec(
            num_scalar_prefetch=2,
            grid=(groups,),
            in_specs=[whole_q, line_spec] + keys + values,
            out_specs=(
                own,
                pl.BlockSpec((1, 1, heads * rows), lambda j, *_: (j, 0, 0)),
                own,
            ),
            scratch_shapes=[
                pltpu.VMEM((heads, table, SUB), F32),
                pltpu.VMEM((heads * rows, SUB), BF16),
                pltpu.VMEM((pieces * rows, heads * rows), F32),
                pltpu.VMEM((pieces * rows, heads * rows), BF16),
                pltpu.VMEM((SUB + 16, pieces * rows), BF16),
            ],
        ),
        name="attend_forward",
    )(qpos, kpos, query, line, *pairs, *pairs)


def attend_backward(query, d_context, lse, context, pairs, shifts, line, first, qpos, kpos):
    rows = query.shape[0]
    heads = line.shape[1]
    groups = pairs[0].shape[2] // SUB
    pieces = len(pairs)
    table = (line.shape[2] - 1) * SUB
    whole_q, own, line_spec, keys, values = attention_specs(rows, first, pieces, shifts, line.shape)
    lse_spec = pl.BlockSpec((1, 1, heads * rows), lambda j, *_: (j, 0, 0))
    pair_specs = [
        pl.BlockSpec((2, rows, SUB), lambda j, *_, d=shifts[p]: (0, 0, j ^ d))
        for p in range(pieces)
    ]
    return pl.pallas_call(
        functools.partial(attend_backward_kernel, pieces, heads),
        out_shape=(
            (jax.ShapeDtypeStruct((rows, groups * SUB), BF16),)
            + tuple(jax.ShapeDtypeStruct(pairs[0].shape, BF16) for _ in range(pieces))
            + (jax.ShapeDtypeStruct((groups,) + line.shape[1:], F32),)
        ),
        grid_spec=pltpu.PrefetchScalarGridSpec(
            num_scalar_prefetch=2,
            grid=(groups,),
            in_specs=[whole_q, whole_q, own, lse_spec, line_spec] + keys + values,
            out_specs=(
                (own,)
                + tuple(pair_specs)
                + (pl.BlockSpec((1,) + line.shape[1:], lambda j, *_: (j, 0, 0, 0)),)
            ),
            scratch_shapes=[
                pltpu.VMEM((heads, table, SUB), F32),
                pltpu.VMEM((heads, table, SUB), F32),
                pltpu.VMEM((heads * rows, SUB), BF16),
                pltpu.VMEM((heads * rows, SUB), BF16),
                pltpu.VMEM((2, rows // 2, heads * rows), BF16),
                pltpu.VMEM((pieces * rows, heads * rows), BF16),
                pltpu.VMEM((SUB, pieces * rows), BF16),
            ],
        ),
        name="attend_backward",
    )(qpos, kpos, query, d_context, context, lse, line, *pairs, *pairs)


def block_step(
    block_input,
    out_cotangent,
    early_up,
    early_down,
    attention_in,
    attention_out,
    relative_bias,
    pointwise_in,
    depthwise,
    batch_norm,
    pointwise_out,
    late_up,
    late_down,
    norm_gains,
):
    dp_n, mp_n = lax.axis_size("dp"), lax.axis_size("mp")
    held_rows, features = block_input.shape[1:]
    block = held_rows // mp_n
    rows = 2 * block
    batch_rows = held_rows * dp_n
    batch = lax.axis_index("dp") % 2
    place = lax.axis_index("mp")
    shard_rows, part = early_up.shape
    heads, table_part = relative_bias.shape
    channel_part, kernel = depthwise.shape
    head_width = attention_out.shape[0]
    channels = mp_n * head_width
    margin = (kernel - 1) // 2
    order_a, order_b = full_order()
    fold = max(1, SUB // head_width)
    groups = mp_n // fold
    blocks = jnp.array(reversed_blocks(dp_n), jnp.int32)
    to_natural = blocks[jnp.arange(dp_n, dtype=jnp.int32) ^ lax.axis_index("dp")]
    to_held = blocks ^ lax.axis_index("dp")
    choice = block_choice(features, dp_n, BF16)

    def exchanged(value):
        mine = lax.dynamic_slice_in_dim(value, place * block, block, 1)
        own = lax.dynamic_index_in_dim(mine, batch, 0, keepdims=False)
        away = lax.dynamic_index_in_dim(mine, 1 - batch, 0, keepdims=False)
        other = flip_pair(away, "dp", 0)
        return mm(jnp.concatenate([own, other], axis=0), choice)

    def listed(parts, widths):
        return regroup([parts[delta] for delta in range(mp_n)], widths, fold)

    def unlisted(parts, widths):
        return dict(enumerate(ungroup(list(parts), widths, fold)))

    bias_rows = heads * table_part // SUB
    tap_n = kernel + 2
    gain_row = bias_rows + channel_part
    small_rows = gain_row + norm_gains.shape[0]
    small = jnp.concatenate(
        [
            relative_bias.reshape(bias_rows, SUB),
            jnp.pad(jnp.concatenate([depthwise, batch_norm.T], axis=1), ((0, 0), (0, SUB - tap_n))),
            jnp.pad(norm_gains, ((0, shard_rows - small_rows), (0, SUB - shard_rows))),
        ],
        axis=0,
    )
    early_u = gather_groups(early_up, order_a)
    early_d = gather_groups(early_down.T, order_b)
    start = exchanged(block_input)
    pair_widths = [head_width] * 3
    att_shard = jnp.concatenate([attention_in[0], attention_in[1], attention_in[2], small], axis=1)
    att_held = gather_groups(att_shard, order_a)
    mid_shard = jnp.concatenate(
        [attention_out.T, pointwise_in[0], pointwise_in[1], pointwise_out.T], axis=1
    )
    late_shard = jnp.concatenate([late_up, late_down.T], axis=1)
    mid = listed(gather_groups(mid_shard, order_b), [head_width] * 4)
    late = listed(gather_groups(late_shard, order_a), [part] * 2)
    if fold == 1:
        att = [att_held[delta] for delta in range(mp_n)]
    else:
        att = listed({d: value[:, : 3 * head_width] for d, value in att_held.items()}, pair_widths)
    gains = (
        att_held[0]
        .reshape(dp_n, shard_rows, -1)[:, gain_row:small_rows, 3 * head_width : 3 * head_width + shard_rows]
        .transpose(1, 0, 2)
        .reshape(5, features)
        .astype(F32)
    )
    gain = [gains[i : i + 1] for i in range(5)]
    tiny = jnp.stack([att_held[delta][:, 3 * head_width :] for delta in range(mp_n)])
    tiny = tiny.reshape(mp_n, dp_n, shard_rows, SUB)[:, to_natural]
    line = (
        tiny[:, :, :bias_rows]
        .reshape(mp_n, dp_n, heads, table_part // SUB, SUB)
        .transpose(0, 2, 1, 3, 4)
        .reshape(mp_n, heads, dp_n * table_part // SUB, SUB)
    )
    line = jnp.einsum("ghcl,lk->ghck", line, lane_flip(BF16), preferred_element_type=F32)
    line = jnp.pad(line, ((0, 0), (0, 0), (1, 0), (0, 0)))
    line = line.reshape(groups, heads * fold, line.shape[2], SUB)
    taps = (
        tiny[:, :, bias_rows : bias_rows + channel_part, :tap_n].reshape(channels, tap_n).T.astype(F32)
    )
    tap_rows = [taps[tap] for tap in range(kernel)]
    bn_rows = taps[kernel:]

    half_of_slot = jnp.stack([batch, 1 - batch]).astype(jnp.int32)
    kept = [0]
    for bit in range(bits_of("mp") - 1, -1, -1):
        kept = kept + [delta ^ 1 << bit for delta in kept]
    qpos = (
        half_of_slot[:, None] * held_rows
        + place * block
        + SUB * jnp.arange(block // SUB, dtype=jnp.int32)[None, :]
    ).reshape(-1)
    kpos = jnp.stack(
        [half_of_slot[r] * held_rows + (place ^ delta) * block for delta in kept for r in (0, 1)]
    )
    wide = (rows, channels)
    halves = 2 if fold == 1 and mp_n >= 4 else 1
    local = groups // halves
    up_list = [early_u[delta] for delta in range(mp_n)]
    down_list = [early_d[delta] for delta in range(mp_n)]
    (after_first,) = call_kernel(
        functools.partial(ffn_forward_kernel, mp_n),
        [((rows, features), F32)],
        start,
        gain[0],
        *up_list,
        *down_list,
    )
    query, *pair_halves = call_kernel(
        functools.partial(project_kernel, groups),
        [(wide, BF16)] + [((2, rows, local * SUB), BF16)] * halves,
        after_first,
        gain[1],
        *att,
    )
    top_bit = bits_of("mp") - 1
    held_pairs = []
    for h in range(halves):
        pieces = [pair_halves[h]]
        away = pair_halves[halves - 1 - h]
        if h > 0:
            away = tied(away, held_pairs[h - 1][1])
        pieces.append(flip_pair(away, "mp", top_bit))
        for bit in range(top_bit - 1, -1, -1):
            pieces = pieces + [flip_pair(piece, "mp", bit) for piece in pieces]
        if fold > 1:
            pieces = [swap_groups(piece, mp_n, delta) for piece, delta in zip(pieces, kept)]
        held_pairs.append(pieces)
    shifts = [delta & (local - 1) if fold == 1 else 0 for delta in kept]
    attended = []
    for h in range(halves):
        attended.append(attend_forward(query, held_pairs[h], shifts, line, h * local, qpos, kpos))
    contexts = [item[0] for item in attended]
    after_second, lin, gate_sig, glu = call_kernel(
        functools.partial(middle_kernel, groups, halves),
        [((rows, features), F32), (wide, F32), (wide, F32), (wide, BF16)],
        after_first,
        gain[2],
        *mid,
        *contexts,
    )
    cotangent = exchanged(out_cotangent)
    glu = tied(glu, cotangent).reshape(2, block, channels)
    edge = margin + 1
    before, after = edge_rows(glu[:, :edge], glu[:, block - edge :], half_of_slot)
    extended = jnp.concatenate([before[:, 1:], glu, after[:, :margin]], axis=1).astype(F32)
    conv = jnp.zeros((2, block, channels), F32)
    for tap in range(kernel):
        conv = conv + tap_rows[tap] * extended[:, tap : tap + block]
    conv = conv.reshape(rows, channels)
    sums = channel_total(jnp.stack([jnp.sum(conv, axis=0), jnp.sum(conv * conv, axis=0)]))
    bmean = sums[0:1] / batch_rows
    binv = lax.rsqrt(sums[1:2] / batch_rows - bmean * bmean + EPS)

    wide_part = part * fold
    turn_widths = [head_width, part, part]
    final_rows, d_third, d_pre, gg_last, local_sums, *turn_grads = pl.pallas_call(
        functools.partial(turn_kernel, groups, batch_rows),
        out_shape=[
            jax.ShapeDtypeStruct((rows, features), BF16),
            jax.ShapeDtypeStruct((rows, features), F32),
            jax.ShapeDtypeStruct(wide, F32),
            jax.ShapeDtypeStruct((2, features), F32),
            jax.ShapeDtypeStruct((2, channels), F32),
        ]
        + [jax.ShapeDtypeStruct((features, SUB + 2 * wide_part), BF16)] * groups,
        scratch_shapes=[pltpu.VMEM((groups, rows, wide_part), F32)],
        name="turn",
    )(conv, sums, bn_rows, after_second, cotangent, gains, *mid, *late)
    turn_marks = []
    own_turn = scatter_groups(unlisted(turn_grads, turn_widths), order_a, turn_marks)

    sums = channel_total(local_sums)
    white = (conv - bmean) * binv
    d_conv = (
        binv * bn_rows[0:1] * (d_pre - sums[0:1] / batch_rows - white * sums[1:2] / batch_rows)
    ).reshape(2, block, channels)
    before, after = edge_rows(d_conv[:, :edge], d_conv[:, block - edge :], half_of_slot)
    d_extended = jnp.concatenate([before[:, 1:], d_conv, after[:, :margin]], axis=1)
    d_glu = jnp.zeros((2, block, channels), F32)
    tap_grads = []
    for tap in range(kernel):
        d_glu = d_glu + tap_rows[tap] * d_extended[:, kernel - 1 - tap : kernel - 1 - tap + block]
        tap_grads.append(jnp.sum(extended[:, tap : tap + block] * d_conv, axis=(0, 1)))
    tap_grads = jnp.stack(tap_grads + [local_sums[1], local_sums[0]])
    d_second, gain_two, d_context, *middle_grads = call_kernel(
        functools.partial(middle_backward_kernel, groups, halves),
        [((rows, features), F32), (gain[2].shape, F32), (wide, BF16)]
        + [((features, 3 * SUB), BF16)] * groups,
        tied(d_glu.reshape(rows, channels), turn_marks[0][1 << top_bit]),
        lin,
        gate_sig,
        after_second,
        d_third,
        gain[2],
        *mid,
        *contexts,
    )
    own_middle = scatter_groups(unlisted(middle_grads, pair_widths), order_b)
    d_queries, kept_pairs, sent_pairs, line_grads = [], [], [], []
    for h in range(halves):
        grads = attend_backward(
            query, d_context, attended[h][1], attended[h][2], held_pairs[h], shifts, line,
            h * local, qpos, kpos,
        )
        d_queries.append(grads[0])
        line_grads.append(grads[-1])
        pieces = dict(zip(kept, grads[1:-1]))
        if fold > 1:
            pieces = {delta: swap_groups(value, mp_n, delta) for delta, value in pieces.items()}
        kept_pairs.append([pieces[0]])
        for bit in range(top_bit):
            for delta in [d for d in pieces if d >> bit & 1]:
                other = flip_pair(pieces.pop(delta), "mp", bit)
                home = delta ^ 1 << bit
                if home == 0:
                    kept_pairs[h].append(other)
                else:
                    pieces[home] = (pieces[home].astype(F32) + other.astype(F32)).astype(BF16)
        sent_pairs.append(flip_pair(pieces[1 << top_bit], "mp", top_bit))
    line_grad = jnp.concatenate(line_grads, axis=0)[:, :, 1:].reshape(mp_n, heads, -1, SUB)
    line_grad = jnp.einsum(
        "ghcl,lk->ghck", line_grad, lane_flip(F32), precision=lax.Precision.HIGHEST
    )
    tiny = jnp.concatenate(
        [
            line_grad.reshape(mp_n, heads, dp_n, table_part // SUB, SUB)
            .transpose(0, 2, 1, 3, 4)
            .reshape(mp_n, dp_n, bias_rows, SUB)[:, to_held],
            jnp.pad(
                tap_grads.T.reshape(mp_n, dp_n, channel_part, tap_n)[:, to_held],
                (
                    (0, 0),
                    (0, 0),
                    (0, shard_rows - bias_rows - channel_part),
                    (0, SUB - tap_n),
                ),
            ),
        ],
        axis=2,
    ).astype(BF16)
    tiny = tiny.reshape(mp_n, features, SUB)
    smalls = [tiny[g] for g in range(groups)]
    d_first, gain_one, *att_grads = call_kernel(
        functools.partial(project_backward_kernel, groups, halves),
        [((rows, features), F32), (gain[1].shape, F32)] + [((features, 4 * SUB), BF16)] * groups,
        after_first,
        d_second,
        gain[1],
        *att,
        *smalls,
        *d_queries,
        *[
            part
            for h in range(halves)
            for part in kept_pairs[h] + [sent_pairs[halves - 1 - h]]
        ],
    )
    if fold > 1:
        att_grads = ungroup([grad[:, : 3 * SUB] for grad in att_grads], pair_widths, fold)
        att_grads = [jnp.concatenate([g, t], axis=1) for g, t in zip(att_grads, tiny)]
    own_att = scatter_groups(dict(enumerate(att_grads)), order_a)
    d_start, *early_grads = call_kernel(
        functools.partial(ffn_backward_kernel, mp_n),
        [((rows, features), F32)]
        + [((features, part), BF16)] * mp_n
        + [((features, part + SUB), BF16)] * mp_n,
        start,
        d_first,
        gain[0],
        gain_one,
        gain_two,
        gg_last,
        *up_list,
        *down_list,
    )
    own_up = scatter_groups(dict(enumerate(early_grads[:mp_n])), order_a)
    down_marks = []
    own_down = scatter_groups(dict(enumerate(early_grads[mp_n:])), order_b, down_marks)

    def returned(own, away):
        other = flip_pair(away, "dp", 0).astype(own.dtype)
        first = batch == 0
        return jnp.stack([jnp.where(first, own, other), jnp.where(first, other, own)])

    def columns(value, index):
        return value[:, index * head_width : (index + 1) * head_width]

    tail = own_att[:, 3 * head_width :]
    per_channel = tail[bias_rows : bias_rows + channel_part]
    natural = lax.dot_general(
        tied(d_start, down_marks[1][1 << top_bit]), choice.astype(F32), NT, precision=lax.Precision.HIGHEST
    )
    final_rows = mm_nt(final_rows, choice).astype(BF16)
    return (
        returned(final_rows[:block], final_rows[block:]),
        returned(natural[:block], natural[block:].astype(BF16)),
        own_up,
        own_down[:, :part].T,
        jnp.stack([columns(own_att, i) for i in range(3)]),
        columns(own_middle, 0).T,
        tail[:bias_rows].reshape(heads, table_part),
        jnp.stack([columns(own_middle, 1), columns(own_middle, 2)]),
        per_channel[:, :kernel],
        per_channel[:, kernel:tap_n].T,
        columns(own_turn, 0).T,
        own_turn[:, head_width : head_width + part],
        own_turn[:, head_width + part :].T,
        own_down[:, part : part + 5].T,
    )


def solution(mesh):
    placed = (
        P(None, "dp", None),
        P(None, "dp", None),
        P("dp", "mp"),
        P("mp", "dp"),
        P(None, "dp", "mp"),
        P("mp", "dp"),
        P("mp", "dp"),
        P(None, "dp", "mp"),
        P(("mp", "dp"), None),
        P(None, ("mp", "dp")),
        P("mp", "dp"),
        P("dp", "mp"),
        P("mp", "dp"),
        P(None, "dp"),
    )
    returned = (P(None, ("dp", "mp"), None), P(None, ("dp", "mp"), None)) + placed[2:]
    return jax.shard_map(block_step, mesh=mesh, in_specs=placed, out_specs=returned, check_vma=False)
```
